256 devices in a mesh: row: 16 (over z, core), col: 16 (over y, x).
Axes of the slice: x: 4, y: 4, z: 8, core: 2. Of those that a mesh axis runs over, the one named last changes fastest.
Arguments:
- right_sides: float32 [4, 1024, 4096], P(None, 'row', 'col'), may hold values from -6 to 6
- low_left: bfloat16 [6, 4096, 128], P(None, 'col'), may hold values from -0.25 to 0.25
- low_right: bfloat16 [6, 4096, 128], P(None, 'col'), may hold values from -0.09375 to 0.09375
- up_left: bfloat16 [6, 4096, 128], P(None, 'col'), may hold values from -0.25 to 0.25
- up_right: bfloat16 [6, 4096, 128], P(None, 'col'), may hold values from -0.09375 to 0.09375
- low_ranks: int32 [6], replicated, may hold values from 1 to 4
- up_ranks: int32 [6], replicated, may hold values from 1 to 4
- inv_lower: bfloat16 [4, 4096, 4096], P(None, 'col', 'row'), may hold values from -0.09375 to 0.09375
- inv_upper: bfloat16 [4, 4096, 4096], P(None, 'col', 'row'), may hold values from -0.09375 to 0.09375
Outputs:
- solution: float32 [4, 1024, 4096], P(None, 'row', 'col')
The draws below stay inside these ranges and needn't reach their ends.
Inputs may be any that keep to these rules, and one draw needn't show every extreme that they name: `low_ranks`: factor columns beyond 32 times this value are padding with arbitrary values and must be masked out. `up_ranks`: factor columns beyond 32 times this value are padding with arbitrary values and must be masked out.
All inputs are finite; a program needn't handle non-finite values.
Results may differ from the reference program's by a relative error of at most 0.03.
Values may be sent and summed in bfloat16 or wider, within the bound.
No kernel may reach another device: no remote copies, remote signals or barrier semaphores. Data moves between devices by JAX's collectives and lax.ppermute only.
A program may use at most 64 MiB of HBM per device.

```python
import jax
import jax.numpy as jnp
import numpy as np
from jax import lax

B = 4096
RBLK = 32
R = 128
NT = 4
NRHS = 1024
PAIRS = 6


def touch_ends(result, rng, low, top_value):
    longest = result.shape.index(max(result.shape))
    spots = []
    for shift in (0, 1):
        where = [jax.random.randint(jax.random.fold_in(rng, axis), (), 0, length) for axis, length in enumerate(result.shape)]
        where[longest] = (where[longest] + shift) % result.shape[longest]
        spots.append(tuple(where))
    return result.at[spots[0]].set(low).at[spots[1]].set(top_value)


def shard_levels(own_key, shape, cuts, low, largest):
    loudness = 1.0
    for axis_at, blocks in cuts:
        draws = jax.random.uniform(jax.random.fold_in(jax.random.fold_in(own_key, 6), axis_at), (blocks,), jnp.float32, low / len(cuts), largest / len(cuts))
        loudness = loudness * jnp.repeat(jnp.exp(draws), shape[axis_at] // blocks).reshape((-1,) + (1,) * (len(shape) - 1 - axis_at))
    return loudness


def gaussian(stream_key, extent, deviation, bound, shards=(), held_as=jnp.bfloat16):
    values = jax.random.normal(stream_key, extent, jnp.float32) * deviation
    if len(shards) > 0:
        values = shard_levels(stream_key, extent, shards, -0.22, 0.18) * values
    return jnp.clip(values, min=-bound, max=bound).astype(held_as)


def setup_inputs(seed: int = 0) -> dict:
    arg_keys = jax.random.split(jax.random.key(seed), 10)
    return {
        "right_sides": gaussian(arg_keys[0], (NT, NRHS, B), 1.0, 6.0, ((1, 16), (2, 16)), jnp.float32),
        "low_left": gaussian(arg_keys[1], (PAIRS, B, R), (4 * R) ** -0.5, 0.25, ((1, 16),)),
        "low_right": gaussian(arg_keys[2], (PAIRS, B, R), B ** -0.5, 0.09375, ((1, 16),)),
        "up_left": gaussian(arg_keys[3], (PAIRS, B, R), (4 * R) ** -0.5, 0.25, ((1, 16),)),
        "up_right": gaussian(arg_keys[4], (PAIRS, B, R), B ** -0.5, 0.09375, ((1, 16),)),
        "low_ranks": touch_ends(jax.random.randint(arg_keys[5], (PAIRS,), 1, 5), jax.random.fold_in(arg_keys[5], 1), 1, 4).astype(jnp.int32),
        "up_ranks": touch_ends(jax.random.randint(arg_keys[6], (PAIRS,), 1, 5), jax.random.fold_in(arg_keys[6], 1), 1, 4).astype(jnp.int32),
        "inv_lower": gaussian(arg_keys[7], (NT, B, B), B ** -0.5, 0.09375, ((1, 16), (2, 16))),
        "inv_upper": gaussian(arg_keys[8], (NT, B, B), B ** -0.5, 0.09375, ((1, 16), (2, 16))),
    }


def project(solved, factors):
    return jnp.einsum("nb,mbr->mnr", solved.astype(jnp.bfloat16).astype(jnp.float32), factors.astype(jnp.float32), precision=lax.Precision.HIGHEST)


def expand(masked, factors):
    return jnp.einsum("mnr,mbr->mnb", masked.astype(jnp.float32), factors.astype(jnp.float32), precision=lax.Precision.HIGHEST)


def apply_inverse(rounded, inverse):
    return lax.dot_general(rounded, inverse, (((1,), (1,)), ((), ())), preferred_element_type=jnp.float32)


def reference(right_sides, low_left, low_right, up_left, up_right, low_ranks, up_ranks, inv_lower, inv_upper):
    columns = jnp.arange(R, dtype=jnp.int32)
    residual = right_sides
    forward = []
    for section in range(NT):
        solved = apply_inverse(residual[section].astype(jnp.bfloat16), inv_lower[section])
        forward.append(solved)
        if section + 1 < NT:
            pair_index = np.array([tile * (tile - 1) // 2 + section for tile in range(section + 1, NT)], dtype=np.int32)
            projections = project(solved, low_right[pair_index])
            rank_mask = (columns[None, :] < RBLK * low_ranks[pair_index][:, None]).astype(jnp.float32)
            masked = (projections * rank_mask[:, None, :]).astype(jnp.bfloat16)
            residual = residual.at[section + 1:].add(-expand(masked, low_left[pair_index]))
    state = jnp.stack(forward)
    solutions = [None] * NT
    for section in range(NT - 1, -1, -1):
        solved = apply_inverse(state[section].astype(jnp.bfloat16), inv_upper[section])
        solutions[section] = solved
        if section > 0:
            pair_index = np.array([section * (section - 1) // 2 + tile for tile in range(section)], dtype=np.int32)
            projections = project(solved, up_right[pair_index])
            rank_mask = (columns[None, :] < RBLK * up_ranks[pair_index][:, None]).astype(jnp.float32)
            masked = (projections * rank_mask[:, None, :]).astype(jnp.bfloat16)
            state = state.at[:section].add(-expand(masked, up_left[pair_index]))
    return jnp.stack(solutions)
```

```python
import jax
import jax.numpy as jnp
from jax import lax
from jax.sharding import PartitionSpec as P

RBLK = 32
BF16 = jnp.bfloat16
F32 = jnp.float32


def from_everyone(value, axis):
    length = lax.axis_size(axis)
    return lax.all_to_all(
        jnp.broadcast_to(value[None], (length, *value.shape)), axis, 0, 0, tiled=True
    )


def matmul(left, right):
    return jnp.dot(left, right, preferred_element_type=F32)


def lower_pair(i, j):
    return i * (i - 1) // 2 + j


def gather_inverse(inverse, group):
    rows = lax.axis_size("row")
    groups = [list(range(s, s + group)) for s in range(0, rows, group)]
    return lax.all_gather(inverse, "row", axis=0, axis_index_groups=groups)


def batched_products(rows, sizes, inverse, group):
    n_rows, n_cols = lax.axis_size("row"), lax.axis_size("col")
    spans = n_rows // group
    inner = n_cols // spans
    moves = []
    for r in range(n_rows):
        for c in range(n_cols):
            to_row = (c // inner) * group + r % group
            to_col = (r // group) * inner + c % inner
            moves.append((r * n_cols + c, to_row * n_cols + to_col))
    swapped = lax.ppermute(rows, ("row", "col"), moves)
    everything = from_everyone(swapped, "col")
    everything = everything.reshape(spans, inner, *rows.shape)
    parts = []
    start = 0
    for tile, size in enumerate(sizes):
        block = everything[:, :, start : start + size]
        parts.append(
            jnp.einsum(
                "sjnw,jaw->sna", block, inverse[:, tile], preferred_element_type=F32
            ).astype(BF16)
        )
        start += size
    partial = jnp.concatenate(parts, axis=1)
    groups = [[s * group + j for s in range(spans)] for j in range(group)]
    received = lax.all_to_all(
        partial, "row", 0, 0, tiled=True, axis_index_groups=groups
    )
    return jnp.sum(received.astype(F32), axis=0)


def summed_over_col(partial):
    length = lax.axis_size("col")
    received = lax.all_to_all(partial.astype(BF16), "col", 0, 0, tiled=True)
    received = received.reshape(length, -1, received.shape[-1])
    mine = jnp.sum(received.astype(F32), axis=0).astype(BF16)
    return from_everyone(mine, "col").reshape(partial.shape)


def sweep(tiles, order, pair, left, right, ranks, inverse, group):
    count = len(order)
    place = {tile: at for at, tile in enumerate(order)}
    before = {tile: order[: place[tile]] for tile in order}
    after = {tile: order[place[tile] + 1 :] for tile in order}
    n, width = tiles[0].shape
    rank_cols = left.shape[2]
    share = rank_cols // lax.axis_size("row")
    mine = lax.axis_index("row") * share
    slices = lax.dynamic_slice_in_dim(left, mine, share, axis=2).transpose(0, 2, 1)
    rows, sizes = [], []
    for tile in range(count):
        rows.append(tiles[tile].astype(BF16))
        for source in before[tile]:
            rows.append(slices[pair(tile, source)])
        sizes.append(n + share * len(before[tile]))
    solved = batched_products(jnp.concatenate(rows, axis=0), sizes, inverse, group)
    dense, extra, extra_at = [], [], {}
    start = 0
    for tile in range(count):
        dense.append(solved[start : start + n])
        for at, source in enumerate(before[tile]):
            extra_at[tile, source] = len(extra)
            extra.append(solved[start + n + share * at : start + n + share * (at + 1)])
        start += sizes[tile]
    extra = from_everyone(jnp.stack(extra).astype(BF16), "row")
    extra = extra.transpose(1, 0, 2, 3).reshape(-1, rank_cols, width)
    projections, at_rows = [], {}
    start = 0
    for tile in order:
        factors = {i: right[pair(i, tile)] for i in after[tile]}
        for i in after[tile]:
            projections.append(matmul(dense[tile].astype(BF16), factors[i]))
            at_rows[i, tile] = start
            start += n
            for source in before[tile]:
                projections.append(matmul(extra[extra_at[tile, source]], factors[i]))
                at_rows[i, tile, source] = start
                start += rank_cols
    sums = summed_over_col(jnp.concatenate(projections, axis=0))
    columns = jnp.arange(rank_cols, dtype=jnp.int32)
    masked = {}
    results = [None] * count
    for tile in order:
        value = dense[tile]
        for source in before[tile]:
            value = value - matmul(masked[tile, source], extra[extra_at[tile, source]])
        results[tile] = value
        for i in after[tile]:
            at = at_rows[i, tile]
            projected = sums[at : at + n].astype(F32)
            for source in before[tile]:
                at = at_rows[i, tile, source]
                projected = projected - matmul(
                    masked[tile, source], sums[at : at + rank_cols]
                )
            keep = (columns < RBLK * ranks[pair(i, tile)]).astype(F32)
            masked[i, tile] = (projected * keep[None, :]).astype(BF16)
    return results


def shards(
    right_sides, low_left, low_right, up_left, up_right, low_ranks, up_ranks, inv_lower, inv_upper
):
    count = right_sides.shape[0]
    group = 4
    lower = gather_inverse(inv_lower, group)
    upper = gather_inverse(inv_upper, group)
    tiles = [right_sides[tile] for tile in range(count)]
    forward = sweep(
        tiles, list(range(count)), lower_pair, low_left, low_right, low_ranks, lower, group
    )
    solved = sweep(
        forward,
        list(range(count))[::-1],
        lambda i, j: lower_pair(j, i),
        up_left,
        up_right,
        up_ranks,
        upper,
        group,
    )
    return jnp.stack(solved)


def solution(mesh):
    in_specs = (
        P(None, "row", "col"),
        P(None, "col", None),
        P(None, "col", None),
        P(None, "col", None),
        P(None, "col", None),
        P(),
        P(),
        P(None, "col", "row"),
        P(None, "col", "row"),
    )
    out_specs = P(None, "row", "col")
    return jax.shard_map(shards, mesh=mesh, in_specs=in_specs, out_specs=out_specs, check_vma=False)
```

```python
import jax
import jax.numpy as jnp
from jax import lax
from jax.sharding import PartitionSpec as P

RBLK = 32
BF16 = jnp.bfloat16
F32 = jnp.float32
SIDE = 4
X_GROUPS = [[SIDE * y + x for x in range(SIDE)] for y in range(SIDE)]
Y_GROUPS = [[SIDE * y + x for y in range(SIDE)] for x in range(SIDE)]
Q_GROUPS = [[SIDE * q + j for q in range(SIDE)] for j in range(SIDE)]
Z_GROUPS = [[2 * z + core for z in range(8)] for core in range(2)]


def routes(to):
    index = lambda q, j, y, x: (SIDE * q + j) * SIDE * SIDE + SIDE * y + x
    span = range(SIDE)
    return [
        (index(q, j, y, x), index(*to(q, j, y, x)))
        for q in span for j in span for y in span for x in span
    ]


def permuted(value, to):
    return lax.ppermute(value, ("row", "col"), routes(to))


def exchanged(value, axis, groups):
    return lax.all_to_all(value, axis, 0, 0, tiled=True, axis_index_groups=groups)


def from_everyone(value, axis, groups):
    return exchanged(
        jnp.broadcast_to(value[None], (len(groups[0]), *value.shape)), axis, groups
    )


def over_x(value):
    return exchanged(value, "col", X_GROUPS)


def swapped(value):
    return permuted(value, lambda q, j, y, x: (y, j, q, x))


def by_flips(value, j):
    pairs = jnp.concatenate([value[1:2], value[0:1], value[3:4], value[2:3]], axis=0)
    value = jnp.where(j % 2 == 1, pairs, value)
    return jnp.where(j >= 2, jnp.concatenate([value[2:], value[:2]], axis=0), value)


def matmul(left, right):
    return jnp.dot(left, right, preferred_element_type=F32)


def quad_of(value):
    core = lambda q, j, y, x: (q, j ^ 1, y, x)
    near = permuted(value, core)
    far = permuted(value, lambda q, j, y, x: (q, j ^ 2, y, x))
    return jnp.stack([value, near, far, permuted(far, core)])


def tile_of_x(inverse):
    mine = over_x(inverse)
    return quad_of(mine.reshape(-1, mine.shape[-1]))


def solved_rows(rows, inverse, j):
    moved = swapped(by_flips(rows, j))
    everything = from_everyone(moved, "col", Y_GROUPS)
    partial = jnp.einsum(
        "sinw,iaw->sna", everything, inverse, preferred_element_type=F32
    ).astype(BF16)
    received = exchanged(partial, "row", Q_GROUPS)
    return jnp.sum(received.astype(F32), axis=0)


def summed_over_y(value):
    return jnp.sum(from_everyone(value, "col", Y_GROUPS).astype(F32), axis=0)


def gathered_over_row(value, core):
    same = from_everyone(value, "row", Z_GROUPS)
    other = permuted(same, lambda q, j, y, x: (q, j ^ 1, y, x))
    even = jnp.where(core == 0, same, other)
    odd = jnp.where(core == 0, other, same)
    return jnp.stack([even, odd], axis=1)


class Sweep:
    def __init__(self, order, pair, left, right, ranks):
        self.order, self.pair, self.left, self.right, self.ranks = order, pair, left, right, ranks
        self.place = {tile: at for at, tile in enumerate(order)}
        self.before = {tile: order[: self.place[tile]] for tile in order}
        self.after = {tile: order[self.place[tile] + 1 :] for tile in order}
        self.slots = len(order) - 1

    def slotted(self, pieces, sources, towards):
        out = []
        for tile in range(len(self.order)):
            for slot in range(self.slots):
                known = sources[tile]
                if slot >= len(known):
                    out.append(pieces[0])
                elif towards:
                    out.append(pieces[self.pair(tile, known[slot])])
                else:
                    out.append(pieces[self.pair(known[slot], tile)])
        return jnp.stack(out).reshape(len(self.order), self.slots, *pieces.shape[1:])

    def left_rows(self, row):
        share = self.left.shape[2] // lax.axis_size("row")
        mine = lax.dynamic_slice_in_dim(self.left, row * share, share, axis=2)
        slots = self.slotted(mine.transpose(0, 2, 1), self.before, True)
        return slots.reshape(len(self.order), -1, slots.shape[-1])

    def set_right(self):
        got = over_x(self.slotted(self.right, self.after, False))
        self.factors = got.transpose(1, 0, 2, 3).reshape(self.slots, -1, got.shape[-1])

    def set_extra(self, slices, core, x):
        whole = gathered_over_row(slices, core)
        share = slices.shape[0] // self.slots
        whole = whole.reshape(-1, self.slots, share, slices.shape[1])
        self.extra = whole.transpose(1, 0, 2, 3).reshape(self.slots, -1, slices.shape[1])
        second = x == self.order[1]
        one = matmul(self.extra[0], self.factors[0])
        two = matmul(
            jnp.where(second, self.extra[0], self.extra[1]),
            jnp.where(second, self.factors[1], self.factors[0]),
        )
        return jnp.stack([one, two]).astype(BF16)

    def couplings(self, found):
        first, second, third = self.order[:3]
        last = self.order[3]
        self.coupling = {
            (third, second, first): found[second, 0],
            (last, second, first): found[second, 1],
            (last, third, first): found[third, 0],
            (last, third, second): found[third, 1],
        }

    def finish(self, dense, x):
        n = dense.shape[0]
        rank_cols = self.factors.shape[2]
        projected = jnp.einsum(
            "na,sar->snr", dense.astype(BF16), self.factors, preferred_element_type=F32
        )
        sums = summed_over_y(projected.astype(BF16)).astype(BF16)
        sums = from_everyone(sums, "col", X_GROUPS)
        columns = jnp.arange(rank_cols, dtype=jnp.int32)
        masked = {}
        for tile in self.order:
            for slot, i in enumerate(self.after[tile]):
                value = sums[tile, slot].astype(F32)
                for source in self.before[tile]:
                    value = value - matmul(
                        masked[tile, source], self.coupling[i, tile, source]
                    )
                keep = (columns < RBLK * self.ranks[self.pair(i, tile)]).astype(F32)
                masked[i, tile] = (value * keep[None, :]).astype(BF16)
        nothing = jnp.zeros((n, rank_cols), BF16)
        table = []
        for tile in range(len(self.order)):
            known = self.before[tile]
            table.append(
                jnp.concatenate(
                    [
                        masked[tile, known[slot]] if slot < len(known) else nothing
                        for slot in range(self.slots)
                    ],
                    axis=1,
                )
            )
        mine = lax.dynamic_index_in_dim(jnp.stack(table), x, 0, keepdims=False)
        return dense - matmul(mine, self.extra.reshape(-1, self.extra.shape[-1]))


def lower_pair(i, j):
    return i * (i - 1) // 2 + j


def shards(
    right_sides, low_left, low_right, up_left, up_right, low_ranks, up_ranks, inv_lower, inv_upper
):
    count = right_sides.shape[0]
    row, col = lax.axis_index("row"), lax.axis_index("col")
    j, core, x = row % SIDE, row % 2, col % SIDE
    tiles = list(range(count))
    low = Sweep(tiles, lower_pair, low_left, low_right, low_ranks)
    up = Sweep(
        tiles[::-1], lambda i, k: lower_pair(k, i), up_left, up_right, up_ranks
    )
    lower = tile_of_x(inv_lower)
    dense = solved_rows(over_x(right_sides.astype(BF16)), lower, j)

    upper = tile_of_x(inv_upper)
    low.set_right()
    up.set_right()
    low_rows, up_rows = low.left_rows(row), up.left_rows(row)
    share = low_rows.shape[1]
    both = over_x(jnp.concatenate([low_rows, up_rows], axis=1))
    moved = swapped(by_flips(both, j))
    everything = from_everyone(moved, "col", Y_GROUPS)
    partial = jnp.concatenate(
        [
            jnp.einsum(
                "sinw,iaw->sna", everything[:, :, at : at + share], inverse,
                preferred_element_type=F32,
            )
            for at, inverse in ((0, lower), (share, upper))
        ],
        axis=1,
    ).astype(BF16)
    slices = jnp.sum(exchanged(partial, "row", Q_GROUPS).astype(F32), axis=0).astype(BF16)
    couplings = jnp.stack(
        [
            low.set_extra(slices[:share], core, x),
            up.set_extra(slices[share:], core, x),
        ]
    )
    couplings = summed_over_y(couplings).astype(BF16)
    couplings = from_everyone(couplings, "col", X_GROUPS)
    low.couplings(couplings[:, 0])
    up.couplings(couplings[:, 1])

    forward = low.finish(dense, x)
    n = forward.shape[0]
    rows = forward.astype(BF16).reshape(n, SIDE, -1).transpose(1, 0, 2)
    solved = up.finish(solved_rows(rows, upper, j), x)
    rows = solved.astype(BF16).reshape(n, SIDE, -1).transpose(1, 0, 2)
    return over_x(rows).astype(F32)


def solution(mesh):
    in_specs = (
        P(None, "row", "col"),
        P(None, "col", None),
        P(None, "col", None),
        P(None, "col", None),
        P(None, "col", None),
        P(),
        P(),
        P(None, "col", "row"),
        P(None, "col", "row"),
    )
    out_specs = P(None, "row", "col")
    return jax.shard_map(shards, mesh=mesh, in_specs=in_specs, out_specs=out_specs, check_vma=False)
```

```python
import jax
import jax.numpy as jnp
from jax import lax
from jax.experimental import pallas as pl
from jax.experimental.pallas import tpu as pltpu
from jax.sharding import PartitionSpec as P

RBLK = 32
BF16 = jnp.bfloat16
F32 = jnp.float32
SIDE = 4
X_GROUPS = [[SIDE * y + x for x in range(SIDE)] for y in range(SIDE)]
Y_GROUPS = [[SIDE * y + x for y in range(SIDE)] for x in range(SIDE)]
Q_GROUPS = [[SIDE * q + j for q in range(SIDE)] for j in range(SIDE)]
Z_GROUPS = [[2 * z + core for z in range(8)] for core in range(2)]


def routes(to):
    index = lambda q, j, y, x: (SIDE * q + j) * SIDE * SIDE + SIDE * y + x
    span = range(SIDE)
    return [
        (index(q, j, y, x), index(*to(q, j, y, x)))
        for q in span for j in span for y in span for x in span
    ]


def permuted(value, to):
    return lax.ppermute(value, ("row", "col"), routes(to))


def exchanged(value, axis, groups):
    return lax.all_to_all(value, axis, 0, 0, tiled=True, axis_index_groups=groups)


def over_x(value):
    return exchanged(value, "col", X_GROUPS)


def from_everyone(value, axis, groups):
    return exchanged(
        jnp.broadcast_to(value[None], (len(groups[0]), *value.shape)), axis, groups
    )


def swapped(value):
    return permuted(value, lambda q, j, y, x: (y, j, q, x))


def swap_core(value):
    return permuted(value, lambda q, j, y, x: (q, j ^ 1, y, x))


def swap_pair(value):
    return permuted(value, lambda q, j, y, x: (q, j ^ 2, y, x))


def dot(left, right):
    return jnp.dot(left, right, preferred_element_type=F32)


def dot_t(left, right):
    return lax.dot_general(
        left, right, (((1,), (1,)), ((), ())), preferred_element_type=F32
    )


def pair_of(i, j):
    high, low = max(i, j), min(i, j)
    return high * (high - 1) // 2 + low


def partners(tile):
    return [t for t in range(SIDE) if t != tile]


def kernel_call(body, out_shape, smem=(), flops=0, grid=None, in_specs=None, out_specs=None):
    def run(*args):
        specs = in_specs or [
            pl.BlockSpec(memory_space=pltpu.SMEM if at in smem else pltpu.VMEM)
            for at in range(len(args))
        ]
        outs = jax.tree.leaves(out_shape)
        moved = sum(a.size * a.dtype.itemsize for a in [*args, *outs])
        more = {} if grid is None else {"grid": grid, "out_specs": out_specs}
        return pl.pallas_call(
            body,
            out_shape=out_shape,
            in_specs=specs,
            compiler_params=pltpu.CompilerParams(vmem_limit_bytes=30 * 2**20),
            cost_estimate=pl.CostEstimate(
                flops=flops, bytes_accessed=moved, transcendentals=0
            ),
            **more,
        )(*args)

    return run


def pack_kernel(right_ref, low_ref, up_ref, out_ref):
    n = right_ref.shape[1]
    rank_cols = low_ref.shape[2]
    share = rank_cols // lax.axis_size("row")
    row = lax.axis_index("row")
    at = lax.broadcasted_iota(jnp.int32, (share, rank_cols), 1)
    want = lax.broadcasted_iota(jnp.int32, (share, rank_cols), 0) + row * share
    pick = (at == want).astype(F32).astype(BF16)
    for tile in range(SIDE):
        out_ref[tile, :n] = right_ref[tile].astype(BF16)
        pieces = [
            dot_t(pick, (low_ref if t < tile else up_ref)[pair_of(tile, t)])
            for t in partners(tile)
        ]
        out_ref[tile, n:] = jnp.concatenate(pieces, axis=0).astype(BF16)


def turn_kernel(low_ref, up_ref, out_ref):
    rank_cols = low_ref.shape[2]
    one = lax.broadcasted_iota(jnp.int32, (rank_cols, rank_cols), 0)
    two = lax.broadcasted_iota(jnp.int32, (rank_cols, rank_cols), 1)
    eye = (one == two).astype(F32).astype(BF16)
    for tile in range(SIDE):
        for slot, t in enumerate(partners(tile)):
            factor = (up_ref if t < tile else low_ref)[pair_of(tile, t)]
            out_ref[tile, slot * rank_cols : (slot + 1) * rank_cols] = dot_t(
                eye, factor
            ).astype(BF16)


def products_kernel(n, x_ref, *refs):
    lower, upper, out_ref = refs[:SIDE], refs[SIDE : 2 * SIDE], refs[-1]
    flip = lax.rem(lax.axis_index("row"), SIDE)
    rows = x_ref.shape[2]
    for span in range(SIDE):
        blocks = [x_ref[span, at ^ flip] for at in range(SIDE)]
        value = sum(dot_t(blocks[at], lower[at][...]) for at in range(SIDE))
        if rows > n:
            tile = lax.rem(lax.axis_index("col"), SIDE)
            other = sum(dot_t(blocks[at][n:], upper[at][...]) for at in range(SIDE))
            share = (rows - n) // (SIDE - 1)
            slot = lax.broadcasted_iota(jnp.int32, other.shape, 0) // share
            out_ref[span, :n] = value[:n].astype(BF16)
            out_ref[span, n:] = jnp.where(slot < tile, value[n:], other).astype(BF16)
        else:
            out_ref[span] = value.astype(BF16)


def products(n, gathered, *inverses):
    spans, blocks, rows, width = gathered.shape
    total = inverses[0].shape[0]
    return kernel_call(
        lambda *refs: products_kernel(n, *refs),
        jax.ShapeDtypeStruct((spans, rows, total), BF16),
        flops=2 * spans * blocks * rows * width * total,
        grid=(total // 256,),
        in_specs=[pl.BlockSpec(gathered.shape, lambda a: (0, 0, 0, 0))]
        + [pl.BlockSpec((256, width), lambda a: (a, 0)) for _ in inverses],
        out_specs=pl.BlockSpec((spans, rows, 256), lambda a: (0, 0, a)),
    )(gathered, *inverses)


def total_kernel(n, part_ref, dense_ref, extra_ref):
    whole = part_ref[0].astype(F32)
    for at in range(1, SIDE):
        whole = whole + part_ref[at].astype(F32)
    dense_ref[...] = whole[:n]
    extra = whole[n:].astype(BF16)
    for at in range(extra_ref.shape[0]):
        extra_ref[at] = extra


def project(dense, turned_ref, slot, rank_cols):
    width = turned_ref.shape[2]
    return sum(
        dot_t(
            dense[:, at * width : (at + 1) * width],
            turned_ref[at, slot * rank_cols : (slot + 1) * rank_cols],
        )
        for at in range(SIDE)
    )


def couple_kernel(dense_ref, mine_ref, other_ref, turned_ref, extra_ref, send_ref, later_ref):
    n = dense_ref.shape[0]
    slots = SIDE - 1
    rank_cols = turned_ref.shape[1] // slots
    width = turned_ref.shape[2]
    share = mine_ref.shape[1] // slots
    even = lax.rem(lax.axis_index("row"), 2) == 0
    tile = lax.rem(lax.axis_index("col"), SIDE)
    for z in range(mine_ref.shape[0]):
        mine, other = mine_ref[z].astype(F32), other_ref[z].astype(F32)
        first = jnp.where(even, mine, other)
        second = jnp.where(even, other, mine)
        for slot in range(slots):
            at = slice(slot * share, (slot + 1) * share)
            start = slot * rank_cols + z * 2 * share
            extra_ref[start : start + 2 * share] = jnp.concatenate(
                [first[at], second[at]], axis=0
            ).astype(BF16)
    dense = dense_ref[...].astype(BF16)
    pieces = [project(dense, turned_ref, slot, rank_cols) for slot in range(slots)]

    def coupling(left, right):
        left = pl.multiple_of(left * rank_cols, rank_cols)
        right = pl.multiple_of(right * rank_cols, rank_cols)
        return sum(
            dot_t(
                extra_ref[pl.ds(left, rank_cols), at * width : (at + 1) * width],
                turned_ref[at, pl.ds(right, rank_cols), :],
            )
            for at in range(SIDE)
        )

    one = tile == 1
    pick = lambda a, b: jnp.where(one, a, b)
    pieces += [coupling(0, pick(1, 2)), coupling(pick(0, 1), 2)]
    send = jnp.concatenate(pieces, axis=0).astype(BF16)
    for at in range(SIDE):
        send_ref[at] = send
    later_ref[:rank_cols] = coupling(pick(1, 2), 0).astype(BF16)
    later_ref[rank_cols:] = coupling(2, pick(0, 1)).astype(BF16)


def last_project_kernel(part_ref, turned_ref, later_ref, dense_ref, send_ref):
    slots = SIDE - 1
    rank_cols = turned_ref.shape[1] // slots
    whole = part_ref[0].astype(F32)
    for at in range(1, SIDE):
        whole = whole + part_ref[at].astype(F32)
    dense_ref[...] = whole
    dense = whole.astype(BF16)
    pieces = [project(dense, turned_ref, slot, rank_cols) for slot in range(slots)]
    send = jnp.concatenate(pieces, axis=0).astype(BF16)
    n = send.shape[0]
    for at in range(SIDE):
        send_ref[at, :n] = send
        send_ref[at, n:] = later_ref[...]


def add_kernel(part_ref, out_ref):
    whole = part_ref[0].astype(F32)
    for at in range(1, SIDE):
        whole = whole + part_ref[at].astype(F32)
    whole = whole.astype(BF16)
    for at in range(SIDE):
        out_ref[at] = whole


def finish_kernel(is_lower, sums_ref, dense_ref, extra_ref, ranks_ref, out_ref):
    n = dense_ref.shape[0]
    rank_cols = extra_ref.shape[0] // (SIDE - 1)
    width = out_ref.shape[2]
    tile = lax.rem(lax.axis_index("col"), SIDE)
    columns = lax.broadcasted_iota(jnp.int32, (n, rank_cols), 1)
    at_coupling = (SIDE - 1) * n
    coupling = {}
    order = list(range(SIDE)) if is_lower else list(range(SIDE))[::-1]
    first, second, third, last = order
    for which, key in enumerate(((third, second, first), (last, second, first))):
        coupling[key] = (second, which)
    for which, key in enumerate(((last, third, first), (last, third, second))):
        coupling[key] = (third, which)
    if not is_lower:
        coupling = {
            (0, 2, 3): (2, 0), (1, 2, 3): (2, 1), (0, 1, 2): (1, 0), (0, 1, 3): (1, 1)
        }
    masked = {}
    for at, source in enumerate(order):
        for target in order[at + 1 :]:
            slot = partners(source).index(target)
            value = sums_ref[source, slot * n : (slot + 1) * n].astype(F32)
            for before in order[:at]:
                held, which = coupling[target, source, before]
                start = at_coupling + which * rank_cols
                value = value - dot(
                    masked[source, before], sums_ref[held, start : start + rank_cols]
                )
            keep = columns < RBLK * ranks_ref[pair_of(source, target)]
            masked[target, source] = jnp.where(keep, value, 0.0).astype(BF16)
    result = dense_ref[...]
    nothing = jnp.zeros((n, rank_cols), BF16)
    for slot in range(SIDE - 1):
        mine = nothing
        for target in range(SIDE):
            source = partners(target)[slot]
            if (target, source) in masked:
                mine = jnp.where(tile == target, masked[target, source], mine)
        result = result - dot(
            mine, extra_ref[slot * rank_cols : (slot + 1) * rank_cols]
        )
    result = result.astype(BF16)
    for at in range(SIDE):
        out_ref[at] = result[:, at * width : (at + 1) * width]


def quad_of(value):
    far = swap_pair(value)
    return [value, swap_core(value), far, swap_core(far)]


def shards(
    right_sides, low_left, low_right, up_left, up_right, low_ranks, up_ranks, inv_lower, inv_upper
):
    n, width = right_sides.shape[1:]
    rank_cols = low_left.shape[2]
    slots = SIDE - 1
    share = rank_cols // lax.axis_size("row")
    total = SIDE * width
    shape = jax.ShapeDtypeStruct

    lower = quad_of(over_x(inv_lower).reshape(total, width))
    rows = kernel_call(
        pack_kernel, shape((SIDE, n + slots * share, width), BF16)
    )(right_sides, low_left, up_left)
    rows = swapped(over_x(rows))
    upper = quad_of(over_x(inv_upper).reshape(total, width))
    gathered = from_everyone(rows, "col", Y_GROUPS).reshape(SIDE, SIDE, -1, width)
    turned = over_x(
        kernel_call(turn_kernel, shape((SIDE, slots * rank_cols, width), BF16))(
            low_right, up_right
        )
    )
    partial = products(n, gathered, *lower, *upper)
    received = exchanged(partial, "row", Q_GROUPS)
    dense, extra = kernel_call(
        lambda *refs: total_kernel(n, *refs),
        (shape((n, total), F32), shape((8, slots * share, total), BF16)),
    )(received)
    mine = exchanged(extra, "row", Z_GROUPS)
    other = swap_core(mine)
    packed = slots * n + 2 * rank_cols
    extra, send, later = kernel_call(
        couple_kernel,
        (
            shape((slots * rank_cols, total), BF16),
            shape((SIDE, packed, rank_cols), BF16),
            shape((2 * rank_cols, rank_cols), BF16),
        ),
    )(dense, mine, other, turned)

    def finished(is_lower, send, dense, ranks):
        sums = kernel_call(add_kernel, shape((SIDE, packed, rank_cols), BF16))(
            exchanged(send, "col", Y_GROUPS)
        )
        return kernel_call(
            lambda *refs: finish_kernel(is_lower, *refs),
            shape((SIDE, n, width), BF16),
            smem=(3,),
        )(over_x(sums), dense, extra, ranks)

    rows = finished(True, send, dense, low_ranks)
    gathered = from_everyone(swapped(rows), "col", Y_GROUPS)
    gathered = gathered.reshape(SIDE, SIDE, n, width)
    received = exchanged(products(n, gathered, *upper), "row", Q_GROUPS)
    dense, send = kernel_call(
        last_project_kernel,
        (shape((n, total), F32), shape((SIDE, packed, rank_cols), BF16)),
    )(received, turned, later)
    rows = finished(False, send, dense, up_ranks)
    return over_x(rows).astype(F32)


def solution(mesh):
    in_specs = (
        P(None, "row", "col"),
        P(None, "col", None),
        P(None, "col", None),
        P(None, "col", None),
        P(None, "col", None),
        P(),
        P(),
        P(None, "col", "row"),
        P(None, "col", "row"),
    )
    out_specs = P(None, "row", "col")
    return jax.shard_map(shards, mesh=mesh, in_specs=in_specs, out_specs=out_specs, check_vma=False)
```

```python
import jax
import jax.numpy as jnp
from jax import lax
from jax.experimental import pallas as pl
from jax.experimental.pallas import tpu as pltpu
from jax.sharding import PartitionSpec as P

RBLK = 32
BF16 = jnp.bfloat16
F32 = jnp.float32
SIDE = 4
X_GROUPS = [[SIDE * y + x for x in range(SIDE)] for y in range(SIDE)]
Z_GROUPS = [[2 * z + core for z in range(8)] for core in range(2)]


def routes(to):
    index = lambda q, j, y, x: (SIDE * q + j) * SIDE * SIDE + SIDE * y + x
    span = range(SIDE)
    return [
        (index(q, j, y, x), index(*to(q, j, y, x)))
        for q in span for j in span for y in span for x in span
    ]


def permuted(value, to):
    return lax.ppermute(value, ("row", "col"), routes(to))


def exchanged(value, axis, groups):
    return lax.all_to_all(value, axis, 0, 0, tiled=True, axis_index_groups=groups)


def over_x(value):
    return exchanged(value, "col", X_GROUPS)


def gathered_y(value):
    return [value] + [
        permuted(value, lambda q, j, y, x: (q, j, (y + s) % SIDE, x)) for s in range(1, SIDE)
    ]


def gathered_x(value):
    return [value] + [
        permuted(value, lambda q, j, y, x: (q, j, y, (x + s) % SIDE)) for s in range(1, SIDE)
    ]


def scattered_q(values):
    return [values[0]] + [
        permuted(values[s], lambda q, j, y, x: ((q + s) % SIDE, j, y, x))
        for s in range(1, SIDE)
    ]


def scattered_x(values):
    return [values[0]] + [
        permuted(values[s], lambda q, j, y, x: (q, j, y, (x + s) % SIDE))
        for s in range(1, SIDE)
    ]


def scattered_and_swapped(values):
    return [
        permuted(values[s], lambda q, j, y, x: (y, j, q, (x + s) % SIDE))
        for s in range(SIDE)
    ]


def own_tile():
    return lax.rem(lax.axis_index("col"), SIDE)


def wrapped(value):
    return lax.rem(value + 2 * SIDE, SIDE)


def swapped(value):
    return permuted(value, lambda q, j, y, x: (y, j, q, x))


def swap_core(value):
    return permuted(value, lambda q, j, y, x: (q, j ^ 1, y, x))


def swap_pair(value):
    return permuted(value, lambda q, j, y, x: (q, j ^ 2, y, x))


def dot(left, right):
    return jnp.dot(left, right, preferred_element_type=F32)


def dot_t(left, right):
    return lax.dot_general(
        left, right, (((1,), (1,)), ((), ())), preferred_element_type=F32
    )


def pair_of(i, j):
    high, low = max(i, j), min(i, j)
    return high * (high - 1) // 2 + low


def partners(tile):
    return [t for t in range(SIDE) if t != tile]


def kernel_call(body, out_shape, smem=(), flops=0, grid=None, in_specs=None, out_specs=None, scratch=()):
    def run(*args):
        specs = in_specs or [
            pl.BlockSpec(memory_space=pltpu.SMEM if at in smem else pltpu.VMEM)
            for at in range(len(args))
        ]
        outs = jax.tree.leaves(out_shape)
        moved = sum(a.size * a.dtype.itemsize for a in [*args, *outs])
        more = {} if grid is None else {"grid": grid, "out_specs": out_specs}
        return pl.pallas_call(
            body,
            out_shape=out_shape,
            in_specs=specs,
            scratch_shapes=list(scratch),
            compiler_params=pltpu.CompilerParams(vmem_limit_bytes=30 * 2**20),
            cost_estimate=pl.CostEstimate(
                flops=flops, bytes_accessed=moved, transcendentals=0
            ),
            **more,
        )(*args)

    return run


def pack_kernel(right_ref, low_ref, up_ref, *out_refs):
    n = right_ref.shape[1]
    rank_cols = low_ref.shape[2]
    share = rank_cols // lax.axis_size("row")
    row = lax.axis_index("row")
    at = lax.broadcasted_iota(jnp.int32, (share, rank_cols), 1)
    want = lax.broadcasted_iota(jnp.int32, (share, rank_cols), 0) + row * share
    pick = (at == want).astype(F32).astype(BF16)
    for s, out_ref in enumerate(out_refs):
        tile = wrapped(own_tile() + s)
        out_ref[:n] = right_ref[tile].astype(BF16)
        pieces = []
        for slot in range(SIDE - 1):
            pair, is_low = partner_pair(tile, slot)
            piece = jnp.where(is_low, dot_t(pick, low_ref[pair]), dot_t(pick, up_ref[pair]))
            pieces.append(piece)
        out_ref[n:] = jnp.concatenate(pieces, axis=0).astype(BF16)


def partner_pair(tile, slot):
    is_low = slot < tile
    partner = jnp.where(is_low, slot, slot + 1)
    high = jnp.where(is_low, tile, partner)
    low = jnp.where(is_low, partner, tile)
    return jnp.where(high == 1, 0, jnp.where(high == 2, 1, 3)) + low, is_low


def order_kernel(*refs):
    out_ref = refs[-1]
    for s in range(SIDE):
        out_ref[wrapped(own_tile() - s)] = refs[s][...].astype(out_ref.dtype)


def turn_kernel(low_ref, up_ref, out_ref):
    rank_cols = low_ref.shape[2]
    one = lax.broadcasted_iota(jnp.int32, (rank_cols, rank_cols), 0)
    two = lax.broadcasted_iota(jnp.int32, (rank_cols, rank_cols), 1)
    eye = (one == two).astype(F32).astype(BF16)
    for tile in range(SIDE):
        for slot, t in enumerate(partners(tile)):
            factor = (up_ref if t < tile else low_ref)[pair_of(tile, t)]
            out_ref[tile, slot * rank_cols : (slot + 1) * rank_cols] = dot_t(
                eye, factor
            ).astype(BF16)


def products_kernel(n, padded, count, *refs):
    x_refs, inverse_refs = refs[:SIDE], refs[SIDE : SIDE + count]
    out_refs = refs[SIDE + count : 2 * SIDE + count]
    joined_ref, extra_ref = refs[2 * SIDE + count :]
    lower, upper = inverse_refs[:SIDE], inverse_refs[SIDE:]
    rows = x_refs[0].shape[1]

    @pl.when(pl.program_id(0) == 0)
    def _():
        row = lax.axis_index("row")
        flip, q = lax.rem(row, SIDE), row // SIDE
        y = lax.axis_index("col") // SIDE
        for s in range(SIDE):
            t = wrapped(y - s - q)
            for at in range(SIDE):
                block = x_refs[s][at ^ flip]
                joined_ref[at, t, :rows] = block
                if rows > n:
                    extra_ref[at, t, : rows - n] = block[n:]

    width = joined_ref.shape[3]
    value = sum(
        dot_t(joined_ref[at].reshape(SIDE * padded, width), lower[at][...])
        for at in range(SIDE)
    )
    if rows > n:
        other = sum(
            dot_t(extra_ref[at].reshape(SIDE * (padded - n), width), upper[at][...])
            for at in range(SIDE)
        )
        share = (rows - n) // (SIDE - 1)
        slot = lax.broadcasted_iota(jnp.int32, (rows - n, value.shape[1]), 0) // share
    for t in range(SIDE):
        start = t * padded
        out_refs[t][:n] = value[start : start + n].astype(BF16)
        if rows > n:
            mine = value[start + n : start + rows]
            its = other[t * (padded - n) : t * (padded - n) + rows - n]
            out_refs[t][n:] = jnp.where(slot < own_tile(), mine, its).astype(BF16)


def products(n, gathered, *inverses):
    blocks, rows, width = gathered[0].shape
    total = inverses[0].shape[0]
    padded = rows + -rows % 16
    count = len(inverses)
    whole = pl.BlockSpec(gathered[0].shape, lambda a: (0, 0, 0))
    return kernel_call(
        lambda *refs: products_kernel(n, padded, count, *refs),
        [jax.ShapeDtypeStruct((rows, total), BF16)] * SIDE,
        flops=2 * SIDE * blocks * rows * width * total,
        grid=(total // 256,),
        in_specs=[whole] * SIDE
        + [pl.BlockSpec((256, width), lambda a: (a, 0)) for _ in inverses],
        out_specs=[pl.BlockSpec((rows, 256), lambda a: (0, a))] * SIDE,
        scratch=[
            pltpu.VMEM((blocks, SIDE, padded, width), BF16),
            pltpu.VMEM((blocks, SIDE, max(padded - n, 16), width), BF16),
        ],
    )(*gathered, *inverses)


def summed(refs):
    whole = refs[0][...].astype(F32)
    for ref in refs[1:]:
        whole = whole + ref[...].astype(F32)
    return whole


def total_kernel(n, *refs):
    dense_ref, extra_ref = refs[SIDE:]
    whole = summed(refs[:SIDE])
    dense_ref[...] = whole[:n]
    extra = whole[n:].astype(BF16)
    for at in range(extra_ref.shape[0]):
        extra_ref[at] = extra


def project(dense, turned_ref, slot, rank_cols):
    width = turned_ref.shape[2]
    return sum(
        dot_t(
            dense[:, at * width : (at + 1) * width],
            turned_ref[at, slot * rank_cols : (slot + 1) * rank_cols],
        )
        for at in range(SIDE)
    )


def couple_kernel(dense_ref, mine_ref, other_ref, turned_ref, extra_ref, send_ref, later_ref):
    n = dense_ref.shape[0]
    slots = SIDE - 1
    rank_cols = turned_ref.shape[1] // slots
    width = turned_ref.shape[2]
    share = mine_ref.shape[1] // slots
    even = lax.rem(lax.axis_index("row"), 2) == 0
    tile = lax.rem(lax.axis_index("col"), SIDE)
    for z in range(mine_ref.shape[0]):
        mine, other = mine_ref[z].astype(F32), other_ref[z].astype(F32)
        first = jnp.where(even, mine, other)
        second = jnp.where(even, other, mine)
        for slot in range(slots):
            at = slice(slot * share, (slot + 1) * share)
            start = slot * rank_cols + z * 2 * share
            extra_ref[start : start + 2 * share] = jnp.concatenate(
                [first[at], second[at]], axis=0
            ).astype(BF16)
    dense = dense_ref[...].astype(BF16)
    pieces = [project(dense, turned_ref, slot, rank_cols) for slot in range(slots)]

    def coupling(left, right):
        left = pl.multiple_of(left * rank_cols, rank_cols)
        right = pl.multiple_of(right * rank_cols, rank_cols)
        return sum(
            dot_t(
                extra_ref[pl.ds(left, rank_cols), at * width : (at + 1) * width],
                turned_ref[at, pl.ds(right, rank_cols), :],
            )
            for at in range(SIDE)
        )

    one = tile == 1
    pick = lambda a, b: jnp.where(one, a, b)
    pieces += [coupling(0, pick(1, 2)), coupling(pick(0, 1), 2)]
    send_ref[...] = jnp.concatenate(pieces, axis=0).astype(BF16)
    later_ref[:rank_cols] = coupling(pick(1, 2), 0).astype(BF16)
    later_ref[rank_cols:] = coupling(2, pick(0, 1)).astype(BF16)


def last_project_kernel(*refs):
    turned_ref, later_ref, dense_ref, send_ref = refs[SIDE:]
    slots = SIDE - 1
    rank_cols = turned_ref.shape[1] // slots
    whole = summed(refs[:SIDE])
    dense_ref[...] = whole
    dense = whole.astype(BF16)
    pieces = [project(dense, turned_ref, slot, rank_cols) for slot in range(slots)]
    send = jnp.concatenate(pieces, axis=0).astype(BF16)
    n = send.shape[0]
    send_ref[:n] = send
    send_ref[n:] = later_ref[...]


def add_kernel(*refs):
    refs[-1][...] = summed(refs[:-1]).astype(BF16)


def finish_kernel(is_lower, *refs):
    dense_ref, extra_ref, ranks_ref = refs[SIDE : SIDE + 3]
    out_refs, (sums_ref, held_ref) = refs[SIDE + 3 : -2], refs[-2:]
    for s in range(SIDE):
        sums_ref[wrapped(own_tile() - s)] = refs[s][...]
    n = dense_ref.shape[0]
    rank_cols = extra_ref.shape[0] // (SIDE - 1)
    width = held_ref.shape[2]
    tile = lax.rem(lax.axis_index("col"), SIDE)
    columns = lax.broadcasted_iota(jnp.int32, (n, rank_cols), 1)
    at_coupling = (SIDE - 1) * n
    coupling = {}
    order = list(range(SIDE)) if is_lower else list(range(SIDE))[::-1]
    first, second, third, last = order
    for which, key in enumerate(((third, second, first), (last, second, first))):
        coupling[key] = (second, which)
    for which, key in enumerate(((last, third, first), (last, third, second))):
        coupling[key] = (third, which)
    if not is_lower:
        coupling = {
            (0, 2, 3): (2, 0), (1, 2, 3): (2, 1), (0, 1, 2): (1, 0), (0, 1, 3): (1, 1)
        }
    masked = {}
    for at, source in enumerate(order):
        for target in order[at + 1 :]:
            slot = partners(source).index(target)
            value = sums_ref[source, slot * n : (slot + 1) * n].astype(F32)
            for before in order[:at]:
                held, which = coupling[target, source, before]
                start = at_coupling + which * rank_cols
                value = value - dot(
                    masked[source, before], sums_ref[held, start : start + rank_cols]
                )
            keep = columns < RBLK * ranks_ref[pair_of(source, target)]
            masked[target, source] = jnp.where(keep, value, 0.0).astype(BF16)
    result = dense_ref[...]
    nothing = jnp.zeros((n, rank_cols), BF16)
    for slot in range(SIDE - 1):
        mine = nothing
        for target in range(SIDE):
            source = partners(target)[slot]
            if (target, source) in masked:
                mine = jnp.where(tile == target, masked[target, source], mine)
        result = result - dot(
            mine, extra_ref[slot * rank_cols : (slot + 1) * rank_cols]
        )
    result = result.astype(BF16)
    if is_lower:
        for at in range(SIDE):
            out_refs[0][at] = result[:, at * width : (at + 1) * width]
    else:
        for at in range(SIDE):
            held_ref[at] = result[:, at * width : (at + 1) * width]
        for s in range(SIDE):
            out_refs[s][...] = held_ref[wrapped(own_tile() + s)]


def quad_of(value):
    far = swap_pair(value)
    return [value, swap_core(value), far, swap_core(far)]


def shards(
    right_sides, low_left, low_right, up_left, up_right, low_ranks, up_ranks, inv_lower, inv_upper
):
    n, width = right_sides.shape[1:]
    rank_cols = low_left.shape[2]
    slots = SIDE - 1
    share = rank_cols // lax.axis_size("row")
    total = SIDE * width
    shape = jax.ShapeDtypeStruct

    height = n + slots * share
    rows = kernel_call(pack_kernel, [shape((height, width), BF16)] * SIDE)(
        right_sides, low_left, up_left
    )
    inv_lower, inv_upper, low_right, up_right, *rows = lax.optimization_barrier(
        (inv_lower, inv_upper, low_right, up_right, *rows)
    )
    lower = quad_of(over_x(inv_lower).reshape(total, width))
    upper = quad_of(over_x(inv_upper).reshape(total, width))
    turned = over_x(
        kernel_call(turn_kernel, shape((SIDE, slots * rank_cols, width), BF16))(
            low_right, up_right
        )
    )
    rows = kernel_call(order_kernel, shape((SIDE, height, width), BF16))(
        *scattered_and_swapped(rows)
    )
    partial = products(n, gathered_y(rows), *lower, *upper)
    dense, extra = kernel_call(
        lambda *refs: total_kernel(n, *refs),
        (shape((n, total), F32), shape((8, slots * share, total), BF16)),
    )(*scattered_q(partial))
    mine = exchanged(extra, "row", Z_GROUPS)
    other = swap_core(mine)
    packed = slots * n + 2 * rank_cols
    extra, send, later = kernel_call(
        couple_kernel,
        (
            shape((slots * rank_cols, total), BF16),
            shape((packed, rank_cols), BF16),
            shape((2 * rank_cols, rank_cols), BF16),
        ),
    )(dense, mine, other, turned)

    def finished(is_lower, send, dense, ranks):
        sums = kernel_call(add_kernel, shape((packed, rank_cols), BF16))(*gathered_y(send))
        outs = [shape((SIDE, n, width), BF16)] if is_lower else [shape((n, width), BF16)] * SIDE
        return kernel_call(
            lambda *refs: finish_kernel(is_lower, *refs),
            outs,
            smem=(SIDE + 2,),
            scratch=[
                pltpu.VMEM((SIDE, packed, rank_cols), BF16),
                pltpu.VMEM((SIDE, n, width), BF16),
            ],
        )(*gathered_x(sums), dense, extra, ranks)

    [rows] = finished(True, send, dense, low_ranks)
    received = scattered_q(products(n, gathered_y(swapped(rows)), *upper))
    dense, send = kernel_call(
        last_project_kernel,
        (shape((n, total), F32), shape((packed, rank_cols), BF16)),
    )(*received, turned, later)
    rows = finished(False, send, dense, up_ranks)
    return kernel_call(order_kernel, shape((SIDE, n, width), F32))(*scattered_x(rows))


def solution(mesh):
    in_specs = (
        P(None, "row", "col"),
        P(None, "col", None),
        P(None, "col", None),
        P(None, "col", None),
        P(None, "col", None),
        P(),
        P(),
        P(None, "col", "row"),
        P(None, "col", "row"),
    )
    out_specs = P(None, "row", "col")
    return jax.shard_map(shards, mesh=mesh, in_specs=in_specs, out_specs=out_specs, check_vma=False)
```

```python
import jax
import jax.numpy as jnp
from jax import lax
from jax.experimental import pallas as pl
from jax.experimental.pallas import tpu as pltpu
from jax.sharding import PartitionSpec as P

RBLK = 32
BF16 = jnp.bfloat16
F32 = jnp.float32
SIDE = 4


def routes(to):
    index = lambda q, j, y, x: (SIDE * q + j) * SIDE * SIDE + SIDE * y + x
    span = range(SIDE)
    return [
        (index(q, j, y, x), index(*to(q, j, y, x)))
        for q in span for j in span for y in span for x in span
    ]


def permuted(value, to):
    return lax.ppermute(value, ("row", "col"), routes(to))


def gathered_y(value):
    return [value] + [
        permuted(value, lambda q, j, y, x: (q, j, (y + s) % SIDE, x)) for s in range(1, SIDE)
    ]


def gathered_x(value):
    return [value] + [
        permuted(value, lambda q, j, y, x: (q, j, y, (x + s) % SIDE)) for s in range(1, SIDE)
    ]


def scattered_q(values):
    return [values[0]] + [
        permuted(values[s], lambda q, j, y, x: ((q + s) % SIDE, j, y, x))
        for s in range(1, SIDE)
    ]


def scattered_x(values, sign=1):
    return [values[0]] + [
        permuted(values[s], lambda q, j, y, x: (q, j, y, (x + sign * s) % SIDE))
        for s in range(1, SIDE)
    ]


def gathered_z(value):
    def to(s):
        def move(q, j, y, x):
            z = (2 * q + j // 2 + s) % 8
            return (z // 2, z % 2 * 2 + j % 2, y, x)

        return move

    return [value] + [permuted(value, to(s)) for s in range(1, 8)]


def scattered_and_swapped(values):
    return [
        permuted(values[s], lambda q, j, y, x: (y, j, q, (x + s) % SIDE))
        for s in range(SIDE)
    ]


def own_tile():
    return lax.rem(lax.axis_index("col"), SIDE)


def wrapped(value):
    return lax.rem(value + 2 * SIDE, SIDE)


def swapped(value):
    return permuted(value, lambda q, j, y, x: (y, j, q, x))


def swap_core(value):
    return permuted(value, lambda q, j, y, x: (q, j ^ 1, y, x))


def swap_pair(value):
    return permuted(value, lambda q, j, y, x: (q, j ^ 2, y, x))


def dot(left, right):
    return jnp.dot(left, right, preferred_element_type=F32)


def dot_t(left, right):
    return lax.dot_general(
        left, right, (((1,), (1,)), ((), ())), preferred_element_type=F32
    )


def pair_of(i, j):
    high, low = max(i, j), min(i, j)
    return high * (high - 1) // 2 + low


def partners(tile):
    return [t for t in range(SIDE) if t != tile]


def kernel_call(body, out_shape, smem=(), flops=0, grid=None, in_specs=None, out_specs=None, scratch=()):
    def run(*args):
        specs = in_specs or [
            pl.BlockSpec(memory_space=pltpu.SMEM if at in smem else pltpu.VMEM)
            for at in range(len(args))
        ]
        outs = jax.tree.leaves(out_shape)
        moved = sum(a.size * a.dtype.itemsize for a in [*args, *outs])
        more = {} if grid is None else {"grid": grid, "out_specs": out_specs}
        return pl.pallas_call(
            body,
            out_shape=out_shape,
            in_specs=specs,
            scratch_shapes=list(scratch),
            compiler_params=pltpu.CompilerParams(vmem_limit_bytes=30 * 2**20),
            cost_estimate=pl.CostEstimate(
                flops=flops, bytes_accessed=moved, transcendentals=0
            ),
            **more,
        )(*args)

    return run


def pack_kernel(right_ref, low_ref, up_ref, *out_refs):
    n = right_ref.shape[1]
    rank_cols = low_ref.shape[2]
    share = rank_cols // lax.axis_size("row")
    row = lax.axis_index("row")
    at = lax.broadcasted_iota(jnp.int32, (share, rank_cols), 1)
    want = lax.broadcasted_iota(jnp.int32, (share, rank_cols), 0) + row * share
    pick = (at == want).astype(F32).astype(BF16)
    for s, out_ref in enumerate(out_refs):
        tile = wrapped(own_tile() + s)
        out_ref[:n] = right_ref[tile].astype(BF16)
        pieces = []
        for slot in range(SIDE - 1):
            pair, is_low = partner_pair(tile, slot)
            piece = jnp.where(is_low, dot_t(pick, low_ref[pair]), dot_t(pick, up_ref[pair]))
            pieces.append(piece)
        out_ref[n:] = jnp.concatenate(pieces, axis=0).astype(BF16)


def partner_pair(tile, slot):
    is_low = slot < tile
    partner = jnp.where(is_low, slot, slot + 1)
    high = jnp.where(is_low, tile, partner)
    low = jnp.where(is_low, partner, tile)
    return jnp.where(high == 1, 0, jnp.where(high == 2, 1, 3)) + low, is_low


def order_kernel(sign, *refs):
    out_ref = refs[-1]
    for s in range(SIDE):
        out_ref[wrapped(own_tile() - sign * s)] = refs[s][...].astype(out_ref.dtype)


def stack_kernel(*refs):
    rows = refs[0].shape[0]
    for s, ref in enumerate(refs[:-1]):
        refs[-1][s * rows : (s + 1) * rows] = ref[...]


def deal_kernel(lower_ref, upper_ref, *out_refs):
    for s in range(SIDE):
        tile = wrapped(own_tile() + s)
        out_refs[s][...] = lower_ref[tile]
        out_refs[SIDE + s][...] = upper_ref[tile]


def turn_kernel(low_ref, up_ref, *out_refs):
    rank_cols = low_ref.shape[2]
    one = lax.broadcasted_iota(jnp.int32, (rank_cols, rank_cols), 0)
    two = lax.broadcasted_iota(jnp.int32, (rank_cols, rank_cols), 1)
    eye = (one == two).astype(F32).astype(BF16)
    for s, out_ref in enumerate(out_refs):
        tile = wrapped(own_tile() + s)
        for slot in range(SIDE - 1):
            pair, is_low = partner_pair(tile, slot)
            factor = jnp.where(is_low, up_ref[pair], low_ref[pair])
            out_ref[slot * rank_cols : (slot + 1) * rank_cols] = dot_t(eye, factor).astype(BF16)


def products_kernel(n, padded, count, *refs):
    x_refs, inverse_refs = refs[:SIDE], refs[SIDE : SIDE + count]
    out_refs = refs[SIDE + count : -2]
    dense_refs, more_refs = out_refs[:SIDE], out_refs[SIDE:]
    joined_ref, extra_ref = refs[-2:]
    lower, upper = inverse_refs[:SIDE], inverse_refs[SIDE:]
    rows = x_refs[0].shape[1]

    @pl.when(pl.program_id(0) == 0)
    def _():
        row = lax.axis_index("row")
        flip, q = lax.rem(row, SIDE), row // SIDE
        y = lax.axis_index("col") // SIDE
        for s in range(SIDE):
            t = wrapped(y - s - q)
            for at in range(SIDE):
                block = x_refs[s][at ^ flip]
                joined_ref[at, t, :rows] = block
                if rows > n:
                    extra_ref[at, t, : rows - n] = block[n:]

    width = joined_ref.shape[3]
    value = sum(
        dot_t(joined_ref[at].reshape(SIDE * padded, width), lower[at][...])
        for at in range(SIDE)
    )
    if rows > n:
        other = sum(
            dot_t(extra_ref[at].reshape(SIDE * (padded - n), width), upper[at][...])
            for at in range(SIDE)
        )
        share = (rows - n) // (SIDE - 1)
        slot = lax.broadcasted_iota(jnp.int32, (rows - n, value.shape[1]), 0) // share
    for t in range(SIDE):
        start = t * padded
        dense_refs[t][...] = value[start : start + n].astype(BF16)
        if rows > n:
            mine = value[start + n : start + rows]
            its = other[t * (padded - n) : t * (padded - n) + rows - n]
            more_refs[t][...] = jnp.where(slot < own_tile(), mine, its).astype(BF16)


def products(n, gathered, *inverses):
    blocks, rows, width = gathered[0].shape
    total = inverses[0].shape[0]
    padded = rows + -rows % 16
    count = len(inverses)
    whole = pl.BlockSpec(gathered[0].shape, lambda a: (0, 0, 0))
    heights = [n] * SIDE + [rows - n] * SIDE * (rows > n)
    outs = kernel_call(
        lambda *refs: products_kernel(n, padded, count, *refs),
        [jax.ShapeDtypeStruct((height, total), BF16) for height in heights],
        flops=2 * SIDE * blocks * rows * width * total,
        grid=(total // 256,),
        in_specs=[whole] * SIDE
        + [pl.BlockSpec((256, width), lambda a: (a, 0)) for _ in inverses],
        out_specs=[pl.BlockSpec((height, 256), lambda a: (0, a)) for height in heights],
        scratch=[
            pltpu.VMEM((blocks, SIDE, padded, width), BF16),
            pltpu.VMEM((blocks, SIDE, max(padded - n, 16), width), BF16),
        ],
    )(*gathered, *inverses)
    return outs[:SIDE], outs[SIDE:]


def summed(refs):
    whole = refs[0][...].astype(F32)
    for ref in refs[1:]:
        whole = whole + ref[...].astype(F32)
    return whole


def project(dense, turned, slot, rank_cols):
    width = turned[0].shape[1]
    return sum(
        dot_t(
            dense[:, at * width : (at + 1) * width],
            turned[at][slot * rank_cols : (slot + 1) * rank_cols],
        )
        for at in range(SIDE)
    )


def couple_kernel(*refs):
    parts, refs = refs[:SIDE], refs[SIDE:]
    mine_ref, other_ref, refs = refs[0], refs[1], refs[2:]
    turned, (dense_ref, extra_ref, send_ref, later_ref) = refs[:SIDE], refs[SIDE:]
    slots = SIDE - 1
    rank_cols = turned[0].shape[0] // slots
    width = turned[0].shape[1]
    steps = mine_ref.shape[0]
    share = mine_ref.shape[1] // slots
    row = lax.axis_index("row")
    even = lax.rem(row, 2) == 0
    tile = own_tile()
    dense_ref[...] = summed(parts)
    for s in range(steps):
        z = lax.rem(row // 2 - s + steps, steps)
        mine, other = mine_ref[s].astype(F32), other_ref[s].astype(F32)
        first = jnp.where(even, mine, other)
        second = jnp.where(even, other, mine)
        for slot in range(slots):
            at = slice(slot * share, (slot + 1) * share)
            start = pl.multiple_of(slot * rank_cols + z * 2 * share, 2 * share)
            extra_ref[pl.ds(start, 2 * share), :] = jnp.concatenate(
                [first[at], second[at]], axis=0
            ).astype(BF16)
    dense = dense_ref[...].astype(BF16)
    pieces = [project(dense, turned, slot, rank_cols) for slot in range(slots)]

    def coupling(left, right):
        left = pl.multiple_of(left * rank_cols, rank_cols)
        right = pl.multiple_of(right * rank_cols, rank_cols)
        return sum(
            dot_t(
                extra_ref[pl.ds(left, rank_cols), at * width : (at + 1) * width],
                turned[at][pl.ds(right, rank_cols), :],
            )
            for at in range(SIDE)
        )

    one = tile == 1
    pick = lambda a, b: jnp.where(one, a, b)
    pieces += [coupling(0, pick(1, 2)), coupling(pick(0, 1), 2)]
    send_ref[...] = jnp.concatenate(pieces, axis=0).astype(BF16)
    later_ref[:rank_cols] = coupling(pick(1, 2), 0).astype(BF16)
    later_ref[rank_cols:] = coupling(2, pick(0, 1)).astype(BF16)


def last_project_kernel(*refs):
    turned, (later_ref, dense_ref, send_ref) = refs[SIDE : 2 * SIDE], refs[2 * SIDE :]
    slots = SIDE - 1
    rank_cols = turned[0].shape[0] // slots
    whole = summed(refs[:SIDE])
    dense_ref[...] = whole
    dense = whole.astype(BF16)
    pieces = [project(dense, turned, slot, rank_cols) for slot in range(slots)]
    send = jnp.concatenate(pieces, axis=0).astype(BF16)
    n = send.shape[0]
    send_ref[:n] = send
    send_ref[n:] = later_ref[...]


def add_kernel(*refs):
    refs[-1][...] = summed(refs[:-1]).astype(BF16)


def finish_kernel(is_lower, *refs):
    dense_ref, extra_ref, ranks_ref = refs[SIDE : SIDE + 3]
    out_refs, sums_ref = refs[SIDE + 3 : -1], refs[-1]
    for s in range(SIDE):
        sums_ref[wrapped(own_tile() - s)] = refs[s][...]
    n = dense_ref.shape[0]
    rank_cols = extra_ref.shape[0] // (SIDE - 1)
    width = dense_ref.shape[1] // SIDE
    tile = lax.rem(lax.axis_index("col"), SIDE)
    columns = lax.broadcasted_iota(jnp.int32, (n, rank_cols), 1)
    at_coupling = (SIDE - 1) * n
    coupling = {}
    order = list(range(SIDE)) if is_lower else list(range(SIDE))[::-1]
    first, second, third, last = order
    for which, key in enumerate(((third, second, first), (last, second, first))):
        coupling[key] = (second, which)
    for which, key in enumerate(((last, third, first), (last, third, second))):
        coupling[key] = (third, which)
    if not is_lower:
        coupling = {
            (0, 2, 3): (2, 0), (1, 2, 3): (2, 1), (0, 1, 2): (1, 0), (0, 1, 3): (1, 1)
        }
    masked = {}
    for at, source in enumerate(order):
        for target in order[at + 1 :]:
            slot = partners(source).index(target)
            value = sums_ref[source, slot * n : (slot + 1) * n].astype(F32)
            for before in order[:at]:
                held, which = coupling[target, source, before]
                start = at_coupling + which * rank_cols
                value = value - dot(
                    masked[source, before], sums_ref[held, start : start + rank_cols]
                )
            keep = columns < RBLK * ranks_ref[pair_of(source, target)]
            masked[target, source] = jnp.where(keep, value, 0.0).astype(BF16)
    result = dense_ref[...]
    nothing = jnp.zeros((n, rank_cols), BF16)
    for slot in range(SIDE - 1):
        mine = nothing
        for target in range(SIDE):
            source = partners(target)[slot]
            if (target, source) in masked:
                mine = jnp.where(tile == target, masked[target, source], mine)
        result = result - dot(
            mine, extra_ref[slot * rank_cols : (slot + 1) * rank_cols]
        )
    result = result.astype(BF16)
    for at in range(SIDE):
        block = result[:, at * width : (at + 1) * width]
        if is_lower:
            out_refs[0][wrapped(tile - at)] = block
        else:
            out_refs[at][...] = block


def quad_of(value):
    far = swap_pair(value)
    return [value, swap_core(value), far, swap_core(far)]


def shards(
    right_sides, low_left, low_right, up_left, up_right, low_ranks, up_ranks, inv_lower, inv_upper
):
    n, width = right_sides.shape[1:]
    rank_cols = low_left.shape[2]
    slots = SIDE - 1
    share = rank_cols // lax.axis_size("row")
    total = SIDE * width
    shape = jax.ShapeDtypeStruct

    height = n + slots * share
    rows = kernel_call(pack_kernel, [shape((height, width), BF16)] * SIDE)(
        right_sides, low_left, up_left
    )
    rows, inv_lower, inv_upper = lax.optimization_barrier((rows, inv_lower, inv_upper))
    rows = scattered_and_swapped(rows)
    dealt = kernel_call(deal_kernel, [shape((width, width), BF16)] * 2 * SIDE)(
        inv_lower, inv_upper
    )
    dealt, low_right, up_right = lax.optimization_barrier((dealt, low_right, up_right))
    stack = kernel_call(stack_kernel, shape((total, width), BF16))
    lower = quad_of(stack(*scattered_x(dealt[:SIDE])))
    upper = quad_of(stack(*scattered_x(dealt[SIDE:])))
    turned = scattered_x(
        kernel_call(turn_kernel, [shape((slots * rank_cols, width), BF16)] * SIDE)(
            low_right, up_right
        )
    )
    rows = kernel_call(
        lambda *refs: order_kernel(1, *refs), shape((SIDE, height, width), BF16)
    )(*rows)
    dense, extra = products(n, gathered_y(rows), *lower, *upper)
    extra = scattered_q(extra)
    dense = scattered_q(dense)
    extra = kernel_call(add_kernel, shape((slots * share, total), BF16))(*extra)
    mine = jnp.stack(gathered_z(extra))
    other = swap_core(mine)
    packed = slots * n + 2 * rank_cols
    dense, extra, send, later = kernel_call(
        couple_kernel,
        (
            shape((n, total), F32),
            shape((slots * rank_cols, total), BF16),
            shape((packed, rank_cols), BF16),
            shape((2 * rank_cols, rank_cols), BF16),
        ),
    )(*dense, mine, other, *turned)

    def finished(is_lower, send, dense, ranks):
        sums = kernel_call(add_kernel, shape((packed, rank_cols), BF16))(*gathered_y(send))
        outs = [shape((SIDE, n, width), BF16)] if is_lower else [shape((n, width), BF16)] * SIDE
        return kernel_call(
            lambda *refs: finish_kernel(is_lower, *refs),
            outs,
            smem=(SIDE + 2,),
            scratch=[pltpu.VMEM((SIDE, packed, rank_cols), BF16)],
        )(*gathered_x(sums), dense, extra, ranks)

    [rows] = finished(True, send, dense, low_ranks)
    parts, _ = products(n, gathered_y(swapped(rows)), *upper)
    dense, send = kernel_call(
        last_project_kernel,
        (shape((n, total), F32), shape((packed, rank_cols), BF16)),
    )(*scattered_q(parts), *turned, later)
    rows = finished(False, send, dense, up_ranks)
    return kernel_call(
        lambda *refs: order_kernel(-1, *refs), shape((SIDE, n, width), F32)
    )(*scattered_x(rows, -1))


def solution(mesh):
    in_specs = (
        P(None, "row", "col"),
        P(None, "col", None),
        P(None, "col", None),
        P(None, "col", None),
        P(None, "col", None),
        P(),
        P(),
        P(None, "col", "row"),
        P(None, "col", "row"),
    )
    out_specs = P(None, "row", "col")
    return jax.shard_map(shards, mesh=mesh, in_specs=in_specs, out_specs=out_specs, check_vma=False)
```

```python
import jax
import jax.numpy as jnp
from jax import lax
from jax.experimental import pallas as pl
from jax.experimental.pallas import tpu as pltpu
from jax.sharding import PartitionSpec as P

RBLK = 32
BF16 = jnp.bfloat16
F32 = jnp.float32
SIDE = 4
Z_GROUPS = [[2 * z + core for z in range(8)] for core in range(2)]


def routes(to):
    index = lambda q, j, y, x: (SIDE * q + j) * SIDE * SIDE + SIDE * y + x
    span = range(SIDE)
    return [
        (index(q, j, y, x), index(*to(q, j, y, x)))
        for q in span for j in span for y in span for x in span
    ]


def permuted(value, to):
    return lax.ppermute(value, ("row", "col"), routes(to))


def gathered_y(value):
    return [value] + [
        permuted(value, lambda q, j, y, x: (q, j, (y + s) % SIDE, x)) for s in range(1, SIDE)
    ]


def gathered_x(value):
    return [value] + [
        permuted(value, lambda q, j, y, x: (q, j, y, (x + s) % SIDE)) for s in range(1, SIDE)
    ]


def scattered_q(values):
    return [values[0]] + [
        permuted(values[s], lambda q, j, y, x: ((q + s) % SIDE, j, y, x))
        for s in range(1, SIDE)
    ]


def scattered_x(values, sign=1):
    return [values[0]] + [
        permuted(values[s], lambda q, j, y, x: (q, j, y, (x + sign * s) % SIDE))
        for s in range(1, SIDE)
    ]


def from_every_z(value):
    return lax.all_to_all(value, "row", 0, 0, tiled=True, axis_index_groups=Z_GROUPS)


def own_tile():
    return lax.rem(lax.axis_index("col"), SIDE)


def wrapped(value):
    return lax.rem(value + 2 * SIDE, SIDE)


def swapped(value):
    return permuted(value, lambda q, j, y, x: (y, j, q, x))


def swap_core(value):
    return permuted(value, lambda q, j, y, x: (q, j ^ 1, y, x))


def swap_pair(value):
    return permuted(value, lambda q, j, y, x: (q, j ^ 2, y, x))


def dot(left, right):
    return jnp.dot(left, right, preferred_element_type=F32)


def dot_t(left, right):
    return lax.dot_general(
        left, right, (((1,), (1,)), ((), ())), preferred_element_type=F32
    )


def pair_of(i, j):
    high, low = max(i, j), min(i, j)
    return high * (high - 1) // 2 + low


def partners(tile):
    return [t for t in range(SIDE) if t != tile]


def kernel_call(body, out_shape, smem=(), flops=0, grid=None, in_specs=None, out_specs=None, scratch=()):
    def run(*args):
        specs = in_specs or [
            pl.BlockSpec(memory_space=pltpu.SMEM if at in smem else pltpu.VMEM)
            for at in range(len(args))
        ]
        outs = jax.tree.leaves(out_shape)
        moved = sum(a.size * a.dtype.itemsize for a in [*args, *outs])
        more = {} if grid is None else {"grid": grid, "out_specs": out_specs}
        return pl.pallas_call(
            body,
            out_shape=out_shape,
            in_specs=specs,
            scratch_shapes=list(scratch),
            compiler_params=pltpu.CompilerParams(vmem_limit_bytes=30 * 2**20),
            cost_estimate=pl.CostEstimate(
                flops=flops, bytes_accessed=moved, transcendentals=0
            ),
            **more,
        )(*args)

    return run


def pack_kernel(right_ref, low_ref, up_ref, *out_refs):
    n = right_ref.shape[1]
    rank_cols = low_ref.shape[2]
    share = rank_cols // lax.axis_size("row")
    row = lax.axis_index("row")
    at = lax.broadcasted_iota(jnp.int32, (share, rank_cols), 1)
    want = lax.broadcasted_iota(jnp.int32, (share, rank_cols), 0) + row * share
    pick = (at == want).astype(F32).astype(BF16)
    for s, out_ref in enumerate(out_refs):
        tile = wrapped(own_tile() + s)
        out_ref[:n] = right_ref[tile].astype(BF16)
        pieces = []
        for slot in range(SIDE - 1):
            pair, is_low = partner_pair(tile, slot)
            piece = jnp.where(is_low, dot_t(pick, low_ref[pair]), dot_t(pick, up_ref[pair]))
            pieces.append(piece)
        out_ref[n:] = jnp.concatenate(pieces, axis=0).astype(BF16)


def partner_pair(tile, slot):
    is_low = slot < tile
    partner = jnp.where(is_low, slot, slot + 1)
    high = jnp.where(is_low, tile, partner)
    low = jnp.where(is_low, partner, tile)
    return jnp.where(high == 1, 0, jnp.where(high == 2, 1, 3)) + low, is_low


def order_kernel(sign, *refs):
    out_ref = refs[-1]
    for s in range(SIDE):
        out_ref[wrapped(own_tile() - sign * s)] = refs[s][...].astype(out_ref.dtype)


def stack_kernel(*refs):
    rows = refs[0].shape[0]
    for s, ref in enumerate(refs[:-1]):
        refs[-1][s * rows : (s + 1) * rows] = ref[...]


def deal_kernel(lower_ref, upper_ref, *out_refs):
    for s in range(SIDE):
        tile = wrapped(own_tile() + s)
        out_refs[s][...] = lower_ref[tile]
        out_refs[SIDE + s][...] = upper_ref[tile]


def turn_kernel(low_ref, up_ref, *out_refs):
    rank_cols = low_ref.shape[2]
    one = lax.broadcasted_iota(jnp.int32, (rank_cols, rank_cols), 0)
    two = lax.broadcasted_iota(jnp.int32, (rank_cols, rank_cols), 1)
    eye = (one == two).astype(F32).astype(BF16)
    for s, out_ref in enumerate(out_refs):
        tile = wrapped(own_tile() + s)
        for slot in range(SIDE - 1):
            pair, is_low = partner_pair(tile, slot)
            factor = jnp.where(is_low, up_ref[pair], low_ref[pair])
            out_ref[slot * rank_cols : (slot + 1) * rank_cols] = dot_t(eye, factor).astype(BF16)


def products_kernel(n, padded, count, *refs):
    x_refs, inverse_refs = refs[:SIDE], refs[SIDE : SIDE + count]
    out_refs = refs[SIDE + count : -2]
    joined_ref, extra_ref = refs[-2:]
    lower, upper = inverse_refs[:SIDE], inverse_refs[SIDE:]
    rows = x_refs[0].shape[1]

    @pl.when(pl.program_id(0) == 0)
    def _():
        row = lax.axis_index("row")
        flip, q = lax.rem(row, SIDE), row // SIDE
        y = lax.axis_index("col") // SIDE
        for s in range(SIDE):
            t = wrapped(y - s - q)
            for at in range(SIDE):
                block = x_refs[s][at ^ flip]
                joined_ref[at, t, :rows] = block
                if rows > n:
                    extra_ref[at, t, : rows - n] = block[n:]

    width = joined_ref.shape[3]
    value = sum(
        dot_t(joined_ref[at].reshape(SIDE * padded, width), lower[at][...])
        for at in range(SIDE)
    )
    if rows > n:
        other = sum(
            dot_t(extra_ref[at].reshape(SIDE * (padded - n), width), upper[at][...])
            for at in range(SIDE)
        )
        share = (rows - n) // (SIDE - 1)
        slot = lax.broadcasted_iota(jnp.int32, (rows - n, value.shape[1]), 0) // share
    for t in range(SIDE):
        start = t * padded
        out_refs[t][:n] = value[start : start + n].astype(BF16)
        if rows > n:
            mine = value[start + n : start + rows]
            its = other[t * (padded - n) : t * (padded - n) + rows - n]
            out_refs[t][n:] = jnp.where(slot < own_tile(), mine, its).astype(BF16)


def products(n, gathered, *inverses):
    blocks, rows, width = gathered[0].shape
    total = inverses[0].shape[0]
    padded = rows + -rows % 16
    count = len(inverses)
    whole = pl.BlockSpec(gathered[0].shape, lambda a: (0, 0, 0))
    return kernel_call(
        lambda *refs: products_kernel(n, padded, count, *refs),
        [jax.ShapeDtypeStruct((rows, total), BF16)] * SIDE,
        flops=2 * SIDE * blocks * rows * width * total,
        grid=(total // 256,),
        in_specs=[whole] * SIDE
        + [pl.BlockSpec((256, width), lambda a: (a, 0)) for _ in inverses],
        out_specs=[pl.BlockSpec((rows, 256), lambda a: (0, a))] * SIDE,
        scratch=[
            pltpu.VMEM((blocks, SIDE, padded, width), BF16),
            pltpu.VMEM((blocks, SIDE, max(padded - n, 16), width), BF16),
        ],
    )(*gathered, *inverses)


def summed(refs):
    whole = refs[0][...].astype(F32)
    for ref in refs[1:]:
        whole = whole + ref[...].astype(F32)
    return whole


def total_kernel(n, *refs):
    dense_ref, extra_ref = refs[SIDE:]
    whole = summed(refs[:SIDE])
    dense_ref[...] = whole[:n]
    extra = whole[n:].astype(BF16)
    for at in range(extra_ref.shape[0]):
        extra_ref[at] = extra


def project(dense, turned, slot, rank_cols):
    width = turned[0].shape[1]
    return sum(
        dot_t(
            dense[:, at * width : (at + 1) * width],
            turned[at][slot * rank_cols : (slot + 1) * rank_cols],
        )
        for at in range(SIDE)
    )


def couple_kernel(dense_ref, mine_ref, other_ref, *refs):
    turned, (extra_ref, send_ref, later_ref) = refs[:SIDE], refs[SIDE:]
    slots = SIDE - 1
    rank_cols = turned[0].shape[0] // slots
    width = turned[0].shape[1]
    share = mine_ref.shape[1] // slots
    even = lax.rem(lax.axis_index("row"), 2) == 0
    tile = own_tile()
    for z in range(mine_ref.shape[0]):
        mine, other = mine_ref[z].astype(F32), other_ref[z].astype(F32)
        first = jnp.where(even, mine, other)
        second = jnp.where(even, other, mine)
        for slot in range(slots):
            at = slice(slot * share, (slot + 1) * share)
            start = slot * rank_cols + z * 2 * share
            extra_ref[start : start + 2 * share] = jnp.concatenate(
                [first[at], second[at]], axis=0
            ).astype(BF16)
    dense = dense_ref[...].astype(BF16)
    pieces = [project(dense, turned, slot, rank_cols) for slot in range(slots)]

    def coupling(left, right):
        left = pl.multiple_of(left * rank_cols, rank_cols)
        right = pl.multiple_of(right * rank_cols, rank_cols)
        return sum(
            dot_t(
                extra_ref[pl.ds(left, rank_cols), at * width : (at + 1) * width],
                turned[at][pl.ds(right, rank_cols), :],
            )
            for at in range(SIDE)
        )

    one = tile == 1
    pick = lambda a, b: jnp.where(one, a, b)
    pieces += [coupling(0, pick(1, 2)), coupling(pick(0, 1), 2)]
    send_ref[...] = jnp.concatenate(pieces, axis=0).astype(BF16)
    later_ref[:rank_cols] = coupling(pick(1, 2), 0).astype(BF16)
    later_ref[rank_cols:] = coupling(2, pick(0, 1)).astype(BF16)


def last_project_kernel(*refs):
    turned, (later_ref, dense_ref, send_ref) = refs[SIDE : 2 * SIDE], refs[2 * SIDE :]
    slots = SIDE - 1
    rank_cols = turned[0].shape[0] // slots
    whole = summed(refs[:SIDE])
    dense_ref[...] = whole
    dense = whole.astype(BF16)
    pieces = [project(dense, turned, slot, rank_cols) for slot in range(slots)]
    send = jnp.concatenate(pieces, axis=0).astype(BF16)
    n = send.shape[0]
    send_ref[:n] = send
    send_ref[n:] = later_ref[...]


def add_kernel(*refs):
    refs[-1][...] = summed(refs[:-1]).astype(BF16)


def finish_kernel(is_lower, *refs):
    dense_ref, extra_ref, ranks_ref = refs[SIDE : SIDE + 3]
    out_refs, sums_ref = refs[SIDE + 3 : -1], refs[-1]
    for s in range(SIDE):
        sums_ref[wrapped(own_tile() - s)] = refs[s][...]
    n = dense_ref.shape[0]
    rank_cols = extra_ref.shape[0] // (SIDE - 1)
    width = dense_ref.shape[1] // SIDE
    tile = lax.rem(lax.axis_index("col"), SIDE)
    columns = lax.broadcasted_iota(jnp.int32, (n, rank_cols), 1)
    at_coupling = (SIDE - 1) * n
    coupling = {}
    order = list(range(SIDE)) if is_lower else list(range(SIDE))[::-1]
    first, second, third, last = order
    for which, key in enumerate(((third, second, first), (last, second, first))):
        coupling[key] = (second, which)
    for which, key in enumerate(((last, third, first), (last, third, second))):
        coupling[key] = (third, which)
    if not is_lower:
        coupling = {
            (0, 2, 3): (2, 0), (1, 2, 3): (2, 1), (0, 1, 2): (1, 0), (0, 1, 3): (1, 1)
        }
    masked = {}
    for at, source in enumerate(order):
        for target in order[at + 1 :]:
            slot = partners(source).index(target)
            value = sums_ref[source, slot * n : (slot + 1) * n].astype(F32)
            for before in order[:at]:
                held, which = coupling[target, source, before]
                start = at_coupling + which * rank_cols
                value = value - dot(
                    masked[source, before], sums_ref[held, start : start + rank_cols]
                )
            keep = columns < RBLK * ranks_ref[pair_of(source, target)]
            masked[target, source] = jnp.where(keep, value, 0.0).astype(BF16)
    result = dense_ref[...]
    nothing = jnp.zeros((n, rank_cols), BF16)
    for slot in range(SIDE - 1):
        mine = nothing
        for target in range(SIDE):
            source = partners(target)[slot]
            if (target, source) in masked:
                mine = jnp.where(tile == target, masked[target, source], mine)
        result = result - dot(
            mine, extra_ref[slot * rank_cols : (slot + 1) * rank_cols]
        )
    result = result.astype(BF16)
    for at in range(SIDE):
        block = result[:, at * width : (at + 1) * width]
        if is_lower:
            out_refs[0][wrapped(tile - at)] = block
        else:
            out_refs[at][...] = block


def shards(
    right_sides, low_left, low_right, up_left, up_right, low_ranks, up_ranks, inv_lower, inv_upper
):
    n, width = right_sides.shape[1:]
    rank_cols = low_left.shape[2]
    slots = SIDE - 1
    share = rank_cols // lax.axis_size("row")
    total = SIDE * width
    shape = jax.ShapeDtypeStruct

    height = n + slots * share
    rows = kernel_call(pack_kernel, [shape((height, width), BF16)] * SIDE)(
        right_sides, low_left, up_left
    )
    tied = lax.optimization_barrier
    rows = scattered_x(rows)
    rows, inv_lower, inv_upper = tied((rows, inv_lower, inv_upper))
    dealt = kernel_call(deal_kernel, [shape((width, width), BF16)] * 2 * SIDE)(
        inv_lower, inv_upper
    )
    rows = kernel_call(
        lambda *refs: order_kernel(1, *refs), shape((SIDE, height, width), BF16)
    )(*rows)
    rows = swapped(rows)
    stack = kernel_call(stack_kernel, shape((total, width), BF16))
    lower = stack(*scattered_x(dealt[:SIDE]))
    far_lower = swap_pair(lower)
    upper_parts, lower = tied((dealt[SIDE:], lower))
    upper = stack(*scattered_x(upper_parts))
    near = (swap_core(lower), swap_core(upper))
    gathered = gathered_y(rows)
    far_lower, upper, near, gathered = tied((far_lower, upper, near, gathered))
    far_upper = swap_pair(upper)
    lower = [lower, near[0], far_lower, swap_core(far_lower)]
    low_right, up_right, gathered = tied((low_right, up_right, gathered))
    turned = scattered_x(
        kernel_call(turn_kernel, [shape((slots * rank_cols, width), BF16)] * SIDE)(
            low_right, up_right
        )
    )
    turned, far_upper = tied((turned, far_upper))
    upper = [upper, near[1], far_upper, swap_core(far_upper)]
    dense, extra = kernel_call(
        lambda *refs: total_kernel(n, *refs),
        (shape((n, total), F32), shape((8, slots * share, total), BF16)),
    )(*scattered_q(products(n, gathered, *lower, *upper)))
    mine = from_every_z(extra)
    packed = slots * n + 2 * rank_cols
    extra, send, later = kernel_call(
        couple_kernel,
        (
            shape((slots * rank_cols, total), BF16),
            shape((packed, rank_cols), BF16),
            shape((2 * rank_cols, rank_cols), BF16),
        ),
    )(dense, mine, swap_core(mine), *turned)

    def finished(is_lower, send, dense, ranks):
        sums = kernel_call(add_kernel, shape((packed, rank_cols), BF16))(*gathered_y(send))
        outs = [shape((SIDE, n, width), BF16)] if is_lower else [shape((n, width), BF16)] * SIDE
        return kernel_call(
            lambda *refs: finish_kernel(is_lower, *refs),
            outs,
            smem=(SIDE + 2,),
            scratch=[pltpu.VMEM((SIDE, packed, rank_cols), BF16)],
        )(*gathered_x(sums), dense, extra, ranks)

    [rows] = finished(True, send, dense, low_ranks)
    parts = products(n, gathered_y(swapped(rows)), *upper)
    dense, send = kernel_call(
        last_project_kernel,
        (shape((n, total), F32), shape((packed, rank_cols), BF16)),
    )(*scattered_q(parts), *turned, later)
    rows = finished(False, send, dense, up_ranks)
    return kernel_call(
        lambda *refs: order_kernel(-1, *refs), shape((SIDE, n, width), F32)
    )(*scattered_x(rows, -1))


def solution(mesh):
    in_specs = (
        P(None, "row", "col"),
        P(None, "col", None),
        P(None, "col", None),
        P(None, "col", None),
        P(None, "col", None),
        P(),
        P(),
        P(None, "col", "row"),
        P(None, "col", "row"),
    )
    out_specs = P(None, "row", "col")
    return jax.shard_map(shards, mesh=mesh, in_specs=in_specs, out_specs=out_specs, check_vma=False)
```

```python
import jax
import jax.numpy as jnp
from jax import lax
from jax.experimental import pallas as pl
from jax.experimental.pallas import tpu as pltpu
from jax.sharding import PartitionSpec as P

RBLK = 32
BF16 = jnp.bfloat16
F32 = jnp.float32
SIDE = 4
Z_GROUPS = [[2 * z + core for z in range(8)] for core in range(2)]


def routes(to):
    index = lambda q, j, y, x: (SIDE * q + j) * SIDE * SIDE + SIDE * y + x
    span = range(SIDE)
    return [
        (index(q, j, y, x), index(*to(q, j, y, x)))
        for q in span for j in span for y in span for x in span
    ]


def permuted(value, to):
    return lax.ppermute(value, ("row", "col"), routes(to))


def gathered_y(value):
    return [value] + [
        permuted(value, lambda q, j, y, x: (q, j, (y + s) % SIDE, x)) for s in range(1, SIDE)
    ]


def gathered_x(value):
    return [value] + [
        permuted(value, lambda q, j, y, x: (q, j, y, (x + s) % SIDE)) for s in range(1, SIDE)
    ]


def scattered_q(values):
    return [values[0]] + [
        permuted(values[s], lambda q, j, y, x: ((q + s) % SIDE, j, y, x))
        for s in range(1, SIDE)
    ]


def scattered_x(values, sign=1):
    return [values[0]] + [
        permuted(values[s], lambda q, j, y, x: (q, j, y, (x + sign * s) % SIDE))
        for s in range(1, SIDE)
    ]


def from_every_z(value):
    return lax.all_to_all(value, "row", 0, 0, tiled=True, axis_index_groups=Z_GROUPS)


def own_tile():
    return lax.rem(lax.axis_index("col"), SIDE)


def wrapped(value):
    return lax.rem(value + 2 * SIDE, SIDE)


def swapped(value):
    return permuted(value, lambda q, j, y, x: (y, j, q, x))


def swap_core(value):
    return permuted(value, lambda q, j, y, x: (q, j ^ 1, y, x))


def swap_pair(value):
    return permuted(value, lambda q, j, y, x: (q, j ^ 2, y, x))


def dot(left, right):
    return jnp.dot(left, right, preferred_element_type=F32)


def dot_t(left, right):
    return lax.dot_general(
        left, right, (((1,), (1,)), ((), ())), preferred_element_type=F32
    )


def pair_of(i, j):
    high, low = max(i, j), min(i, j)
    return high * (high - 1) // 2 + low


def partners(tile):
    return [t for t in range(SIDE) if t != tile]


def kernel_call(body, out_shape, smem=(), flops=0, grid=None, in_specs=None, out_specs=None, scratch=()):
    def run(*args):
        specs = in_specs or [
            pl.BlockSpec(memory_space=pltpu.SMEM if at in smem else pltpu.VMEM)
            for at in range(len(args))
        ]
        outs = jax.tree.leaves(out_shape)
        moved = sum(a.size * a.dtype.itemsize for a in [*args, *outs])
        more = {} if grid is None else {"grid": grid, "out_specs": out_specs}
        return pl.pallas_call(
            body,
            out_shape=out_shape,
            in_specs=specs,
            scratch_shapes=list(scratch),
            compiler_params=pltpu.CompilerParams(vmem_limit_bytes=30 * 2**20),
            cost_estimate=pl.CostEstimate(
                flops=flops, bytes_accessed=moved, transcendentals=0
            ),
            **more,
        )(*args)

    return run


def pack_kernel(right_ref, low_ref, up_ref, *out_refs):
    n = right_ref.shape[1]
    rank_cols = low_ref.shape[2]
    share = rank_cols // lax.axis_size("row")
    row = lax.axis_index("row")
    at = lax.broadcasted_iota(jnp.int32, (share, rank_cols), 1)
    want = lax.broadcasted_iota(jnp.int32, (share, rank_cols), 0) + row * share
    pick = (at == want).astype(F32).astype(BF16)
    for s, out_ref in enumerate(out_refs):
        tile = wrapped(own_tile() + s)
        out_ref[:n] = right_ref[tile].astype(BF16)
        pieces = []
        for slot in range(SIDE - 1):
            pair, is_low = partner_pair(tile, slot)
            piece = jnp.where(is_low, dot_t(pick, low_ref[pair]), dot_t(pick, up_ref[pair]))
            pieces.append(piece)
        out_ref[n:] = jnp.concatenate(pieces, axis=0).astype(BF16)


def partner_pair(tile, slot):
    is_low = slot < tile
    partner = jnp.where(is_low, slot, slot + 1)
    high = jnp.where(is_low, tile, partner)
    low = jnp.where(is_low, partner, tile)
    return jnp.where(high == 1, 0, jnp.where(high == 2, 1, 3)) + low, is_low


def order_kernel(sign, *refs):
    out_ref = refs[-1]
    for s in range(SIDE):
        out_ref[wrapped(own_tile() - sign * s)] = refs[s][...].astype(out_ref.dtype)


def stack_kernel(*refs):
    rows = refs[0].shape[0]
    for s, ref in enumerate(refs[:-1]):
        refs[-1][s * rows : (s + 1) * rows] = ref[...]


def deal_kernel(inverse_ref, *out_refs):
    for s in range(SIDE):
        out_refs[s][...] = inverse_ref[wrapped(own_tile() + s)]


def turn_kernel(low_ref, up_ref, *out_refs):
    rank_cols = low_ref.shape[2]
    one = lax.broadcasted_iota(jnp.int32, (rank_cols, rank_cols), 0)
    two = lax.broadcasted_iota(jnp.int32, (rank_cols, rank_cols), 1)
    eye = (one == two).astype(F32).astype(BF16)
    for s, out_ref in enumerate(out_refs):
        tile = wrapped(own_tile() + s)
        for slot in range(SIDE - 1):
            pair, is_low = partner_pair(tile, slot)
            factor = jnp.where(is_low, up_ref[pair], low_ref[pair])
            out_ref[slot * rank_cols : (slot + 1) * rank_cols] = dot_t(eye, factor).astype(BF16)


def products_kernel(start, rows, padded, *refs):
    x_refs, inverse_refs = refs[:SIDE], refs[SIDE : 2 * SIDE]
    out_refs, joined_ref = refs[2 * SIDE : -1], refs[-1]

    @pl.when(pl.program_id(0) == 0)
    def _():
        row = lax.axis_index("row")
        flip, q = lax.rem(row, SIDE), row // SIDE
        y = lax.axis_index("col") // SIDE
        for s in range(SIDE):
            t = wrapped(y - s - q)
            for at in range(SIDE):
                joined_ref[at, t, :rows] = x_refs[s][at ^ flip][start : start + rows]

    width = joined_ref.shape[3]
    value = sum(
        dot_t(joined_ref[at].reshape(SIDE * padded, width), inverse_refs[at][...])
        for at in range(SIDE)
    )
    for t in range(SIDE):
        out_refs[t][...] = value[t * padded : t * padded + rows].astype(BF16)


def products(start, rows, gathered, inverses):
    blocks, all_rows, width = gathered[0].shape
    total = inverses[0].shape[0]
    padded = rows + -rows % 16
    whole = pl.BlockSpec(gathered[0].shape, lambda a: (0, 0, 0))
    return kernel_call(
        lambda *refs: products_kernel(start, rows, padded, *refs),
        [jax.ShapeDtypeStruct((rows, total), BF16)] * SIDE,
        flops=2 * SIDE * blocks * rows * width * total,
        grid=(total // 256,),
        in_specs=[whole] * SIDE
        + [pl.BlockSpec((256, width), lambda a: (a, 0)) for _ in inverses],
        out_specs=[pl.BlockSpec((rows, 256), lambda a: (0, a))] * SIDE,
        scratch=[pltpu.VMEM((blocks, SIDE, padded, width), BF16)],
    )(*gathered, *inverses)


def summed(refs):
    whole = refs[0][...].astype(F32)
    for ref in refs[1:]:
        whole = whole + ref[...].astype(F32)
    return whole


def total_kernel(n, *refs):
    dense_refs, extra_ref = refs[SIDE:-1], refs[-1]
    whole = summed(refs[:SIDE])
    for dense_ref in dense_refs:
        dense_ref[...] = whole[:n]
    extra = whole[n:].astype(BF16)
    for at in range(extra_ref.shape[0]):
        extra_ref[at] = extra


def project(dense, turned, slot, rank_cols):
    width = turned[0].shape[1]
    return sum(
        dot_t(
            dense[:, at * width : (at + 1) * width],
            turned[at][slot * rank_cols : (slot + 1) * rank_cols],
        )
        for at in range(SIDE)
    )


def couple_kernel(is_lower, mine_ref, other_ref, *refs):
    turned, refs = refs[:SIDE], refs[SIDE:]
    extra_ref, send_ref = refs[-2:]
    slots = SIDE - 1
    rank_cols = turned[0].shape[0] // slots
    width = turned[0].shape[1]
    share = mine_ref.shape[1] // slots
    even = lax.rem(lax.axis_index("row"), 2) == 0
    for z in range(mine_ref.shape[0]):
        mine, other = mine_ref[z].astype(F32), other_ref[z].astype(F32)
        first = jnp.where(even, mine, other)
        second = jnp.where(even, other, mine)
        for slot in range(slots):
            at = slice(slot * share, (slot + 1) * share)
            start = slot * rank_cols + z * 2 * share
            extra_ref[start : start + 2 * share] = jnp.concatenate(
                [first[at], second[at]], axis=0
            ).astype(BF16)

    def coupling(left, right):
        left = pl.multiple_of(left * rank_cols, rank_cols)
        right = pl.multiple_of(right * rank_cols, rank_cols)
        return sum(
            dot_t(
                extra_ref[pl.ds(left, rank_cols), at * width : (at + 1) * width],
                turned[at][pl.ds(right, rank_cols), :],
            )
            for at in range(SIDE)
        )

    one = own_tile() == 1
    pick = lambda a, b: jnp.where(one, a, b)
    if is_lower:
        dense = refs[0][...].astype(BF16)
        pieces = [project(dense, turned, slot, rank_cols) for slot in range(slots)]
        pieces += [coupling(0, pick(1, 2)), coupling(pick(0, 1), 2)]
    else:
        pieces = [coupling(pick(1, 2), 0), coupling(2, pick(0, 1))]
    send_ref[...] = jnp.concatenate(pieces, axis=0).astype(BF16)


def last_project_kernel(*refs):
    turned, (later_ref, dense_ref, send_ref) = refs[SIDE : 2 * SIDE], refs[2 * SIDE :]
    slots = SIDE - 1
    rank_cols = turned[0].shape[0] // slots
    whole = summed(refs[:SIDE])
    dense_ref[...] = whole
    dense = whole.astype(BF16)
    pieces = [project(dense, turned, slot, rank_cols) for slot in range(slots)]
    send = jnp.concatenate(pieces, axis=0).astype(BF16)
    n = send.shape[0]
    send_ref[:n] = send
    send_ref[n:] = later_ref[...]


def add_kernel(*refs):
    refs[-1][...] = summed(refs[:-1]).astype(BF16)


def finish_kernel(is_lower, *refs):
    dense_ref, extra_ref, ranks_ref = refs[SIDE : SIDE + 3]
    out_refs, sums_ref = refs[SIDE + 3 : -1], refs[-1]
    for s in range(SIDE):
        sums_ref[wrapped(own_tile() - s)] = refs[s][...]
    n = dense_ref.shape[0]
    rank_cols = extra_ref.shape[0] // (SIDE - 1)
    width = dense_ref.shape[1] // SIDE
    tile = lax.rem(lax.axis_index("col"), SIDE)
    columns = lax.broadcasted_iota(jnp.int32, (n, rank_cols), 1)
    at_coupling = (SIDE - 1) * n
    coupling = {}
    order = list(range(SIDE)) if is_lower else list(range(SIDE))[::-1]
    first, second, third, last = order
    for which, key in enumerate(((third, second, first), (last, second, first))):
        coupling[key] = (second, which)
    for which, key in enumerate(((last, third, first), (last, third, second))):
        coupling[key] = (third, which)
    if not is_lower:
        coupling = {
            (0, 2, 3): (2, 0), (1, 2, 3): (2, 1), (0, 1, 2): (1, 0), (0, 1, 3): (1, 1)
        }
    masked = {}
    for at, source in enumerate(order):
        for target in order[at + 1 :]:
            slot = partners(source).index(target)
            value = sums_ref[source, slot * n : (slot + 1) * n].astype(F32)
            for before in order[:at]:
                held, which = coupling[target, source, before]
                start = at_coupling + which * rank_cols
                value = value - dot(
                    masked[source, before], sums_ref[held, start : start + rank_cols]
                )
            keep = columns < RBLK * ranks_ref[pair_of(source, target)]
            masked[target, source] = jnp.where(keep, value, 0.0).astype(BF16)
    result = dense_ref[...]
    nothing = jnp.zeros((n, rank_cols), BF16)
    for slot in range(SIDE - 1):
        mine = nothing
        for target in range(SIDE):
            source = partners(target)[slot]
            if (target, source) in masked:
                mine = jnp.where(tile == target, masked[target, source], mine)
        result = result - dot(
            mine, extra_ref[slot * rank_cols : (slot + 1) * rank_cols]
        )
    result = result.astype(BF16)
    for at in range(SIDE):
        block = result[:, at * width : (at + 1) * width]
        if is_lower:
            out_refs[0][wrapped(tile - at)] = block
        else:
            out_refs[at][...] = block


def shards(
    right_sides, low_left, low_right, up_left, up_right, low_ranks, up_ranks, inv_lower, inv_upper
):
    n, width = right_sides.shape[1:]
    rank_cols = low_left.shape[2]
    slots = SIDE - 1
    share = rank_cols // lax.axis_size("row")
    total = SIDE * width
    shape = jax.ShapeDtypeStruct

    more = slots * share
    height = n + more
    packed = slots * n + 2 * rank_cols
    tied = lax.optimization_barrier
    deal = kernel_call(deal_kernel, [shape((width, width), BF16)] * SIDE)
    stack = kernel_call(stack_kernel, shape((total, width), BF16))
    parts = scattered_x(deal(inv_lower))
    rows = scattered_x(
        kernel_call(pack_kernel, [shape((height, width), BF16)] * SIDE)(
            right_sides, low_left, up_left
        )
    )
    parts, rows = tied((parts, rows))
    lower = stack(*parts)
    far = swap_pair(lower)
    near = swap_core(lower)
    rows = kernel_call(
        lambda *refs: order_kernel(1, *refs), shape((SIDE, height, width), BF16)
    )(*rows)
    gathered = gathered_y(swapped(rows))
    near, low_right, up_right = tied((near, low_right, up_right))
    turned = scattered_x(
        kernel_call(turn_kernel, [shape((slots * rank_cols, width), BF16)] * SIDE)(
            low_right, up_right
        )
    )
    turned, gathered = tied((turned, gathered))
    partial = products(0, height, gathered, [lower, near, far, swap_core(far)])
    partial, inv_upper = tied((partial, inv_upper))
    upper = stack(*scattered_x(deal(inv_upper)))
    dense, extra = kernel_call(
        lambda *refs: total_kernel(n, *refs),
        [shape((n, total), F32), shape((8, more, total), BF16)],
    )(*scattered_q(partial))
    extra, upper = tied((extra, upper))
    mine = from_every_z(extra)
    mine, other, far, near = tied(
        (mine, swap_core(mine), swap_pair(upper), swap_core(upper))
    )
    low_extra, send = kernel_call(
        lambda *refs: couple_kernel(True, *refs),
        [shape((slots * rank_cols, total), BF16), shape((packed, rank_cols), BF16)],
    )(mine, other, *turned, dense)
    send, far = tied((send, far))

    def added(parts):
        return kernel_call(add_kernel, shape((packed, rank_cols), BF16))(*parts)

    def finished(is_lower, sums, dense, extra, ranks):
        outs = [shape((SIDE, n, width), BF16)] if is_lower else [shape((n, width), BF16)] * SIDE
        return kernel_call(
            lambda *refs: finish_kernel(is_lower, *refs),
            outs,
            smem=(SIDE + 2,),
            scratch=[pltpu.VMEM((SIDE, packed, rank_cols), BF16)],
        )(*sums, dense, extra, ranks)

    parts, far_near = tied((gathered_y(send), swap_core(far)))
    upper = [upper, near, far, far_near]
    more_parts = scattered_q(products(n, more, gathered, upper))
    sums, more_parts = tied((gathered_x(added(parts)), more_parts))
    [rows] = finished(True, sums, dense, low_extra, low_ranks)
    [more_sum] = kernel_call(
        lambda *refs: total_kernel(0, *refs), [shape((8, more, total), BF16)]
    )(*more_parts)
    rows, more_sum = tied((rows, more_sum))
    rows, mine = tied((swapped(rows), from_every_z(more_sum)))
    gathered, other = tied((gathered_y(rows), swap_core(mine)))
    up_extra, later = kernel_call(
        lambda *refs: couple_kernel(False, *refs),
        [shape((slots * rank_cols, total), BF16), shape((2 * rank_cols, rank_cols), BF16)],
    )(mine, other, *turned)
    dense, send = kernel_call(
        last_project_kernel,
        (shape((n, total), F32), shape((packed, rank_cols), BF16)),
    )(*scattered_q(products(0, n, gathered, upper)), *turned, later)
    sums = gathered_x(added(gathered_y(send)))
    rows = finished(False, sums, dense, up_extra, up_ranks)
    return kernel_call(
        lambda *refs: order_kernel(-1, *refs), shape((SIDE, n, width), F32)
    )(*scattered_x(rows, -1))


def solution(mesh):
    in_specs = (
        P(None, "row", "col"),
        P(None, "col", None),
        P(None, "col", None),
        P(None, "col", None),
        P(None, "col", None),
        P(),
        P(),
        P(None, "col", "row"),
        P(None, "col", "row"),
    )
    out_specs = P(None, "row", "col")
    return jax.shard_map(shards, mesh=mesh, in_specs=in_specs, out_specs=out_specs, check_vma=False)
```

```python
import jax
import jax.numpy as jnp
from jax import lax
from jax.experimental import pallas as pl
from jax.experimental.pallas import tpu as pltpu
from jax.sharding import PartitionSpec as P

RBLK = 32
BF16 = jnp.bfloat16
F32 = jnp.float32
SIDE = 4
Z_GROUPS = [[2 * z + core for z in range(8)] for core in range(2)]


def routes(to):
    index = lambda q, j, y, x: (SIDE * q + j) * SIDE * SIDE + SIDE * y + x
    span = range(SIDE)
    return [
        (index(q, j, y, x), index(*to(q, j, y, x)))
        for q in span for j in span for y in span for x in span
    ]


def permuted(value, to):
    return lax.ppermute(value, ("row", "col"), routes(to))


def gathered_y(value):
    return [value] + [
        permuted(value, lambda q, j, y, x: (q, j, (y + s) % SIDE, x)) for s in range(1, SIDE)
    ]


def gathered_x(value):
    return [value] + [
        permuted(value, lambda q, j, y, x: (q, j, y, (x + s) % SIDE)) for s in range(1, SIDE)
    ]


def scattered_q(values):
    return [values[0]] + [
        permuted(values[s], lambda q, j, y, x: ((q + s) % SIDE, j, y, x))
        for s in range(1, SIDE)
    ]


def scattered_x(values, sign=1):
    return [values[0]] + [
        permuted(values[s], lambda q, j, y, x: (q, j, y, (x + sign * s) % SIDE))
        for s in range(1, SIDE)
    ]


def from_every_z(value):
    return lax.all_to_all(value, "row", 0, 0, tiled=True, axis_index_groups=Z_GROUPS)


def own_tile():
    return lax.rem(lax.axis_index("col"), SIDE)


def wrapped(value):
    return lax.rem(value + 2 * SIDE, SIDE)


def swapped(value):
    return permuted(value, lambda q, j, y, x: (y, j, q, x))


def swap_core(value):
    return permuted(value, lambda q, j, y, x: (q, j ^ 1, y, x))


def swap_pair(value):
    return permuted(value, lambda q, j, y, x: (q, j ^ 2, y, x))


def dot(left, right):
    return jnp.dot(left, right, preferred_element_type=F32)


def dot_t(left, right):
    return lax.dot_general(
        left, right, (((1,), (1,)), ((), ())), preferred_element_type=F32
    )


def pair_of(i, j):
    high, low = max(i, j), min(i, j)
    return high * (high - 1) // 2 + low


def partners(tile):
    return [t for t in range(SIDE) if t != tile]


def kernel_call(body, out_shape, smem=(), flops=0, grid=None, in_specs=None, out_specs=None, scratch=()):
    def run(*args):
        specs = in_specs or [
            pl.BlockSpec(memory_space=pltpu.SMEM if at in smem else pltpu.VMEM)
            for at in range(len(args))
        ]
        outs = jax.tree.leaves(out_shape)
        moved = sum(a.size * a.dtype.itemsize for a in [*args, *outs])
        more = {} if grid is None else {"grid": grid, "out_specs": out_specs}
        return pl.pallas_call(
            body,
            out_shape=out_shape,
            in_specs=specs,
            scratch_shapes=list(scratch),
            compiler_params=pltpu.CompilerParams(vmem_limit_bytes=30 * 2**20),
            cost_estimate=pl.CostEstimate(
                flops=flops, bytes_accessed=moved, transcendentals=0
            ),
            **more,
        )(*args)

    return run


def pack_kernel(right_ref, low_ref, up_ref, *out_refs):
    n = right_ref.shape[1]
    rank_cols = low_ref.shape[2]
    share = rank_cols // lax.axis_size("row")
    row = lax.axis_index("row")
    at = lax.broadcasted_iota(jnp.int32, (share, rank_cols), 1)
    want = lax.broadcasted_iota(jnp.int32, (share, rank_cols), 0) + row * share
    pick = (at == want).astype(F32).astype(BF16)
    for s, out_ref in enumerate(out_refs):
        tile = wrapped(own_tile() + s)
        out_ref[:n] = right_ref[tile].astype(BF16)
        pieces = []
        for slot in range(SIDE - 1):
            pair, is_low = partner_pair(tile, slot)
            piece = jnp.where(is_low, dot_t(pick, low_ref[pair]), dot_t(pick, up_ref[pair]))
            pieces.append(piece)
        out_ref[n:] = jnp.concatenate(pieces, axis=0).astype(BF16)


def partner_pair(tile, slot):
    is_low = slot < tile
    partner = jnp.where(is_low, slot, slot + 1)
    high = jnp.where(is_low, tile, partner)
    low = jnp.where(is_low, partner, tile)
    return jnp.where(high == 1, 0, jnp.where(high == 2, 1, 3)) + low, is_low


def order_kernel(sign, *refs):
    out_ref = refs[-1]
    for s in range(SIDE):
        out_ref[wrapped(own_tile() - sign * s)] = refs[s][...].astype(out_ref.dtype)


def stack_kernel(*refs):
    half = refs[0].shape[0] // 2
    for s, ref in enumerate(refs[:-1]):
        refs[-1][0, s * half : (s + 1) * half] = ref[:half]
        refs[-1][1, s * half : (s + 1) * half] = ref[half:]


def deal_kernel(lower_ref, upper_ref, *out_refs):
    rows = lower_ref.shape[1]
    for s in range(SIDE):
        tile = wrapped(own_tile() + s)
        out_refs[s][:rows] = lower_ref[tile]
        out_refs[s][rows:] = upper_ref[tile]


def turn_kernel(low_ref, up_ref, *out_refs):
    rank_cols = low_ref.shape[2]
    one = lax.broadcasted_iota(jnp.int32, (rank_cols, rank_cols), 0)
    two = lax.broadcasted_iota(jnp.int32, (rank_cols, rank_cols), 1)
    eye = (one == two).astype(F32).astype(BF16)
    for s, out_ref in enumerate(out_refs):
        tile = wrapped(own_tile() + s)
        for slot in range(SIDE - 1):
            pair, is_low = partner_pair(tile, slot)
            factor = jnp.where(is_low, up_ref[pair], low_ref[pair])
            out_ref[slot * rank_cols : (slot + 1) * rank_cols] = dot_t(eye, factor).astype(BF16)


def products_kernel(n, padded, which, *refs):
    x_refs, inverse_refs = refs[:SIDE], refs[SIDE : 2 * SIDE]
    out_refs = refs[2 * SIDE : -2]
    joined_ref, extra_ref = refs[-2:]
    lower = [ref.at[0] for ref in inverse_refs]
    upper = [ref.at[len(which) - 1] for ref in inverse_refs]
    rows = x_refs[0].shape[1]

    @pl.when(pl.program_id(0) == 0)
    def _():
        row = lax.axis_index("row")
        flip, q = lax.rem(row, SIDE), row // SIDE
        y = lax.axis_index("col") // SIDE
        for s in range(SIDE):
            t = wrapped(y - s - q)
            for at in range(SIDE):
                block = x_refs[s][at ^ flip]
                joined_ref[at, t, :rows] = block
                if rows > n:
                    extra_ref[at, t, : rows - n] = block[n:]

    width = joined_ref.shape[3]
    value = sum(
        dot_t(joined_ref[at].reshape(SIDE * padded, width), lower[at][...])
        for at in range(SIDE)
    )
    if rows > n:
        other = sum(
            dot_t(extra_ref[at].reshape(SIDE * (padded - n), width), upper[at][...])
            for at in range(SIDE)
        )
        share = (rows - n) // (SIDE - 1)
        slot = lax.broadcasted_iota(jnp.int32, (rows - n, value.shape[1]), 0) // share
    for t in range(SIDE):
        start = t * padded
        out_refs[t][:n] = value[start : start + n].astype(BF16)
        if rows > n:
            mine = value[start + n : start + rows]
            its = other[t * (padded - n) : t * (padded - n) + rows - n]
            out_refs[t][n:] = jnp.where(slot < own_tile(), mine, its).astype(BF16)


def products(n, gathered, which, inverses):
    blocks, rows, width = gathered[0].shape
    total = inverses[0].shape[1]
    padded = rows + -rows % 16
    count = len(which)
    whole = pl.BlockSpec(gathered[0].shape, lambda a: (0, 0, 0))
    return kernel_call(
        lambda *refs: products_kernel(n, padded, which, *refs),
        [jax.ShapeDtypeStruct((rows, total), BF16)] * SIDE,
        flops=2 * SIDE * blocks * rows * width * total,
        grid=(total // 256,),
        in_specs=[whole] * SIDE
        + [pl.BlockSpec((count, 256, width), lambda a: (which[-1] // count, a, 0))] * SIDE,
        out_specs=[pl.BlockSpec((rows, 256), lambda a: (0, a))] * SIDE,
        scratch=[
            pltpu.VMEM((blocks, SIDE, padded, width), BF16),
            pltpu.VMEM((blocks, SIDE, max(padded - n, 16), width), BF16),
        ],
    )(*gathered, *inverses)


def summed(refs):
    whole = refs[0][...].astype(F32)
    for ref in refs[1:]:
        whole = whole + ref[...].astype(F32)
    return whole


def total_kernel(n, *refs):
    dense_ref, extra_ref = refs[SIDE:]
    whole = summed(refs[:SIDE])
    dense_ref[...] = whole[:n]
    extra = whole[n:].astype(BF16)
    for at in range(extra_ref.shape[0]):
        extra_ref[at] = extra


def project(dense, turned, slot, rank_cols):
    width = turned[0].shape[1]
    return sum(
        dot_t(
            dense[:, at * width : (at + 1) * width],
            turned[at][slot * rank_cols : (slot + 1) * rank_cols],
        )
        for at in range(SIDE)
    )


def couple_kernel(dense_ref, mine_ref, other_ref, *refs):
    turned, (extra_ref, send_ref, later_ref) = refs[:SIDE], refs[SIDE:]
    slots = SIDE - 1
    rank_cols = turned[0].shape[0] // slots
    width = turned[0].shape[1]
    share = mine_ref.shape[1] // slots
    even = lax.rem(lax.axis_index("row"), 2) == 0
    tile = own_tile()
    for z in range(mine_ref.shape[0]):
        mine, other = mine_ref[z].astype(F32), other_ref[z].astype(F32)
        first = jnp.where(even, mine, other)
        second = jnp.where(even, other, mine)
        for slot in range(slots):
            at = slice(slot * share, (slot + 1) * share)
            start = slot * rank_cols + z * 2 * share
            extra_ref[start : start + 2 * share] = jnp.concatenate(
                [first[at], second[at]], axis=0
            ).astype(BF16)
    dense = dense_ref[...].astype(BF16)
    pieces = [project(dense, turned, slot, rank_cols) for slot in range(slots)]

    def coupling(left, right):
        left = pl.multiple_of(left * rank_cols, rank_cols)
        right = pl.multiple_of(right * rank_cols, rank_cols)
        return sum(
            dot_t(
                extra_ref[pl.ds(left, rank_cols), at * width : (at + 1) * width],
                turned[at][pl.ds(right, rank_cols), :],
            )
            for at in range(SIDE)
        )

    one = tile == 1
    pick = lambda a, b: jnp.where(one, a, b)
    pieces += [coupling(0, pick(1, 2)), coupling(pick(0, 1), 2)]
    send_ref[...] = jnp.concatenate(pieces, axis=0).astype(BF16)
    later_ref[:rank_cols] = coupling(pick(1, 2), 0).astype(BF16)
    later_ref[rank_cols:] = coupling(2, pick(0, 1)).astype(BF16)


def last_project_kernel(*refs):
    turned, (later_ref, dense_ref, send_ref) = refs[SIDE : 2 * SIDE], refs[2 * SIDE :]
    slots = SIDE - 1
    rank_cols = turned[0].shape[0] // slots
    whole = summed(refs[:SIDE])
    dense_ref[...] = whole
    dense = whole.astype(BF16)
    pieces = [project(dense, turned, slot, rank_cols) for slot in range(slots)]
    send = jnp.concatenate(pieces, axis=0).astype(BF16)
    n = send.shape[0]
    send_ref[:n] = send
    send_ref[n:] = later_ref[...]


def add_kernel(*refs):
    refs[-1][...] = summed(refs[:-1]).astype(BF16)


def finish_kernel(is_lower, *refs):
    dense_ref, extra_ref, ranks_ref = refs[SIDE : SIDE + 3]
    out_refs, sums_ref = refs[SIDE + 3 : -1], refs[-1]
    for s in range(SIDE):
        sums_ref[wrapped(own_tile() - s)] = refs[s][...]
    n = dense_ref.shape[0]
    rank_cols = extra_ref.shape[0] // (SIDE - 1)
    width = dense_ref.shape[1] // SIDE
    tile = lax.rem(lax.axis_index("col"), SIDE)
    columns = lax.broadcasted_iota(jnp.int32, (n, rank_cols), 1)
    at_coupling = (SIDE - 1) * n
    coupling = {}
    order = list(range(SIDE)) if is_lower else list(range(SIDE))[::-1]
    first, second, third, last = order
    for which, key in enumerate(((third, second, first), (last, second, first))):
        coupling[key] = (second, which)
    for which, key in enumerate(((last, third, first), (last, third, second))):
        coupling[key] = (third, which)
    if not is_lower:
        coupling = {
            (0, 2, 3): (2, 0), (1, 2, 3): (2, 1), (0, 1, 2): (1, 0), (0, 1, 3): (1, 1)
        }
    masked = {}
    for at, source in enumerate(order):
        for target in order[at + 1 :]:
            slot = partners(source).index(target)
            value = sums_ref[source, slot * n : (slot + 1) * n].astype(F32)
            for before in order[:at]:
                held, which = coupling[target, source, before]
                start = at_coupling + which * rank_cols
                value = value - dot(
                    masked[source, before], sums_ref[held, start : start + rank_cols]
                )
            keep = columns < RBLK * ranks_ref[pair_of(source, target)]
            masked[target, source] = jnp.where(keep, value, 0.0).astype(BF16)
    result = dense_ref[...]
    nothing = jnp.zeros((n, rank_cols), BF16)
    for slot in range(SIDE - 1):
        mine = nothing
        for target in range(SIDE):
            source = partners(target)[slot]
            if (target, source) in masked:
                mine = jnp.where(tile == target, masked[target, source], mine)
        result = result - dot(
            mine, extra_ref[slot * rank_cols : (slot + 1) * rank_cols]
        )
    result = result.astype(BF16)
    for at in range(SIDE):
        block = result[:, at * width : (at + 1) * width]
        if is_lower:
            out_refs[0][wrapped(tile - at)] = block
        else:
            out_refs[at][...] = block


def shards(
    right_sides, low_left, low_right, up_left, up_right, low_ranks, up_ranks, inv_lower, inv_upper
):
    n, width = right_sides.shape[1:]
    rank_cols = low_left.shape[2]
    slots = SIDE - 1
    share = rank_cols // lax.axis_size("row")
    total = SIDE * width
    shape = jax.ShapeDtypeStruct

    height = n + slots * share
    rows = kernel_call(pack_kernel, [shape((height, width), BF16)] * SIDE)(
        right_sides, low_left, up_left
    )
    tied = lax.optimization_barrier
    rows = scattered_x(rows)
    rows = kernel_call(
        lambda *refs: order_kernel(1, *refs), shape((SIDE, height, width), BF16)
    )(*rows)
    rows, inv_lower, inv_upper = tied((rows, inv_lower, inv_upper))
    parts = scattered_x(
        kernel_call(deal_kernel, [shape((2 * width, width), BF16)] * SIDE)(
            inv_lower, inv_upper
        )
    )
    parts, rows = tied((parts, swapped(rows)))
    inverse = kernel_call(stack_kernel, shape((2, total, width), BF16))(*parts)
    far = swap_pair(inverse)
    near, gathered = tied((swap_core(inverse), gathered_y(rows)))
    gathered, low_right, up_right = tied((gathered, low_right, up_right))
    turned = scattered_x(
        kernel_call(turn_kernel, [shape((slots * rank_cols, width), BF16)] * SIDE)(
            low_right, up_right
        )
    )
    turned, far = tied((turned, far))
    inverses = [inverse, near, far, swap_core(far)]
    received = scattered_q(products(n, gathered, (0, 1), inverses))
    dense, extra = kernel_call(
        lambda *refs: total_kernel(n, *refs),
        (shape((n, total), F32), shape((8, slots * share, total), BF16)),
    )(*received)
    mine = from_every_z(extra)
    packed = slots * n + 2 * rank_cols
    extra, send, later = kernel_call(
        couple_kernel,
        (
            shape((slots * rank_cols, total), BF16),
            shape((packed, rank_cols), BF16),
            shape((2 * rank_cols, rank_cols), BF16),
        ),
    )(dense, mine, swap_core(mine), *turned)

    def finished(is_lower, send, dense, ranks):
        sums = kernel_call(add_kernel, shape((packed, rank_cols), BF16))(*gathered_y(send))
        outs = [shape((SIDE, n, width), BF16)] if is_lower else [shape((n, width), BF16)] * SIDE
        return kernel_call(
            lambda *refs: finish_kernel(is_lower, *refs),
            outs,
            smem=(SIDE + 2,),
            scratch=[pltpu.VMEM((SIDE, packed, rank_cols), BF16)],
        )(*gathered_x(sums), dense, extra, ranks)

    [rows] = finished(True, send, dense, low_ranks)
    parts = products(n, gathered_y(swapped(rows)), (1,), inverses)
    dense, send = kernel_call(
        last_project_kernel,
        (shape((n, total), F32), shape((packed, rank_cols), BF16)),
    )(*scattered_q(parts), *turned, later)
    rows = finished(False, send, dense, up_ranks)
    return kernel_call(
        lambda *refs: order_kernel(-1, *refs), shape((SIDE, n, width), F32)
    )(*scattered_x(rows, -1))


def solution(mesh):
    in_specs = (
        P(None, "row", "col"),
        P(None, "col", None),
        P(None, "col", None),
        P(None, "col", None),
        P(None, "col", None),
        P(),
        P(),
        P(None, "col", "row"),
        P(None, "col", "row"),
    )
    out_specs = P(None, "row", "col")
    return jax.shard_map(shards, mesh=mesh, in_specs=in_specs, out_specs=out_specs, check_vma=False)
```

```python
import jax
import jax.numpy as jnp
from jax import lax
from jax.experimental import pallas as pl
from jax.experimental.pallas import tpu as pltpu
from jax.sharding import PartitionSpec as P

RBLK = 32
BF16 = jnp.bfloat16
F32 = jnp.float32
SIDE = 4
Z_GROUPS = [[2 * z + core for z in range(8)] for core in range(2)]


def routes(to):
    index = lambda q, j, y, x: (SIDE * q + j) * SIDE * SIDE + SIDE * y + x
    span = range(SIDE)
    return [
        (index(q, j, y, x), index(*to(q, j, y, x)))
        for q in span for j in span for y in span for x in span
    ]


def permuted(value, to):
    return lax.ppermute(value, ("row", "col"), routes(to))


def gathered_y(value):
    return [value] + [
        permuted(value, lambda q, j, y, x: (q, j, (y + s) % SIDE, x)) for s in range(1, SIDE)
    ]


def gathered_x(value):
    return [value] + [
        permuted(value, lambda q, j, y, x: (q, j, y, (x + s) % SIDE)) for s in range(1, SIDE)
    ]


def scattered_q(values):
    return [values[0]] + [
        permuted(values[s], lambda q, j, y, x: ((q + s) % SIDE, j, y, x))
        for s in range(1, SIDE)
    ]


def scattered_x(values, sign=1):
    return [values[0]] + [
        permuted(values[s], lambda q, j, y, x: (q, j, y, (x + sign * s) % SIDE))
        for s in range(1, SIDE)
    ]


def from_every_z(value):
    return lax.all_to_all(value, "row", 0, 0, tiled=True, axis_index_groups=Z_GROUPS)


def own_tile():
    return lax.rem(lax.axis_index("col"), SIDE)


def wrapped(value):
    return lax.rem(value + 2 * SIDE, SIDE)


def swapped(value):
    return permuted(value, lambda q, j, y, x: (y, j, q, x))


def swap_core(value):
    return permuted(value, lambda q, j, y, x: (q, j ^ 1, y, x))


def swap_pair(value):
    return permuted(value, lambda q, j, y, x: (q, j ^ 2, y, x))


def dot(left, right):
    return jnp.dot(left, right, preferred_element_type=F32)


def dot_t(left, right):
    return lax.dot_general(
        left, right, (((1,), (1,)), ((), ())), preferred_element_type=F32
    )


def pair_of(i, j):
    high, low = max(i, j), min(i, j)
    return high * (high - 1) // 2 + low


def partners(tile):
    return [t for t in range(SIDE) if t != tile]


def kernel_call(body, out_shape, smem=(), flops=0, grid=None, in_specs=None, out_specs=None, scratch=()):
    def run(*args):
        specs = in_specs or [
            pl.BlockSpec(memory_space=pltpu.SMEM if at in smem else pltpu.VMEM)
            for at in range(len(args))
        ]
        outs = jax.tree.leaves(out_shape)
        moved = sum(a.size * a.dtype.itemsize for a in [*args, *outs])
        more = {} if grid is None else {"grid": grid, "out_specs": out_specs}
        return pl.pallas_call(
            body,
            out_shape=out_shape,
            in_specs=specs,
            scratch_shapes=list(scratch),
            compiler_params=pltpu.CompilerParams(vmem_limit_bytes=30 * 2**20),
            cost_estimate=pl.CostEstimate(
                flops=flops, bytes_accessed=moved, transcendentals=0
            ),
            **more,
        )(*args)

    return run


def pack_kernel(right_ref, low_ref, up_ref, lower_ref, upper_ref, *out_refs):
    n = right_ref.shape[1]
    half = lower_ref.shape[1]
    rank_cols = low_ref.shape[2]
    share = rank_cols // lax.axis_size("row")
    row = lax.axis_index("row")
    at = lax.broadcasted_iota(jnp.int32, (share, rank_cols), 1)
    want = lax.broadcasted_iota(jnp.int32, (share, rank_cols), 0) + row * share
    pick = (at == want).astype(F32).astype(BF16)
    for s, out_ref in enumerate(out_refs):
        tile = wrapped(own_tile() + s)
        out_ref[:half] = lower_ref[tile]
        out_ref[half : 2 * half] = upper_ref[tile]
        out_ref[2 * half : 2 * half + n] = right_ref[tile].astype(BF16)
        pieces = []
        for slot in range(SIDE - 1):
            pair, is_low = partner_pair(tile, slot)
            pieces.append(
                dot_t(pick, jnp.where(is_low, low_ref[pair], up_ref[pair]))
            )
        out_ref[2 * half + n :] = jnp.concatenate(pieces, axis=0).astype(BF16)


def partner_pair(tile, slot):
    is_low = slot < tile
    partner = jnp.where(is_low, slot, slot + 1)
    high = jnp.where(is_low, tile, partner)
    low = jnp.where(is_low, partner, tile)
    return jnp.where(high == 1, 0, jnp.where(high == 2, 1, 3)) + low, is_low


def order_kernel(sign, start, *refs):
    out_ref = refs[-1]
    for s in range(SIDE):
        out_ref[wrapped(own_tile() - sign * s)] = refs[s][start:].astype(out_ref.dtype)


def stack_kernel(*refs):
    half = refs[-1].shape[1] // SIDE
    for s, ref in enumerate(refs[:-1]):
        refs[-1][0, s * half : (s + 1) * half] = ref[:half]
        refs[-1][1, s * half : (s + 1) * half] = ref[half : 2 * half]


def turn_kernel(low_ref, up_ref, *out_refs):
    rank_cols = low_ref.shape[2]
    one = lax.broadcasted_iota(jnp.int32, (rank_cols, rank_cols), 0)
    two = lax.broadcasted_iota(jnp.int32, (rank_cols, rank_cols), 1)
    eye = (one == two).astype(F32).astype(BF16)
    for s, out_ref in enumerate(out_refs):
        tile = wrapped(own_tile() + s)
        for slot in range(SIDE - 1):
            pair, is_low = partner_pair(tile, slot)
            factor = jnp.where(is_low, up_ref[pair], low_ref[pair])
            out_ref[slot * rank_cols : (slot + 1) * rank_cols] = dot_t(eye, factor).astype(BF16)


def products_kernel(n, padded, which, *refs):
    x_refs, inverse_refs = refs[:SIDE], refs[SIDE : 2 * SIDE]
    out_refs, more_refs = refs[2 * SIDE : 3 * SIDE], refs[3 * SIDE : -2]
    joined_ref, extra_ref = refs[-2:]
    lower = [ref.at[0] for ref in inverse_refs]
    upper = [ref.at[len(which) - 1] for ref in inverse_refs]
    rows = x_refs[0].shape[1]

    @pl.when(pl.program_id(0) == 0)
    def _():
        row = lax.axis_index("row")
        flip, q = lax.rem(row, SIDE), row // SIDE
        y = lax.axis_index("col") // SIDE
        for s in range(SIDE):
            t = wrapped(y - s - q)
            for at in range(SIDE):
                block = x_refs[s][at ^ flip]
                joined_ref[at, t, :rows] = block
                if rows > n:
                    extra_ref[at, t, : rows - n] = block[n:]

    width = joined_ref.shape[3]
    value = sum(
        dot_t(joined_ref[at].reshape(SIDE * padded, width), lower[at][...])
        for at in range(SIDE)
    )
    if rows > n:
        other = sum(
            dot_t(extra_ref[at].reshape(SIDE * (padded - n), width), upper[at][...])
            for at in range(SIDE)
        )
        share = (rows - n) // (SIDE - 1)
        slot = lax.broadcasted_iota(jnp.int32, (rows - n, value.shape[1]), 0) // share
    for t in range(SIDE):
        start = t * padded
        out_refs[t][...] = value[start : start + n].astype(BF16)
        if rows > n:
            mine = value[start + n : start + rows]
            its = other[t * (padded - n) : t * (padded - n) + rows - n]
            more_refs[t][...] = jnp.where(slot < own_tile(), mine, its).astype(BF16)


def products(n, gathered, which, inverses):
    blocks, rows, width = gathered[0].shape
    total = inverses[0].shape[1]
    padded = rows + -rows % 16
    count = len(which)
    whole = pl.BlockSpec(gathered[0].shape, lambda a: (0, 0, 0))
    heights = [n] * SIDE + [rows - n] * SIDE * (rows > n)
    return kernel_call(
        lambda *refs: products_kernel(n, padded, which, *refs),
        [jax.ShapeDtypeStruct((height, total), BF16) for height in heights],
        flops=2 * SIDE * blocks * rows * width * total,
        grid=(total // 256,),
        in_specs=[whole] * SIDE
        + [pl.BlockSpec((count, 256, width), lambda a: (which[-1] // count, a, 0))] * SIDE,
        out_specs=[pl.BlockSpec((height, 256), lambda a: (0, a)) for height in heights],
        scratch=[
            pltpu.VMEM((blocks, SIDE, padded, width), BF16),
            pltpu.VMEM((blocks, SIDE, max(padded - n, 16), width), BF16),
        ],
    )(*gathered, *inverses)


def summed(refs):
    whole = refs[0][...].astype(F32)
    for ref in refs[1:]:
        whole = whole + ref[...].astype(F32)
    return whole


def total_kernel(*refs):
    extra = summed(refs[:SIDE]).astype(BF16)
    for at in range(refs[-1].shape[0]):
        refs[-1][at] = extra


def project(dense, turned, slot, rank_cols):
    width = turned[0].shape[1]
    return sum(
        dot_t(
            dense[:, at * width : (at + 1) * width],
            turned[at][slot * rank_cols : (slot + 1) * rank_cols],
        )
        for at in range(SIDE)
    )


def couple_kernel(mine_ref, other_ref, *refs):
    turned, parts = refs[:SIDE], refs[SIDE : 2 * SIDE]
    dense_ref, extra_ref, send_ref, later_ref = refs[2 * SIDE :]
    dense_ref[...] = summed(parts)
    slots = SIDE - 1
    rank_cols = extra_ref.shape[0] // slots
    width = turned[0].shape[1]
    share = mine_ref.shape[1] // slots
    even = lax.rem(lax.axis_index("row"), 2) == 0
    tile = own_tile()
    for z in range(mine_ref.shape[0]):
        mine, other = mine_ref[z].astype(F32), other_ref[z].astype(F32)
        first = jnp.where(even, mine, other)
        second = jnp.where(even, other, mine)
        for slot in range(slots):
            at = slice(slot * share, (slot + 1) * share)
            start = slot * rank_cols + z * 2 * share
            extra_ref[start : start + 2 * share] = jnp.concatenate(
                [first[at], second[at]], axis=0
            ).astype(BF16)
    dense = dense_ref[...].astype(BF16)
    pieces = [project(dense, turned, slot, rank_cols) for slot in range(slots)]

    def coupling(left, right):
        left = pl.multiple_of(left * rank_cols, rank_cols)
        right = pl.multiple_of(right * rank_cols, rank_cols)
        return sum(
            dot_t(
                extra_ref[pl.ds(left, rank_cols), at * width : (at + 1) * width],
                turned[at][pl.ds(right, rank_cols), :],
            )
            for at in range(SIDE)
        )

    one = tile == 1
    pick = lambda a, b: jnp.where(one, a, b)
    pieces += [coupling(0, pick(1, 2)), coupling(pick(0, 1), 2)]
    send_ref[...] = jnp.concatenate(pieces, axis=0).astype(BF16)
    later_ref[:rank_cols] = coupling(pick(1, 2), 0).astype(BF16)
    later_ref[rank_cols:] = coupling(2, pick(0, 1)).astype(BF16)


def last_project_kernel(*refs):
    turned, (later_ref, dense_ref, send_ref) = refs[SIDE : 2 * SIDE], refs[2 * SIDE :]
    slots = SIDE - 1
    rank_cols = later_ref.shape[0] // 2
    whole = summed(refs[:SIDE])
    dense_ref[...] = whole
    dense = whole.astype(BF16)
    pieces = [project(dense, turned, slot, rank_cols) for slot in range(slots)]
    send = jnp.concatenate(pieces, axis=0).astype(BF16)
    n = send.shape[0]
    send_ref[:n] = send
    send_ref[n:] = later_ref[...]


def add_kernel(*refs):
    refs[-1][...] = summed(refs[:-1]).astype(BF16)


def finish_kernel(is_lower, *refs):
    dense_ref, extra_ref, ranks_ref = refs[SIDE : SIDE + 3]
    out_refs, sums_ref = refs[SIDE + 3 : -1], refs[-1]
    for s in range(SIDE):
        sums_ref[wrapped(own_tile() - s)] = refs[s][...]
    n = dense_ref.shape[0]
    rank_cols = extra_ref.shape[0] // (SIDE - 1)
    width = dense_ref.shape[1] // SIDE
    tile = lax.rem(lax.axis_index("col"), SIDE)
    columns = lax.broadcasted_iota(jnp.int32, (n, rank_cols), 1)
    at_coupling = (SIDE - 1) * n
    coupling = {}
    order = list(range(SIDE)) if is_lower else list(range(SIDE))[::-1]
    first, second, third, last = order
    for which, key in enumerate(((third, second, first), (last, second, first))):
        coupling[key] = (second, which)
    for which, key in enumerate(((last, third, first), (last, third, second))):
        coupling[key] = (third, which)
    if not is_lower:
        coupling = {
            (0, 2, 3): (2, 0), (1, 2, 3): (2, 1), (0, 1, 2): (1, 0), (0, 1, 3): (1, 1)
        }
    masked = {}
    for at, source in enumerate(order):
        for target in order[at + 1 :]:
            slot = partners(source).index(target)
            value = sums_ref[source, slot * n : (slot + 1) * n].astype(F32)
            for before in order[:at]:
                held, which = coupling[target, source, before]
                start = at_coupling + which * rank_cols
                value = value - dot(
                    masked[source, before], sums_ref[held, start : start + rank_cols]
                )
            keep = columns < RBLK * ranks_ref[pair_of(source, target)]
            masked[target, source] = jnp.where(keep, value, 0.0).astype(BF16)
    result = dense_ref[...]
    nothing = jnp.zeros((n, rank_cols), BF16)
    for slot in range(SIDE - 1):
        mine = nothing
        for target in range(SIDE):
            source = partners(target)[slot]
            if (target, source) in masked:
                mine = jnp.where(tile == target, masked[target, source], mine)
        result = result - dot(
            mine, extra_ref[slot * rank_cols : (slot + 1) * rank_cols]
        )
    result = result.astype(BF16)
    for at in range(SIDE):
        block = result[:, at * width : (at + 1) * width]
        if is_lower:
            out_refs[0][wrapped(tile - at)] = block
        else:
            out_refs[at][...] = block


def shards(
    right_sides, low_left, low_right, up_left, up_right, low_ranks, up_ranks, inv_lower, inv_upper
):
    n, width = right_sides.shape[1:]
    rank_cols = low_left.shape[2]
    slots = SIDE - 1
    share = rank_cols // lax.axis_size("row")
    total = SIDE * width
    shape = jax.ShapeDtypeStruct

    more = slots * share
    height = n + more
    packed = slots * n + 2 * rank_cols
    tied = lax.optimization_barrier
    parts = scattered_x(
        kernel_call(pack_kernel, [shape((2 * width + height, width), BF16)] * SIDE)(
            right_sides, low_left, up_left, inv_lower, inv_upper
        )
    )
    rows = kernel_call(
        lambda *refs: order_kernel(1, 2 * width, *refs),
        shape((SIDE, height, width), BF16),
    )(*parts)
    inverse = kernel_call(stack_kernel, shape((2, total, width), BF16))(*parts)
    inverse, rows = tied((inverse, rows))
    far, near = swap_pair(inverse), swap_core(inverse)
    near, low_right, up_right = tied((near, low_right, up_right))
    turned = scattered_x(
        kernel_call(turn_kernel, [shape((slots * rank_cols, width), BF16)] * SIDE)(
            low_right, up_right
        )
    )
    turned, rows = tied((turned, swapped(rows)))
    inverses = [inverse, near, far, swap_core(far)]
    partial = products(n, gathered_y(rows), (0, 1), inverses)
    dense, extra = tied((partial[:SIDE], scattered_q(partial[SIDE:])))
    dense = scattered_q(dense)
    mine = from_every_z(
        kernel_call(total_kernel, shape((8, more, total), BF16))(*extra)
    )
    mine, dense = tied((mine, dense))
    dense, extra, send, later = kernel_call(
        couple_kernel,
        (
            shape((n, total), F32),
            shape((slots * rank_cols, total), BF16),
            shape((packed, rank_cols), BF16),
            shape((2 * rank_cols, rank_cols), BF16),
        ),
    )(mine, swap_core(mine), *turned, *dense)

    def finished(is_lower, send, dense, ranks):
        sums = kernel_call(add_kernel, shape((packed, rank_cols), BF16))(*gathered_y(send))
        outs = [shape((SIDE, n, width), BF16)] if is_lower else [shape((n, width), BF16)] * SIDE
        return kernel_call(
            lambda *refs: finish_kernel(is_lower, *refs),
            outs,
            smem=(SIDE + 2,),
            scratch=[pltpu.VMEM((SIDE, packed, rank_cols), BF16)],
        )(*gathered_x(sums), dense, extra, ranks)

    [rows] = finished(True, send, dense, low_ranks)
    parts = products(n, gathered_y(swapped(rows)), (1,), inverses)
    dense, send = kernel_call(
        last_project_kernel,
        (shape((n, total), F32), shape((packed, rank_cols), BF16)),
    )(*scattered_q(parts), *turned, later)
    rows = finished(False, send, dense, up_ranks)
    return kernel_call(
        lambda *refs: order_kernel(-1, 0, *refs), shape((SIDE, n, width), F32)
    )(*scattered_x(rows, -1))


def solution(mesh):
    in_specs = (
        P(None, "row", "col"),
        P(None, "col", None),
        P(None, "col", None),
        P(None, "col", None),
        P(None, "col", None),
        P(),
        P(),
        P(None, "col", "row"),
        P(None, "col", "row"),
    )
    out_specs = P(None, "row", "col")
    return jax.shard_map(shards, mesh=mesh, in_specs=in_specs, out_specs=out_specs, check_vma=False)
```

```python
import jax
import jax.numpy as jnp
from jax import lax
from jax.experimental import pallas as pl
from jax.experimental.pallas import tpu as pltpu
from jax.sharding import PartitionSpec as P

RBLK = 32
BF16 = jnp.bfloat16
F32 = jnp.float32
SIDE = 4
Z_GROUPS = [[2 * z + core for z in range(8)] for core in range(2)]


def routes(to):
    index = lambda q, j, y, x: (SIDE * q + j) * SIDE * SIDE + SIDE * y + x
    span = range(SIDE)
    return [
        (index(q, j, y, x), index(*to(q, j, y, x)))
        for q in span for j in span for y in span for x in span
    ]


def permuted(value, to):
    return lax.ppermute(value, ("row", "col"), routes(to))


def gathered_y(value):
    return [value] + [
        permuted(value, lambda q, j, y, x: (q, j, (y + s) % SIDE, x)) for s in range(1, SIDE)
    ]


def gathered_x(value):
    return [value] + [
        permuted(value, lambda q, j, y, x: (q, j, y, (x + s) % SIDE)) for s in range(1, SIDE)
    ]


def scattered_q(values):
    return [values[0]] + [
        permuted(values[s], lambda q, j, y, x: ((q + s) % SIDE, j, y, x))
        for s in range(1, SIDE)
    ]


def scattered_x(values, sign=1):
    return [values[0]] + [
        permuted(values[s], lambda q, j, y, x: (q, j, y, (x + sign * s) % SIDE))
        for s in range(1, SIDE)
    ]


def from_every_z(value):
    return lax.all_to_all(value, "row", 0, 0, tiled=True, axis_index_groups=Z_GROUPS)


def own_tile():
    return lax.rem(lax.axis_index("col"), SIDE)


def wrapped(value):
    return lax.rem(value + 2 * SIDE, SIDE)


def swapped(value):
    return permuted(value, lambda q, j, y, x: (y, j, q, x))


def swap_core(value):
    return permuted(value, lambda q, j, y, x: (q, j ^ 1, y, x))


def swap_pair(value):
    return permuted(value, lambda q, j, y, x: (q, j ^ 2, y, x))


def dot(left, right):
    return jnp.dot(left, right, preferred_element_type=F32)


def dot_t(left, right):
    return lax.dot_general(
        left, right, (((1,), (1,)), ((), ())), preferred_element_type=F32
    )


def pair_of(i, j):
    high, low = max(i, j), min(i, j)
    return high * (high - 1) // 2 + low


def partners(tile):
    return [t for t in range(SIDE) if t != tile]


def kernel_call(body, out_shape, smem=(), flops=0, grid=None, in_specs=None, out_specs=None, scratch=()):
    def run(*args):
        specs = in_specs or [
            pl.BlockSpec(memory_space=pltpu.SMEM if at in smem else pltpu.VMEM)
            for at in range(len(args))
        ]
        outs = jax.tree.leaves(out_shape)
        moved = sum(a.size * a.dtype.itemsize for a in [*args, *outs])
        more = {} if grid is None else {"grid": grid, "out_specs": out_specs}
        return pl.pallas_call(
            body,
            out_shape=out_shape,
            in_specs=specs,
            scratch_shapes=list(scratch),
            compiler_params=pltpu.CompilerParams(vmem_limit_bytes=14 * 2**20),
            cost_estimate=pl.CostEstimate(
                flops=flops, bytes_accessed=moved, transcendentals=0
            ),
            **more,
        )(*args)

    return run


def pack_kernel(right_ref, low_ref, up_ref, lower_ref, upper_ref, *out_refs):
    n = right_ref.shape[1]
    half = lower_ref.shape[1]
    rank_cols = low_ref.shape[2]
    share = rank_cols // lax.axis_size("row")
    row = lax.axis_index("row")
    at = lax.broadcasted_iota(jnp.int32, (share, rank_cols), 1)
    want = lax.broadcasted_iota(jnp.int32, (share, rank_cols), 0) + row * share
    pick = (at == want).astype(F32).astype(BF16)
    for s, out_ref in enumerate(out_refs):
        tile = wrapped(own_tile() + s)
        out_ref[:half] = lower_ref[tile]
        out_ref[half : 2 * half] = upper_ref[tile]
        out_ref[2 * half : 2 * half + n] = right_ref[tile].astype(BF16)
        pieces = []
        for slot in range(SIDE - 1):
            pair, is_low = partner_pair(tile, slot)
            pieces.append(
                dot_t(pick, jnp.where(is_low, low_ref[pair], up_ref[pair]))
            )
        out_ref[2 * half + n :] = jnp.concatenate(pieces, axis=0).astype(BF16)


def partner_pair(tile, slot):
    is_low = slot < tile
    partner = jnp.where(is_low, slot, slot + 1)
    high = jnp.where(is_low, tile, partner)
    low = jnp.where(is_low, partner, tile)
    return jnp.where(high == 1, 0, jnp.where(high == 2, 1, 3)) + low, is_low


def order_kernel(sign, start, *refs):
    out_ref = refs[-1]
    for s in range(SIDE):
        out_ref[wrapped(own_tile() - sign * s)] = refs[s][start:].astype(out_ref.dtype)


def stack_kernel(*refs):
    half = refs[-1].shape[1] // SIDE
    for s, ref in enumerate(refs[:-1]):
        refs[-1][0, s * half : (s + 1) * half] = ref[:half]
        refs[-1][1, s * half : (s + 1) * half] = ref[half : 2 * half]


def turn_kernel(low_ref, up_ref, *out_refs):
    rank_cols = low_ref.shape[2]
    one = lax.broadcasted_iota(jnp.int32, (rank_cols, rank_cols), 0)
    two = lax.broadcasted_iota(jnp.int32, (rank_cols, rank_cols), 1)
    eye = (one == two).astype(F32).astype(BF16)
    for s, out_ref in enumerate(out_refs):
        tile = wrapped(own_tile() + s)
        for slot in range(SIDE - 1):
            pair, is_low = partner_pair(tile, slot)
            factor = jnp.where(is_low, up_ref[pair], low_ref[pair])
            out_ref[slot * rank_cols : (slot + 1) * rank_cols] = dot_t(eye, factor).astype(BF16)


def products_kernel(n, padded, which, *refs):
    x_refs, inverse_refs = refs[:SIDE], refs[SIDE : 2 * SIDE]
    out_refs = refs[2 * SIDE : -2]
    joined_ref, extra_ref = refs[-2:]
    lower = [ref.at[0] for ref in inverse_refs]
    upper = [ref.at[len(which) - 1] for ref in inverse_refs]
    rows = x_refs[0].shape[1]

    @pl.when(pl.program_id(0) == 0)
    def _():
        row = lax.axis_index("row")
        flip, q = lax.rem(row, SIDE), row // SIDE
        y = lax.axis_index("col") // SIDE
        for s in range(SIDE):
            t = wrapped(y - s - q)
            for at in range(SIDE):
                block = x_refs[s][at ^ flip]
                joined_ref[at, t, :rows] = block
                if rows > n:
                    extra_ref[at, t, : rows - n] = block[n:]

    width = joined_ref.shape[3]
    value = sum(
        dot_t(joined_ref[at].reshape(SIDE * padded, width), lower[at][...])
        for at in range(SIDE)
    )
    if rows > n:
        other = sum(
            dot_t(extra_ref[at].reshape(SIDE * (padded - n), width), upper[at][...])
            for at in range(SIDE)
        )
        share = (rows - n) // (SIDE - 1)
        slot = lax.broadcasted_iota(jnp.int32, (rows - n, value.shape[1]), 0) // share
    for t in range(SIDE):
        start = t * padded
        out_refs[t][:n] = value[start : start + n].astype(BF16)
        if rows > n:
            mine = value[start + n : start + rows]
            its = other[t * (padded - n) : t * (padded - n) + rows - n]
            out_refs[t][n:] = jnp.where(slot < own_tile(), mine, its).astype(BF16)


def products(n, gathered, which, inverses):
    blocks, rows, width = gathered[0].shape
    total = inverses[0].shape[1]
    padded = rows + -rows % 16
    count = len(which)
    whole = pl.BlockSpec(gathered[0].shape, lambda a: (0, 0, 0))
    return kernel_call(
        lambda *refs: products_kernel(n, padded, which, *refs),
        [jax.ShapeDtypeStruct((rows, total), BF16)] * SIDE,
        flops=2 * SIDE * blocks * rows * width * total,
        grid=(total // 256,),
        in_specs=[whole] * SIDE
        + [pl.BlockSpec((count, 256, width), lambda a: (which[-1] // count, a, 0))] * SIDE,
        out_specs=[pl.BlockSpec((rows, 256), lambda a: (0, a))] * SIDE,
        scratch=[
            pltpu.VMEM((blocks, SIDE, padded, width), BF16),
            pltpu.VMEM((blocks, SIDE, max(padded - n, 16), width), BF16),
        ],
    )(*gathered, *inverses)


def summed(refs):
    whole = refs[0][...].astype(F32)
    for ref in refs[1:]:
        whole = whole + ref[...].astype(F32)
    return whole


def total_kernel(n, *refs):
    dense_ref, extra_ref = refs[SIDE:]
    whole = summed(refs[:SIDE])
    dense_ref[...] = whole[:n]
    extra = whole[n:].astype(BF16)
    for at in range(extra_ref.shape[0]):
        extra_ref[at] = extra


def project(dense, turned, slot, rank_cols):
    width = turned[0].shape[1]
    return sum(
        dot_t(
            dense[:, at * width : (at + 1) * width],
            turned[at][slot * rank_cols : (slot + 1) * rank_cols],
        )
        for at in range(SIDE)
    )


def couple_kernel(dense_ref, mine_ref, other_ref, *refs):
    turned, (extra_ref, send_ref, later_ref) = refs[:SIDE], refs[SIDE:]
    slots = SIDE - 1
    rank_cols = turned[0].shape[0] // slots
    width = turned[0].shape[1]
    share = mine_ref.shape[1] // slots
    even = lax.rem(lax.axis_index("row"), 2) == 0
    tile = own_tile()
    for z in range(mine_ref.shape[0]):
        mine, other = mine_ref[z].astype(F32), other_ref[z].astype(F32)
        first = jnp.where(even, mine, other)
        second = jnp.where(even, other, mine)
        for slot in range(slots):
            at = slice(slot * share, (slot + 1) * share)
            start = slot * rank_cols + z * 2 * share
            extra_ref[start : start + 2 * share] = jnp.concatenate(
                [first[at], second[at]], axis=0
            ).astype(BF16)
    dense = dense_ref[...].astype(BF16)
    pieces = [project(dense, turned, slot, rank_cols) for slot in range(slots)]

    def coupling(left, right):
        left = pl.multiple_of(left * rank_cols, rank_cols)
        right = pl.multiple_of(right * rank_cols, rank_cols)
        return sum(
            dot_t(
                extra_ref[pl.ds(left, rank_cols), at * width : (at + 1) * width],
                turned[at][pl.ds(right, rank_cols), :],
            )
            for at in range(SIDE)
        )

    one = tile == 1
    pick = lambda a, b: jnp.where(one, a, b)
    pieces += [coupling(0, pick(1, 2)), coupling(pick(0, 1), 2)]
    send_ref[...] = jnp.concatenate(pieces, axis=0).astype(BF16)
    later_ref[:rank_cols] = coupling(pick(1, 2), 0).astype(BF16)
    later_ref[rank_cols:] = coupling(2, pick(0, 1)).astype(BF16)


def last_project_kernel(*refs):
    turned, (later_ref, dense_ref, send_ref) = refs[SIDE : 2 * SIDE], refs[2 * SIDE :]
    slots = SIDE - 1
    rank_cols = turned[0].shape[0] // slots
    whole = summed(refs[:SIDE])
    dense_ref[...] = whole
    dense = whole.astype(BF16)
    pieces = [project(dense, turned, slot, rank_cols) for slot in range(slots)]
    send = jnp.concatenate(pieces, axis=0).astype(BF16)
    n = send.shape[0]
    send_ref[:n] = send
    send_ref[n:] = later_ref[...]


def add_kernel(*refs):
    refs[-1][...] = summed(refs[:-1]).astype(BF16)


def finish_kernel(is_lower, *refs):
    dense_ref, extra_ref, ranks_ref = refs[SIDE : SIDE + 3]
    out_refs, sums_ref = refs[SIDE + 3 : -1], refs[-1]
    for s in range(SIDE):
        sums_ref[wrapped(own_tile() - s)] = refs[s][...]
    n = dense_ref.shape[0]
    rank_cols = extra_ref.shape[0] // (SIDE - 1)
    width = dense_ref.shape[1] // SIDE
    tile = lax.rem(lax.axis_index("col"), SIDE)
    columns = lax.broadcasted_iota(jnp.int32, (n, rank_cols), 1)
    at_coupling = (SIDE - 1) * n
    coupling = {}
    order = list(range(SIDE)) if is_lower else list(range(SIDE))[::-1]
    first, second, third, last = order
    for which, key in enumerate(((third, second, first), (last, second, first))):
        coupling[key] = (second, which)
    for which, key in enumerate(((last, third, first), (last, third, second))):
        coupling[key] = (third, which)
    if not is_lower:
        coupling = {
            (0, 2, 3): (2, 0), (1, 2, 3): (2, 1), (0, 1, 2): (1, 0), (0, 1, 3): (1, 1)
        }
    masked = {}
    for at, source in enumerate(order):
        for target in order[at + 1 :]:
            slot = partners(source).index(target)
            value = sums_ref[source, slot * n : (slot + 1) * n].astype(F32)
            for before in order[:at]:
                held, which = coupling[target, source, before]
                start = at_coupling + which * rank_cols
                value = value - dot(
                    masked[source, before], sums_ref[held, start : start + rank_cols]
                )
            keep = columns < RBLK * ranks_ref[pair_of(source, target)]
            masked[target, source] = jnp.where(keep, value, 0.0).astype(BF16)
    result = dense_ref[...]
    nothing = jnp.zeros((n, rank_cols), BF16)
    for slot in range(SIDE - 1):
        mine = nothing
        for target in range(SIDE):
            source = partners(target)[slot]
            if (target, source) in masked:
                mine = jnp.where(tile == target, masked[target, source], mine)
        result = result - dot(
            mine, extra_ref[slot * rank_cols : (slot + 1) * rank_cols]
        )
    result = result.astype(BF16)
    for at in range(SIDE):
        block = result[:, at * width : (at + 1) * width]
        if is_lower:
            out_refs[0][wrapped(tile - at)] = block
        else:
            out_refs[at][...] = block


def shards(
    right_sides, low_left, low_right, up_left, up_right, low_ranks, up_ranks, inv_lower, inv_upper
):
    n, width = right_sides.shape[1:]
    rank_cols = low_left.shape[2]
    slots = SIDE - 1
    share = rank_cols // lax.axis_size("row")
    total = SIDE * width
    shape = jax.ShapeDtypeStruct

    height = n + slots * share
    tied = lax.optimization_barrier
    parts = scattered_x(
        kernel_call(pack_kernel, [shape((2 * width + height, width), BF16)] * SIDE)(
            right_sides, low_left, up_left, inv_lower, inv_upper
        )
    )
    rows = kernel_call(
        lambda *refs: order_kernel(1, 2 * width, *refs),
        shape((SIDE, height, width), BF16),
    )(*parts)
    inverse = kernel_call(stack_kernel, shape((2, total, width), BF16))(*parts)
    inverse, rows = tied((inverse, rows))
    far, near = swap_pair(inverse), swap_core(inverse)
    near, gathered = tied((near, gathered_y(swapped(rows))))
    gathered, far, low_right, up_right = tied((gathered, far, low_right, up_right))
    turned = scattered_x(
        kernel_call(turn_kernel, [shape((slots * rank_cols, width), BF16)] * SIDE)(
            low_right, up_right
        )
    )
    inverses = [inverse, near, far, swap_core(far)]
    received = scattered_q(products(n, gathered, (0, 1), inverses))
    received, turned = tied((received, turned))
    dense, extra = kernel_call(
        lambda *refs: total_kernel(n, *refs),
        (shape((n, total), F32), shape((8, slots * share, total), BF16)),
    )(*received)
    mine = from_every_z(extra)
    packed = slots * n + 2 * rank_cols
    extra, send, later = kernel_call(
        couple_kernel,
        (
            shape((slots * rank_cols, total), BF16),
            shape((packed, rank_cols), BF16),
            shape((2 * rank_cols, rank_cols), BF16),
        ),
    )(dense, mine, swap_core(mine), *turned)

    def finished(is_lower, send, dense, ranks):
        sums = kernel_call(add_kernel, shape((packed, rank_cols), BF16))(*gathered_y(send))
        outs = [shape((SIDE, n, width), BF16)] if is_lower else [shape((n, width), BF16)] * SIDE
        return kernel_call(
            lambda *refs: finish_kernel(is_lower, *refs),
            outs,
            smem=(SIDE + 2,),
            scratch=[pltpu.VMEM((SIDE, packed, rank_cols), BF16)],
        )(*gathered_x(sums), dense, extra, ranks)

    [rows] = finished(True, send, dense, low_ranks)
    parts = products(n, gathered_y(swapped(rows)), (1,), inverses)
    dense, send = kernel_call(
        last_project_kernel,
        (shape((n, total), F32), shape((packed, rank_cols), BF16)),
    )(*scattered_q(parts), *turned, later)
    rows = finished(False, send, dense, up_ranks)
    return kernel_call(
        lambda *refs: order_kernel(-1, 0, *refs), shape((SIDE, n, width), F32)
    )(*scattered_x(rows, -1))


def solution(mesh):
    in_specs = (
        P(None, "row", "col"),
        P(None, "col", None),
        P(None, "col", None),
        P(None, "col", None),
        P(None, "col", None),
        P(),
        P(),
        P(None, "col", "row"),
        P(None, "col", "row"),
    )
    out_specs = P(None, "row", "col")
    return jax.shard_map(shards, mesh=mesh, in_specs=in_specs, out_specs=out_specs, check_vma=False)
```

```python
import jax
import jax.numpy as jnp
from jax import lax
from jax.experimental import pallas as pl
from jax.experimental.pallas import tpu as pltpu
from jax.sharding import PartitionSpec as P

RBLK = 32
BF16 = jnp.bfloat16
F32 = jnp.float32
SIDE = 4
Z_GROUPS = [[2 * z + core for z in range(8)] for core in range(2)]


def routes(to):
    index = lambda q, j, y, x: (SIDE * q + j) * SIDE * SIDE + SIDE * y + x
    span = range(SIDE)
    return [
        (index(q, j, y, x), index(*to(q, j, y, x)))
        for q in span for j in span for y in span for x in span
    ]


def permuted(value, to):
    return lax.ppermute(value, ("row", "col"), routes(to))


def gathered_y(value):
    return [value] + [
        permuted(value, lambda q, j, y, x: (q, j, (y + s) % SIDE, x)) for s in range(1, SIDE)
    ]


def gathered_x(value):
    return [value] + [
        permuted(value, lambda q, j, y, x: (q, j, y, (x + s) % SIDE)) for s in range(1, SIDE)
    ]


def scattered_q(values):
    return [values[0]] + [
        permuted(values[s], lambda q, j, y, x: ((q + s) % SIDE, j, y, x))
        for s in range(1, SIDE)
    ]


def scattered_x(values, sign=1):
    return [values[0]] + [
        permuted(values[s], lambda q, j, y, x: (q, j, y, (x + sign * s) % SIDE))
        for s in range(1, SIDE)
    ]


def from_every_z(value):
    return lax.all_to_all(value, "row", 0, 0, tiled=True, axis_index_groups=Z_GROUPS)


def own_tile():
    return lax.rem(lax.axis_index("col"), SIDE)


def wrapped(value):
    return lax.rem(value + 2 * SIDE, SIDE)


def swapped(value):
    return permuted(value, lambda q, j, y, x: (y, j, q, x))


def swap_core(value):
    return permuted(value, lambda q, j, y, x: (q, j ^ 1, y, x))


def swap_pair(value):
    return permuted(value, lambda q, j, y, x: (q, j ^ 2, y, x))


def dot(left, right):
    return jnp.dot(left, right, preferred_element_type=F32)


def dot_t(left, right):
    return lax.dot_general(
        left, right, (((1,), (1,)), ((), ())), preferred_element_type=F32
    )


def pair_of(i, j):
    high, low = max(i, j), min(i, j)
    return high * (high - 1) // 2 + low


def partners(tile):
    return [t for t in range(SIDE) if t != tile]


def kernel_call(body, out_shape, smem=(), flops=0, grid=None, in_specs=None, out_specs=None, scratch=()):
    def run(*args):
        specs = in_specs or [
            pl.BlockSpec(memory_space=pltpu.SMEM if at in smem else pltpu.VMEM)
            for at in range(len(args))
        ]
        outs = jax.tree.leaves(out_shape)
        moved = sum(a.size * a.dtype.itemsize for a in [*args, *outs])
        more = {} if grid is None else {"grid": grid, "out_specs": out_specs}
        return pl.pallas_call(
            body,
            out_shape=out_shape,
            in_specs=specs,
            scratch_shapes=list(scratch),
            compiler_params=pltpu.CompilerParams(vmem_limit_bytes=30 * 2**20),
            cost_estimate=pl.CostEstimate(
                flops=flops, bytes_accessed=moved, transcendentals=0
            ),
            **more,
        )(*args)

    return run


def pack_kernel(right_ref, low_ref, up_ref, *out_refs):
    n = right_ref.shape[1]
    rank_cols = low_ref.shape[2]
    share = rank_cols // lax.axis_size("row")
    row = lax.axis_index("row")
    at = lax.broadcasted_iota(jnp.int32, (share, rank_cols), 1)
    want = lax.broadcasted_iota(jnp.int32, (share, rank_cols), 0) + row * share
    pick = (at == want).astype(F32).astype(BF16)
    for s, out_ref in enumerate(out_refs):
        tile = wrapped(own_tile() + s)
        out_ref[:n] = right_ref[tile].astype(BF16)
        pieces = []
        for slot in range(SIDE - 1):
            pair, is_low = partner_pair(tile, slot)
            piece = jnp.where(is_low, dot_t(pick, low_ref[pair]), dot_t(pick, up_ref[pair]))
            pieces.append(piece)
        out_ref[n:] = jnp.concatenate(pieces, axis=0).astype(BF16)


def partner_pair(tile, slot):
    is_low = slot < tile
    partner = jnp.where(is_low, slot, slot + 1)
    high = jnp.where(is_low, tile, partner)
    low = jnp.where(is_low, partner, tile)
    return jnp.where(high == 1, 0, jnp.where(high == 2, 1, 3)) + low, is_low


def order_kernel(sign, *refs):
    out_ref = refs[-1]
    for s in range(SIDE):
        out_ref[wrapped(own_tile() - sign * s)] = refs[s][...].astype(out_ref.dtype)


def stack_kernel(*refs):
    rows = refs[0].shape[0]
    for s, ref in enumerate(refs[:-1]):
        refs[-1][s * rows : (s + 1) * rows] = ref[...]


def deal_kernel(inverse_ref, *out_refs):
    for s in range(SIDE):
        out_refs[s][...] = inverse_ref[wrapped(own_tile() + s)]


def turn_kernel(low_ref, up_ref, *out_refs):
    rank_cols = low_ref.shape[2]
    one = lax.broadcasted_iota(jnp.int32, (rank_cols, rank_cols), 0)
    two = lax.broadcasted_iota(jnp.int32, (rank_cols, rank_cols), 1)
    eye = (one == two).astype(F32).astype(BF16)
    for s, out_ref in enumerate(out_refs):
        tile = wrapped(own_tile() + s)
        for slot in range(SIDE - 1):
            pair, is_low = partner_pair(tile, slot)
            factor = jnp.where(is_low, up_ref[pair], low_ref[pair])
            out_ref[slot * rank_cols : (slot + 1) * rank_cols] = dot_t(eye, factor).astype(BF16)


def products_kernel(n, padded, count, *refs):
    x_refs, inverse_refs = refs[:SIDE], refs[SIDE : SIDE + count]
    out_refs = refs[SIDE + count : -2]
    joined_ref, extra_ref = refs[-2:]
    lower, upper = inverse_refs[:SIDE], inverse_refs[SIDE:]
    rows = x_refs[0].shape[1]

    @pl.when(pl.program_id(0) == 0)
    def _():
        row = lax.axis_index("row")
        flip, q = lax.rem(row, SIDE), row // SIDE
        y = lax.axis_index("col") // SIDE
        for s in range(SIDE):
            t = wrapped(y - s - q)
            for at in range(SIDE):
                block = x_refs[s][at ^ flip]
                joined_ref[at, t, :rows] = block
                if rows > n:
                    extra_ref[at, t, : rows - n] = block[n:]

    width = joined_ref.shape[3]
    value = sum(
        dot_t(joined_ref[at].reshape(SIDE * padded, width), lower[at][...])
        for at in range(SIDE)
    )
    if rows > n:
        other = sum(
            dot_t(extra_ref[at].reshape(SIDE * (padded - n), width), upper[at][...])
            for at in range(SIDE)
        )
        share = (rows - n) // (SIDE - 1)
        slot = lax.broadcasted_iota(jnp.int32, (rows - n, value.shape[1]), 0) // share
    for t in range(SIDE):
        start = t * padded
        out_refs[t][:n] = value[start : start + n].astype(BF16)
        if rows > n:
            mine = value[start + n : start + rows]
            its = other[t * (padded - n) : t * (padded - n) + rows - n]
            out_refs[t][n:] = jnp.where(slot < own_tile(), mine, its).astype(BF16)


def products(n, gathered, *inverses):
    blocks, rows, width = gathered[0].shape
    total = inverses[0].shape[0]
    padded = rows + -rows % 16
    count = len(inverses)
    whole = pl.BlockSpec(gathered[0].shape, lambda a: (0, 0, 0))
    return kernel_call(
        lambda *refs: products_kernel(n, padded, count, *refs),
        [jax.ShapeDtypeStruct((rows, total), BF16)] * SIDE,
        flops=2 * SIDE * blocks * rows * width * total,
        grid=(total // 256,),
        in_specs=[whole] * SIDE
        + [pl.BlockSpec((256, width), lambda a: (a, 0)) for _ in inverses],
        out_specs=[pl.BlockSpec((rows, 256), lambda a: (0, a))] * SIDE,
        scratch=[
            pltpu.VMEM((blocks, SIDE, padded, width), BF16),
            pltpu.VMEM((blocks, SIDE, max(padded - n, 16), width), BF16),
        ],
    )(*gathered, *inverses)


def summed(refs):
    whole = refs[0][...].astype(F32)
    for ref in refs[1:]:
        whole = whole + ref[...].astype(F32)
    return whole


def total_kernel(n, *refs):
    dense_ref, extra_ref = refs[SIDE:]
    whole = summed(refs[:SIDE])
    dense_ref[...] = whole[:n]
    extra = whole[n:].astype(BF16)
    for at in range(extra_ref.shape[0]):
        extra_ref[at] = extra


def project(dense, turned, slot, rank_cols):
    width = turned[0].shape[1]
    return sum(
        dot_t(
            dense[:, at * width : (at + 1) * width],
            turned[at][slot * rank_cols : (slot + 1) * rank_cols],
        )
        for at in range(SIDE)
    )


def couple_kernel(dense_ref, mine_ref, other_ref, *refs):
    turned, (extra_ref, send_ref, later_ref) = refs[:SIDE], refs[SIDE:]
    slots = SIDE - 1
    rank_cols = turned[0].shape[0] // slots
    width = turned[0].shape[1]
    share = mine_ref.shape[1] // slots
    even = lax.rem(lax.axis_index("row"), 2) == 0
    tile = own_tile()
    for z in range(mine_ref.shape[0]):
        mine, other = mine_ref[z].astype(F32), other_ref[z].astype(F32)
        first = jnp.where(even, mine, other)
        second = jnp.where(even, other, mine)
        for slot in range(slots):
            at = slice(slot * share, (slot + 1) * share)
            start = slot * rank_cols + z * 2 * share
            extra_ref[start : start + 2 * share] = jnp.concatenate(
                [first[at], second[at]], axis=0
            ).astype(BF16)
    dense = dense_ref[...].astype(BF16)
    pieces = [project(dense, turned, slot, rank_cols) for slot in range(slots)]

    def coupling(left, right):
        left = pl.multiple_of(left * rank_cols, rank_cols)
        right = pl.multiple_of(right * rank_cols, rank_cols)
        return sum(
            dot_t(
                extra_ref[pl.ds(left, rank_cols), at * width : (at + 1) * width],
                turned[at][pl.ds(right, rank_cols), :],
            )
            for at in range(SIDE)
        )

    one = tile == 1
    pick = lambda a, b: jnp.where(one, a, b)
    pieces += [coupling(0, pick(1, 2)), coupling(pick(0, 1), 2)]
    send_ref[...] = jnp.concatenate(pieces, axis=0).astype(BF16)
    later_ref[:rank_cols] = coupling(pick(1, 2), 0).astype(BF16)
    later_ref[rank_cols:] = coupling(2, pick(0, 1)).astype(BF16)


def last_project_kernel(*refs):
    turned, (later_ref, dense_ref, send_ref) = refs[SIDE : 2 * SIDE], refs[2 * SIDE :]
    slots = SIDE - 1
    rank_cols = turned[0].shape[0] // slots
    whole = summed(refs[:SIDE])
    dense_ref[...] = whole
    dense = whole.astype(BF16)
    pieces = [project(dense, turned, slot, rank_cols) for slot in range(slots)]
    send = jnp.concatenate(pieces, axis=0).astype(BF16)
    n = send.shape[0]
    send_ref[:n] = send
    send_ref[n:] = later_ref[...]


def add_kernel(*refs):
    refs[-1][...] = summed(refs[:-1]).astype(BF16)


def finish_kernel(is_lower, *refs):
    dense_ref, extra_ref, ranks_ref = refs[SIDE : SIDE + 3]
    out_refs, sums_ref = refs[SIDE + 3 : -1], refs[-1]
    for s in range(SIDE):
        sums_ref[wrapped(own_tile() - s)] = refs[s][...]
    n = dense_ref.shape[0]
    rank_cols = extra_ref.shape[0] // (SIDE - 1)
    width = dense_ref.shape[1] // SIDE
    tile = lax.rem(lax.axis_index("col"), SIDE)
    columns = lax.broadcasted_iota(jnp.int32, (n, rank_cols), 1)
    at_coupling = (SIDE - 1) * n
    coupling = {}
    order = list(range(SIDE)) if is_lower else list(range(SIDE))[::-1]
    first, second, third, last = order
    for which, key in enumerate(((third, second, first), (last, second, first))):
        coupling[key] = (second, which)
    for which, key in enumerate(((last, third, first), (last, third, second))):
        coupling[key] = (third, which)
    if not is_lower:
        coupling = {
            (0, 2, 3): (2, 0), (1, 2, 3): (2, 1), (0, 1, 2): (1, 0), (0, 1, 3): (1, 1)
        }
    masked = {}
    for at, source in enumerate(order):
        for target in order[at + 1 :]:
            slot = partners(source).index(target)
            value = sums_ref[source, slot * n : (slot + 1) * n].astype(F32)
            for before in order[:at]:
                held, which = coupling[target, source, before]
                start = at_coupling + which * rank_cols
                value = value - dot(
                    masked[source, before], sums_ref[held, start : start + rank_cols]
                )
            keep = columns < RBLK * ranks_ref[pair_of(source, target)]
            masked[target, source] = jnp.where(keep, value, 0.0).astype(BF16)
    result = dense_ref[...]
    nothing = jnp.zeros((n, rank_cols), BF16)
    for slot in range(SIDE - 1):
        mine = nothing
        for target in range(SIDE):
            source = partners(target)[slot]
            if (target, source) in masked:
                mine = jnp.where(tile == target, masked[target, source], mine)
        result = result - dot(
            mine, extra_ref[slot * rank_cols : (slot + 1) * rank_cols]
        )
    result = result.astype(BF16)
    for at in range(SIDE):
        block = result[:, at * width : (at + 1) * width]
        if is_lower:
            out_refs[0][wrapped(tile - at)] = block
        else:
            out_refs[at][...] = block


def shards(
    right_sides, low_left, low_right, up_left, up_right, low_ranks, up_ranks, inv_lower, inv_upper
):
    n, width = right_sides.shape[1:]
    rank_cols = low_left.shape[2]
    slots = SIDE - 1
    share = rank_cols // lax.axis_size("row")
    total = SIDE * width
    shape = jax.ShapeDtypeStruct

    height = n + slots * share
    tied = lax.optimization_barrier
    deal = kernel_call(deal_kernel, [shape((width, width), BF16)] * SIDE)
    stack = kernel_call(stack_kernel, shape((total, width), BF16))
    parts = scattered_x(deal(inv_lower))
    rows = scattered_x(
        kernel_call(pack_kernel, [shape((height, width), BF16)] * SIDE)(
            right_sides, low_left, up_left
        )
    )
    parts, rows = tied((parts, rows))
    rows = kernel_call(
        lambda *refs: order_kernel(1, *refs), shape((SIDE, height, width), BF16)
    )(*rows)
    lower = stack(*parts)
    rows, lower, inv_upper = tied((rows, lower, inv_upper))
    far_lower = swap_pair(lower)
    parts, rows = tied((scattered_x(deal(inv_upper)), swapped(rows)))
    upper = stack(*parts)
    far_upper = swap_pair(upper)
    gathered = gathered_y(rows)
    gathered, far_lower, lower, near_upper = tied(
        (gathered, far_lower, lower, swap_core(upper))
    )
    lower = [lower, swap_core(lower), far_lower, swap_core(far_lower)]
    gathered, low_right, up_right = tied((gathered, low_right, up_right))
    turned = scattered_x(
        kernel_call(turn_kernel, [shape((slots * rank_cols, width), BF16)] * SIDE)(
            low_right, up_right
        )
    )
    turned, far_upper, lower = tied((turned, far_upper, lower))
    upper = [upper, near_upper, far_upper, swap_core(far_upper)]
    received = scattered_q(products(n, gathered, *lower, *upper))
    dense, extra = kernel_call(
        lambda *refs: total_kernel(n, *refs),
        (shape((n, total), F32), shape((8, slots * share, total), BF16)),
    )(*received)
    mine = from_every_z(extra)
    packed = slots * n + 2 * rank_cols
    extra, send, later = kernel_call(
        couple_kernel,
        (
            shape((slots * rank_cols, total), BF16),
            shape((packed, rank_cols), BF16),
            shape((2 * rank_cols, rank_cols), BF16),
        ),
    )(dense, mine, swap_core(mine), *turned)

    def finished(is_lower, send, dense, ranks):
        sums = kernel_call(add_kernel, shape((packed, rank_cols), BF16))(*gathered_y(send))
        outs = [shape((SIDE, n, width), BF16)] if is_lower else [shape((n, width), BF16)] * SIDE
        return kernel_call(
            lambda *refs: finish_kernel(is_lower, *refs),
            outs,
            smem=(SIDE + 2,),
            scratch=[pltpu.VMEM((SIDE, packed, rank_cols), BF16)],
        )(*gathered_x(sums), dense, extra, ranks)

    [rows] = finished(True, send, dense, low_ranks)
    parts = products(n, gathered_y(swapped(rows)), *upper)
    dense, send = kernel_call(
        last_project_kernel,
        (shape((n, total), F32), shape((packed, rank_cols), BF16)),
    )(*scattered_q(parts), *turned, later)
    rows = finished(False, send, dense, up_ranks)
    return kernel_call(
        lambda *refs: order_kernel(-1, *refs), shape((SIDE, n, width), F32)
    )(*scattered_x(rows, -1))


def solution(mesh):
    in_specs = (
        P(None, "row", "col"),
        P(None, "col", None),
        P(None, "col", None),
        P(None, "col", None),
        P(None, "col", None),
        P(),
        P(),
        P(None, "col", "row"),
        P(None, "col", "row"),
    )
    out_specs = P(None, "row", "col")
    return jax.shard_map(shards, mesh=mesh, in_specs=in_specs, out_specs=out_specs, check_vma=False)
```

```python
import jax
import jax.numpy as jnp
from jax import lax
from jax.experimental import pallas as pl
from jax.experimental.pallas import tpu as pltpu
from jax.sharding import PartitionSpec as P

RBLK = 32
BF16 = jnp.bfloat16
F32 = jnp.float32
SIDE = 4
Z_GROUPS = [[2 * z + core for z in range(8)] for core in range(2)]


def routes(to):
    index = lambda q, j, y, x: (SIDE * q + j) * SIDE * SIDE + SIDE * y + x
    span = range(SIDE)
    return [
        (index(q, j, y, x), index(*to(q, j, y, x)))
        for q in span for j in span for y in span for x in span
    ]


def permuted(value, to):
    return lax.ppermute(value, ("row", "col"), routes(to))


def gathered_y(value):
    return [value] + [
        permuted(value, lambda q, j, y, x: (q, j, (y + s) % SIDE, x)) for s in range(1, SIDE)
    ]


def gathered_x(value):
    return [value] + [
        permuted(value, lambda q, j, y, x: (q, j, y, (x + s) % SIDE)) for s in range(1, SIDE)
    ]


def scattered_q(values):
    return [values[0]] + [
        permuted(values[s], lambda q, j, y, x: ((q + s) % SIDE, j, y, x))
        for s in range(1, SIDE)
    ]


def scattered_x(values, sign=1):
    return [values[0]] + [
        permuted(values[s], lambda q, j, y, x: (q, j, y, (x + sign * s) % SIDE))
        for s in range(1, SIDE)
    ]


def from_every_z(value):
    return lax.all_to_all(value, "row", 0, 0, tiled=True, axis_index_groups=Z_GROUPS)


def own_tile():
    return lax.rem(lax.axis_index("col"), SIDE)


def wrapped(value):
    return lax.rem(value + 2 * SIDE, SIDE)


def swapped(value):
    return permuted(value, lambda q, j, y, x: (y, j, q, x))


def swap_core(value):
    return permuted(value, lambda q, j, y, x: (q, j ^ 1, y, x))


def swap_pair(value):
    return permuted(value, lambda q, j, y, x: (q, j ^ 2, y, x))


def dot(left, right):
    return jnp.dot(left, right, preferred_element_type=F32)


def dot_t(left, right):
    return lax.dot_general(
        left, right, (((1,), (1,)), ((), ())), preferred_element_type=F32
    )


def pair_of(i, j):
    high, low = max(i, j), min(i, j)
    return high * (high - 1) // 2 + low


def partners(tile):
    return [t for t in range(SIDE) if t != tile]


def kernel_call(body, out_shape, smem=(), flops=0, grid=None, in_specs=None, out_specs=None, scratch=()):
    def run(*args):
        specs = in_specs or [
            pl.BlockSpec(memory_space=pltpu.SMEM if at in smem else pltpu.VMEM)
            for at in range(len(args))
        ]
        outs = jax.tree.leaves(out_shape)
        moved = sum(a.size * a.dtype.itemsize for a in [*args, *outs])
        more = {} if grid is None else {"grid": grid, "out_specs": out_specs}
        return pl.pallas_call(
            body,
            out_shape=out_shape,
            in_specs=specs,
            scratch_shapes=list(scratch),
            compiler_params=pltpu.CompilerParams(vmem_limit_bytes=30 * 2**20),
            cost_estimate=pl.CostEstimate(
                flops=flops, bytes_accessed=moved, transcendentals=0
            ),
            **more,
        )(*args)

    return run


def pack_kernel(right_ref, low_ref, up_ref, *out_refs):
    n = right_ref.shape[1]
    rank_cols = low_ref.shape[2]
    share = rank_cols // lax.axis_size("row")
    row = lax.axis_index("row")
    at = lax.broadcasted_iota(jnp.int32, (share, rank_cols), 1)
    want = lax.broadcasted_iota(jnp.int32, (share, rank_cols), 0) + row * share
    pick = (at == want).astype(F32).astype(BF16)
    for s, out_ref in enumerate(out_refs):
        tile = wrapped(own_tile() + s)
        out_ref[:n] = right_ref[tile].astype(BF16)
        pieces = []
        for slot in range(SIDE - 1):
            pair, is_low = partner_pair(tile, slot)
            piece = jnp.where(is_low, dot_t(pick, low_ref[pair]), dot_t(pick, up_ref[pair]))
            pieces.append(piece)
        out_ref[n:] = jnp.concatenate(pieces, axis=0).astype(BF16)


def partner_pair(tile, slot):
    is_low = slot < tile
    partner = jnp.where(is_low, slot, slot + 1)
    high = jnp.where(is_low, tile, partner)
    low = jnp.where(is_low, partner, tile)
    return jnp.where(high == 1, 0, jnp.where(high == 2, 1, 3)) + low, is_low


def order_kernel(sign, *refs):
    out_ref = refs[-1]
    for s in range(SIDE):
        out_ref[wrapped(own_tile() - sign * s)] = refs[s][...].astype(out_ref.dtype)


def stack_kernel(*refs):
    rows = refs[0].shape[0]
    for s, ref in enumerate(refs[:-1]):
        refs[-1][s * rows : (s + 1) * rows] = ref[...]


def deal_kernel(inverse_ref, *out_refs):
    for s in range(SIDE):
        out_refs[s][...] = inverse_ref[wrapped(own_tile() + s)]


def turn_kernel(low_ref, up_ref, *out_refs):
    rank_cols = low_ref.shape[2]
    one = lax.broadcasted_iota(jnp.int32, (rank_cols, rank_cols), 0)
    two = lax.broadcasted_iota(jnp.int32, (rank_cols, rank_cols), 1)
    eye = (one == two).astype(F32).astype(BF16)
    for s, out_ref in enumerate(out_refs):
        tile = wrapped(own_tile() + s)
        for slot in range(SIDE - 1):
            pair, is_low = partner_pair(tile, slot)
            factor = jnp.where(is_low, up_ref[pair], low_ref[pair])
            out_ref[slot * rank_cols : (slot + 1) * rank_cols] = dot_t(eye, factor).astype(BF16)


def products_kernel(n, padded, count, *refs):
    x_refs, inverse_refs = refs[:SIDE], refs[SIDE : SIDE + count]
    out_refs = refs[SIDE + count : -2]
    joined_ref, extra_ref = refs[-2:]
    lower, upper = inverse_refs[:SIDE], inverse_refs[SIDE:]
    rows = x_refs[0].shape[1]

    @pl.when(pl.program_id(0) == 0)
    def _():
        row = lax.axis_index("row")
        flip, q = lax.rem(row, SIDE), row // SIDE
        y = lax.axis_index("col") // SIDE
        for s in range(SIDE):
            t = wrapped(y - s - q)
            for at in range(SIDE):
                block = x_refs[s][at ^ flip]
                joined_ref[at, t, :rows] = block
                if rows > n:
                    extra_ref[at, t, : rows - n] = block[n:]

    width = joined_ref.shape[3]
    value = sum(
        dot_t(joined_ref[at].reshape(SIDE * padded, width), lower[at][...])
        for at in range(SIDE)
    )
    if rows > n:
        other = sum(
            dot_t(extra_ref[at].reshape(SIDE * (padded - n), width), upper[at][...])
            for at in range(SIDE)
        )
        share = (rows - n) // (SIDE - 1)
        slot = lax.broadcasted_iota(jnp.int32, (rows - n, value.shape[1]), 0) // share
    for t in range(SIDE):
        start = t * padded
        out_refs[t][:n] = value[start : start + n].astype(BF16)
        if rows > n:
            mine = value[start + n : start + rows]
            its = other[t * (padded - n) : t * (padded - n) + rows - n]
            out_refs[t][n:] = jnp.where(slot < own_tile(), mine, its).astype(BF16)


def products(n, gathered, *inverses):
    blocks, rows, width = gathered[0].shape
    total = inverses[0].shape[0]
    padded = rows + -rows % 16
    count = len(inverses)
    whole = pl.BlockSpec(gathered[0].shape, lambda a: (0, 0, 0))
    return kernel_call(
        lambda *refs: products_kernel(n, padded, count, *refs),
        [jax.ShapeDtypeStruct((rows, total), BF16)] * SIDE,
        flops=2 * SIDE * blocks * rows * width * total,
        grid=(total // 256,),
        in_specs=[whole] * SIDE
        + [pl.BlockSpec((256, width), lambda a: (a, 0)) for _ in inverses],
        out_specs=[pl.BlockSpec((rows, 256), lambda a: (0, a))] * SIDE,
        scratch=[
            pltpu.VMEM((blocks, SIDE, padded, width), BF16),
            pltpu.VMEM((blocks, SIDE, max(padded - n, 16), width), BF16),
        ],
    )(*gathered, *inverses)


def summed(refs):
    whole = refs[0][...].astype(F32)
    for ref in refs[1:]:
        whole = whole + ref[...].astype(F32)
    return whole


def total_kernel(n, *refs):
    dense_ref, extra_ref = refs[SIDE:]
    whole = summed(refs[:SIDE])
    dense_ref[...] = whole[:n]
    extra = whole[n:].astype(BF16)
    for at in range(extra_ref.shape[0]):
        extra_ref[at] = extra


def project(dense, turned, slot, rank_cols):
    width = turned[0].shape[1]
    return sum(
        dot_t(
            dense[:, at * width : (at + 1) * width],
            turned[at][slot * rank_cols : (slot + 1) * rank_cols],
        )
        for at in range(SIDE)
    )


def couple_kernel(dense_ref, mine_ref, other_ref, *refs):
    turned, (extra_ref, send_ref, later_ref) = refs[:SIDE], refs[SIDE:]
    slots = SIDE - 1
    rank_cols = turned[0].shape[0] // slots
    width = turned[0].shape[1]
    share = mine_ref.shape[1] // slots
    even = lax.rem(lax.axis_index("row"), 2) == 0
    tile = own_tile()
    for z in range(mine_ref.shape[0]):
        mine, other = mine_ref[z].astype(F32), other_ref[z].astype(F32)
        first = jnp.where(even, mine, other)
        second = jnp.where(even, other, mine)
        for slot in range(slots):
            at = slice(slot * share, (slot + 1) * share)
            start = slot * rank_cols + z * 2 * share
            extra_ref[start : start + 2 * share] = jnp.concatenate(
                [first[at], second[at]], axis=0
            ).astype(BF16)
    dense = dense_ref[...].astype(BF16)
    pieces = [project(dense, turned, slot, rank_cols) for slot in range(slots)]

    def coupling(left, right):
        left = pl.multiple_of(left * rank_cols, rank_cols)
        right = pl.multiple_of(right * rank_cols, rank_cols)
        return sum(
            dot_t(
                extra_ref[pl.ds(left, rank_cols), at * width : (at + 1) * width],
                turned[at][pl.ds(right, rank_cols), :],
            )
            for at in range(SIDE)
        )

    one = tile == 1
    pick = lambda a, b: jnp.where(one, a, b)
    pieces += [coupling(0, pick(1, 2)), coupling(pick(0, 1), 2)]
    send_ref[...] = jnp.concatenate(pieces, axis=0).astype(BF16)
    later_ref[:rank_cols] = coupling(pick(1, 2), 0).astype(BF16)
    later_ref[rank_cols:] = coupling(2, pick(0, 1)).astype(BF16)


def last_project_kernel(*refs):
    turned, (later_ref, dense_ref, send_ref) = refs[SIDE : 2 * SIDE], refs[2 * SIDE :]
    slots = SIDE - 1
    rank_cols = turned[0].shape[0] // slots
    whole = summed(refs[:SIDE])
    dense_ref[...] = whole
    dense = whole.astype(BF16)
    pieces = [project(dense, turned, slot, rank_cols) for slot in range(slots)]
    send = jnp.concatenate(pieces, axis=0).astype(BF16)
    n = send.shape[0]
    send_ref[:n] = send
    send_ref[n:] = later_ref[...]


def add_kernel(*refs):
    refs[-1][...] = summed(refs[:-1]).astype(BF16)


def finish_kernel(is_lower, *refs):
    dense_ref, extra_ref, ranks_ref = refs[SIDE : SIDE + 3]
    out_refs, sums_ref = refs[SIDE + 3 : -1], refs[-1]
    for s in range(SIDE):
        sums_ref[wrapped(own_tile() - s)] = refs[s][...]
    n = dense_ref.shape[0]
    rank_cols = extra_ref.shape[0] // (SIDE - 1)
    width = dense_ref.shape[1] // SIDE
    tile = lax.rem(lax.axis_index("col"), SIDE)
    columns = lax.broadcasted_iota(jnp.int32, (n, rank_cols), 1)
    at_coupling = (SIDE - 1) * n
    coupling = {}
    order = list(range(SIDE)) if is_lower else list(range(SIDE))[::-1]
    first, second, third, last = order
    for which, key in enumerate(((third, second, first), (last, second, first))):
        coupling[key] = (second, which)
    for which, key in enumerate(((last, third, first), (last, third, second))):
        coupling[key] = (third, which)
    if not is_lower:
        coupling = {
            (0, 2, 3): (2, 0), (1, 2, 3): (2, 1), (0, 1, 2): (1, 0), (0, 1, 3): (1, 1)
        }
    masked = {}
    for at, source in enumerate(order):
        for target in order[at + 1 :]:
            slot = partners(source).index(target)
            value = sums_ref[source, slot * n : (slot + 1) * n].astype(F32)
            for before in order[:at]:
                held, which = coupling[target, source, before]
                start = at_coupling + which * rank_cols
                value = value - dot(
                    masked[source, before], sums_ref[held, start : start + rank_cols]
                )
            keep = columns < RBLK * ranks_ref[pair_of(source, target)]
            masked[target, source] = jnp.where(keep, value, 0.0).astype(BF16)
    result = dense_ref[...]
    nothing = jnp.zeros((n, rank_cols), BF16)
    for slot in range(SIDE - 1):
        mine = nothing
        for target in range(SIDE):
            source = partners(target)[slot]
            if (target, source) in masked:
                mine = jnp.where(tile == target, masked[target, source], mine)
        result = result - dot(
            mine, extra_ref[slot * rank_cols : (slot + 1) * rank_cols]
        )
    result = result.astype(BF16)
    for at in range(SIDE):
        block = result[:, at * width : (at + 1) * width]
        if is_lower:
            out_refs[0][wrapped(tile - at)] = block
        else:
            out_refs[at][...] = block


def shards(
    right_sides, low_left, low_right, up_left, up_right, low_ranks, up_ranks, inv_lower, inv_upper
):
    n, width = right_sides.shape[1:]
    rank_cols = low_left.shape[2]
    slots = SIDE - 1
    share = rank_cols // lax.axis_size("row")
    total = SIDE * width
    shape = jax.ShapeDtypeStruct

    height = n + slots * share
    tied = lax.optimization_barrier
    deal = kernel_call(deal_kernel, [shape((width, width), BF16)] * SIDE)
    stack = kernel_call(stack_kernel, shape((total, width), BF16))
    parts = scattered_x(deal(inv_lower))
    rows = scattered_x(
        kernel_call(pack_kernel, [shape((height, width), BF16)] * SIDE)(
            right_sides, low_left, up_left
        )
    )
    parts, rows = tied((parts, rows))
    rows = kernel_call(
        lambda *refs: order_kernel(1, *refs), shape((SIDE, height, width), BF16)
    )(*rows)
    lower = stack(*parts)
    rows, lower, inv_upper = tied((rows, lower, inv_upper))
    far_lower = swap_pair(lower)
    parts, rows = tied((scattered_x(deal(inv_upper)), swapped(rows)))
    upper = stack(*parts)
    far_upper = swap_pair(upper)
    gathered = gathered_y(rows)
    gathered, far_lower, lower, upper = tied((gathered, far_lower, lower, upper))
    near_upper = swap_core(upper)
    lower = [lower, swap_core(lower), far_lower, swap_core(far_lower)]
    gathered, low_right, up_right = tied((gathered, low_right, up_right))
    turned = scattered_x(
        kernel_call(turn_kernel, [shape((slots * rank_cols, width), BF16)] * SIDE)(
            low_right, up_right
        )
    )
    upper = [upper, near_upper, far_upper, swap_core(far_upper)]
    received = scattered_q(products(n, gathered, *lower, *upper))
    received, turned = tied((received, turned))
    dense, extra = kernel_call(
        lambda *refs: total_kernel(n, *refs),
        (shape((n, total), F32), shape((8, slots * share, total), BF16)),
    )(*received)
    mine = from_every_z(extra)
    packed = slots * n + 2 * rank_cols
    extra, send, later = kernel_call(
        couple_kernel,
        (
            shape((slots * rank_cols, total), BF16),
            shape((packed, rank_cols), BF16),
            shape((2 * rank_cols, rank_cols), BF16),
        ),
    )(dense, mine, swap_core(mine), *turned)

    def finished(is_lower, send, dense, ranks):
        sums = kernel_call(add_kernel, shape((packed, rank_cols), BF16))(*gathered_y(send))
        outs = [shape((SIDE, n, width), BF16)] if is_lower else [shape((n, width), BF16)] * SIDE
        return kernel_call(
            lambda *refs: finish_kernel(is_lower, *refs),
            outs,
            smem=(SIDE + 2,),
            scratch=[pltpu.VMEM((SIDE, packed, rank_cols), BF16)],
        )(*gathered_x(sums), dense, extra, ranks)

    [rows] = finished(True, send, dense, low_ranks)
    parts = products(n, gathered_y(swapped(rows)), *upper)
    dense, send = kernel_call(
        last_project_kernel,
        (shape((n, total), F32), shape((packed, rank_cols), BF16)),
    )(*scattered_q(parts), *turned, later)
    rows = finished(False, send, dense, up_ranks)
    return kernel_call(
        lambda *refs: order_kernel(-1, *refs), shape((SIDE, n, width), F32)
    )(*scattered_x(rows, -1))


def solution(mesh):
    in_specs = (
        P(None, "row", "col"),
        P(None, "col", None),
        P(None, "col", None),
        P(None, "col", None),
        P(None, "col", None),
        P(),
        P(),
        P(None, "col", "row"),
        P(None, "col", "row"),
    )
    out_specs = P(None, "row", "col")
    return jax.shard_map(shards, mesh=mesh, in_specs=in_specs, out_specs=out_specs, check_vma=False)
```

```python
import jax
import jax.numpy as jnp
from jax import lax
from jax.experimental import pallas as pl
from jax.experimental.pallas import tpu as pltpu
from jax.sharding import PartitionSpec as P

RBLK = 32
BF16 = jnp.bfloat16
F32 = jnp.float32
SIDE = 4
Z_GROUPS = [[2 * z + core for z in range(8)] for core in range(2)]


def routes(to):
    index = lambda q, j, y, x: (SIDE * q + j) * SIDE * SIDE + SIDE * y + x
    span = range(SIDE)
    return [
        (index(q, j, y, x), index(*to(q, j, y, x)))
        for q in span for j in span for y in span for x in span
    ]


def permuted(value, to):
    return lax.ppermute(value, ("row", "col"), routes(to))


def gathered_y(value):
    return [value] + [
        permuted(value, lambda q, j, y, x: (q, j, (y + s) % SIDE, x)) for s in range(1, SIDE)
    ]


def gathered_x(value):
    return [value] + [
        permuted(value, lambda q, j, y, x: (q, j, y, (x + s) % SIDE)) for s in range(1, SIDE)
    ]


def scattered_q(values):
    return [values[0]] + [
        permuted(values[s], lambda q, j, y, x: ((q + s) % SIDE, j, y, x))
        for s in range(1, SIDE)
    ]


def scattered_x(values, sign=1):
    return [values[0]] + [
        permuted(values[s], lambda q, j, y, x: (q, j, y, (x + sign * s) % SIDE))
        for s in range(1, SIDE)
    ]


def from_every_z(value):
    return lax.all_to_all(value, "row", 0, 0, tiled=True, axis_index_groups=Z_GROUPS)


def own_tile():
    return lax.rem(lax.axis_index("col"), SIDE)


def wrapped(value):
    return lax.rem(value + 2 * SIDE, SIDE)


def swapped(value):
    return permuted(value, lambda q, j, y, x: (y, j, q, x))


def swap_core(value):
    return permuted(value, lambda q, j, y, x: (q, j ^ 1, y, x))


def swap_pair(value):
    return permuted(value, lambda q, j, y, x: (q, j ^ 2, y, x))


def dot(left, right):
    return jnp.dot(left, right, preferred_element_type=F32)


def dot_t(left, right):
    return lax.dot_general(
        left, right, (((1,), (1,)), ((), ())), preferred_element_type=F32
    )


def pair_of(i, j):
    high, low = max(i, j), min(i, j)
    return high * (high - 1) // 2 + low


def partners(tile):
    return [t for t in range(SIDE) if t != tile]


def kernel_call(body, out_shape, smem=(), flops=0, grid=None, in_specs=None, out_specs=None, scratch=()):
    def run(*args):
        specs = in_specs or [
            pl.BlockSpec(memory_space=pltpu.SMEM if at in smem else pltpu.VMEM)
            for at in range(len(args))
        ]
        outs = jax.tree.leaves(out_shape)
        moved = sum(a.size * a.dtype.itemsize for a in [*args, *outs])
        more = {} if grid is None else {"grid": grid, "out_specs": out_specs}
        return pl.pallas_call(
            body,
            out_shape=out_shape,
            in_specs=specs,
            scratch_shapes=list(scratch),
            compiler_params=pltpu.CompilerParams(vmem_limit_bytes=30 * 2**20),
            cost_estimate=pl.CostEstimate(
                flops=flops, bytes_accessed=moved, transcendentals=0
            ),
            **more,
        )(*args)

    return run


def pack_kernel(right_ref, low_ref, up_ref, *out_refs):
    n = right_ref.shape[1]
    rank_cols = low_ref.shape[2]
    share = rank_cols // lax.axis_size("row")
    row = lax.axis_index("row")
    at = lax.broadcasted_iota(jnp.int32, (share, rank_cols), 1)
    want = lax.broadcasted_iota(jnp.int32, (share, rank_cols), 0) + row * share
    pick = (at == want).astype(F32).astype(BF16)
    for s, out_ref in enumerate(out_refs):
        tile = wrapped(own_tile() + s)
        out_ref[:n] = right_ref[tile].astype(BF16)
        pieces = []
        for slot in range(SIDE - 1):
            pair, is_low = partner_pair(tile, slot)
            piece = jnp.where(is_low, dot_t(pick, low_ref[pair]), dot_t(pick, up_ref[pair]))
            pieces.append(piece)
        out_ref[n:] = jnp.concatenate(pieces, axis=0).astype(BF16)


def partner_pair(tile, slot):
    is_low = slot < tile
    partner = jnp.where(is_low, slot, slot + 1)
    high = jnp.where(is_low, tile, partner)
    low = jnp.where(is_low, partner, tile)
    return jnp.where(high == 1, 0, jnp.where(high == 2, 1, 3)) + low, is_low


def order_kernel(sign, *refs):
    out_ref = refs[-1]
    for s in range(SIDE):
        out_ref[wrapped(own_tile() - sign * s)] = refs[s][...].astype(out_ref.dtype)


def stack_kernel(*refs):
    rows = refs[0].shape[0]
    for s, ref in enumerate(refs[:-1]):
        refs[-1][s * rows : (s + 1) * rows] = ref[...]


def deal_kernel(inverse_ref, *out_refs):
    for s in range(SIDE):
        out_refs[s][...] = inverse_ref[wrapped(own_tile() + s)]


def turn_kernel(low_ref, up_ref, *out_refs):
    rank_cols = low_ref.shape[2]
    one = lax.broadcasted_iota(jnp.int32, (rank_cols, rank_cols), 0)
    two = lax.broadcasted_iota(jnp.int32, (rank_cols, rank_cols), 1)
    eye = (one == two).astype(F32).astype(BF16)
    for s, out_ref in enumerate(out_refs):
        tile = wrapped(own_tile() + s)
        for slot in range(SIDE - 1):
            pair, is_low = partner_pair(tile, slot)
            factor = jnp.where(is_low, up_ref[pair], low_ref[pair])
            out_ref[slot * rank_cols : (slot + 1) * rank_cols] = dot_t(eye, factor).astype(BF16)


def products_kernel(n, padded, count, *refs):
    x_refs, inverse_refs = refs[:SIDE], refs[SIDE : SIDE + count]
    out_refs = refs[SIDE + count : -2]
    joined_ref, extra_ref = refs[-2:]
    lower, upper = inverse_refs[:SIDE], inverse_refs[SIDE:]
    rows = x_refs[0].shape[1]

    @pl.when(pl.program_id(0) == 0)
    def _():
        row = lax.axis_index("row")
        flip, q = lax.rem(row, SIDE), row // SIDE
        y = lax.axis_index("col") // SIDE
        for s in range(SIDE):
            t = wrapped(y - s - q)
            for at in range(SIDE):
                block = x_refs[s][at ^ flip]
                joined_ref[at, t, :rows] = block
                if rows > n:
                    extra_ref[at, t, : rows - n] = block[n:]

    width = joined_ref.shape[3]
    value = sum(
        dot_t(joined_ref[at].reshape(SIDE * padded, width), lower[at][...])
        for at in range(SIDE)
    )
    if rows > n:
        other = sum(
            dot_t(extra_ref[at].reshape(SIDE * (padded - n), width), upper[at][...])
            for at in range(SIDE)
        )
        share = (rows - n) // (SIDE - 1)
        slot = lax.broadcasted_iota(jnp.int32, (rows - n, value.shape[1]), 0) // share
    for t in range(SIDE):
        start = t * padded
        out_refs[t][:n] = value[start : start + n].astype(BF16)
        if rows > n:
            mine = value[start + n : start + rows]
            its = other[t * (padded - n) : t * (padded - n) + rows - n]
            out_refs[t][n:] = jnp.where(slot < own_tile(), mine, its).astype(BF16)


def products(n, gathered, *inverses):
    blocks, rows, width = gathered[0].shape
    total = inverses[0].shape[0]
    padded = rows + -rows % 16
    count = len(inverses)
    whole = pl.BlockSpec(gathered[0].shape, lambda a: (0, 0, 0))
    return kernel_call(
        lambda *refs: products_kernel(n, padded, count, *refs),
        [jax.ShapeDtypeStruct((rows, total), BF16)] * SIDE,
        flops=2 * SIDE * blocks * rows * width * total,
        grid=(total // 256,),
        in_specs=[whole] * SIDE
        + [pl.BlockSpec((256, width), lambda a: (a, 0)) for _ in inverses],
        out_specs=[pl.BlockSpec((rows, 256), lambda a: (0, a))] * SIDE,
        scratch=[
            pltpu.VMEM((blocks, SIDE, padded, width), BF16),
            pltpu.VMEM((blocks, SIDE, max(padded - n, 16), width), BF16),
        ],
    )(*gathered, *inverses)


def summed(refs):
    whole = refs[0][...].astype(F32)
    for ref in refs[1:]:
        whole = whole + ref[...].astype(F32)
    return whole


def total_kernel(n, *refs):
    dense_ref, extra_ref = refs[SIDE:]
    whole = summed(refs[:SIDE])
    dense_ref[...] = whole[:n]
    extra = whole[n:].astype(BF16)
    for at in range(extra_ref.shape[0]):
        extra_ref[at] = extra


def project(dense, turned, slot, rank_cols):
    width = turned[0].shape[1]
    return sum(
        dot_t(
            dense[:, at * width : (at + 1) * width],
            turned[at][slot * rank_cols : (slot + 1) * rank_cols],
        )
        for at in range(SIDE)
    )


def couple_kernel(dense_ref, mine_ref, other_ref, *refs):
    turned, (extra_ref, send_ref, later_ref) = refs[:SIDE], refs[SIDE:]
    slots = SIDE - 1
    rank_cols = turned[0].shape[0] // slots
    width = turned[0].shape[1]
    share = mine_ref.shape[1] // slots
    even = lax.rem(lax.axis_index("row"), 2) == 0
    tile = own_tile()
    for z in range(mine_ref.shape[0]):
        mine, other = mine_ref[z].astype(F32), other_ref[z].astype(F32)
        first = jnp.where(even, mine, other)
        second = jnp.where(even, other, mine)
        for slot in range(slots):
            at = slice(slot * share, (slot + 1) * share)
            start = slot * rank_cols + z * 2 * share
            extra_ref[start : start + 2 * share] = jnp.concatenate(
                [first[at], second[at]], axis=0
            ).astype(BF16)
    dense = dense_ref[...].astype(BF16)
    pieces = [project(dense, turned, slot, rank_cols) for slot in range(slots)]

    def coupling(left, right):
        left = pl.multiple_of(left * rank_cols, rank_cols)
        right = pl.multiple_of(right * rank_cols, rank_cols)
        return sum(
            dot_t(
                extra_ref[pl.ds(left, rank_cols), at * width : (at + 1) * width],
                turned[at][pl.ds(right, rank_cols), :],
            )
            for at in range(SIDE)
        )

    one = tile == 1
    pick = lambda a, b: jnp.where(one, a, b)
    pieces += [coupling(0, pick(1, 2)), coupling(pick(0, 1), 2)]
    send_ref[...] = jnp.concatenate(pieces, axis=0).astype(BF16)
    later_ref[:rank_cols] = coupling(pick(1, 2), 0).astype(BF16)
    later_ref[rank_cols:] = coupling(2, pick(0, 1)).astype(BF16)


def last_project_kernel(*refs):
    turned, (dense_ref, send_ref) = refs[SIDE : 2 * SIDE], refs[2 * SIDE :]
    slots = SIDE - 1
    rank_cols = turned[0].shape[0] // slots
    whole = summed(refs[:SIDE])
    dense_ref[...] = whole
    dense = whole.astype(BF16)
    pieces = [project(dense, turned, slot, rank_cols) for slot in range(slots)]
    send_ref[...] = jnp.concatenate(pieces, axis=0).astype(BF16)


def add_kernel(*refs):
    refs[-1][...] = summed(refs[:-1]).astype(BF16)


def finish_kernel(is_lower, *refs):
    count = SIDE if is_lower else 2 * SIDE
    dense_ref, extra_ref, ranks_ref = refs[count : count + 3]
    out_refs, sums_ref = refs[count + 3 : -1], refs[-1]
    for s in range(SIDE):
        tile = wrapped(own_tile() - s)
        held = refs[s].shape[0]
        sums_ref[tile, :held] = refs[s][...]
        if not is_lower:
            sums_ref[tile, held:] = refs[SIDE + s][...]
    n = dense_ref.shape[0]
    rank_cols = extra_ref.shape[0] // (SIDE - 1)
    width = dense_ref.shape[1] // SIDE
    tile = lax.rem(lax.axis_index("col"), SIDE)
    columns = lax.broadcasted_iota(jnp.int32, (n, rank_cols), 1)
    at_coupling = (SIDE - 1) * n
    coupling = {}
    order = list(range(SIDE)) if is_lower else list(range(SIDE))[::-1]
    first, second, third, last = order
    for which, key in enumerate(((third, second, first), (last, second, first))):
        coupling[key] = (second, which)
    for which, key in enumerate(((last, third, first), (last, third, second))):
        coupling[key] = (third, which)
    if not is_lower:
        coupling = {
            (0, 2, 3): (2, 0), (1, 2, 3): (2, 1), (0, 1, 2): (1, 0), (0, 1, 3): (1, 1)
        }
    masked = {}
    for at, source in enumerate(order):
        for target in order[at + 1 :]:
            slot = partners(source).index(target)
            value = sums_ref[source, slot * n : (slot + 1) * n].astype(F32)
            for before in order[:at]:
                held, which = coupling[target, source, before]
                start = at_coupling + which * rank_cols
                value = value - dot(
                    masked[source, before], sums_ref[held, start : start + rank_cols]
                )
            keep = columns < RBLK * ranks_ref[pair_of(source, target)]
            masked[target, source] = jnp.where(keep, value, 0.0).astype(BF16)
    result = dense_ref[...]
    nothing = jnp.zeros((n, rank_cols), BF16)
    for slot in range(SIDE - 1):
        mine = nothing
        for target in range(SIDE):
            source = partners(target)[slot]
            if (target, source) in masked:
                mine = jnp.where(tile == target, masked[target, source], mine)
        result = result - dot(
            mine, extra_ref[slot * rank_cols : (slot + 1) * rank_cols]
        )
    result = result.astype(BF16)
    for at in range(SIDE):
        block = result[:, at * width : (at + 1) * width]
        if is_lower:
            out_refs[0][wrapped(tile - at)] = block
        else:
            out_refs[at][...] = block


def shards(
    right_sides, low_left, low_right, up_left, up_right, low_ranks, up_ranks, inv_lower, inv_upper
):
    n, width = right_sides.shape[1:]
    rank_cols = low_left.shape[2]
    slots = SIDE - 1
    share = rank_cols // lax.axis_size("row")
    total = SIDE * width
    shape = jax.ShapeDtypeStruct

    height = n + slots * share
    tied = lax.optimization_barrier
    deal = kernel_call(deal_kernel, [shape((width, width), BF16)] * SIDE)
    stack = kernel_call(stack_kernel, shape((total, width), BF16))
    parts = scattered_x(deal(inv_lower))
    rows = scattered_x(
        kernel_call(pack_kernel, [shape((height, width), BF16)] * SIDE)(
            right_sides, low_left, up_left
        )
    )
    parts, rows = tied((parts, rows))
    rows = kernel_call(
        lambda *refs: order_kernel(1, *refs), shape((SIDE, height, width), BF16)
    )(*rows)
    lower = stack(*parts)
    rows, lower, inv_upper = tied((rows, lower, inv_upper))
    far_lower = swap_pair(lower)
    parts, rows = tied((scattered_x(deal(inv_upper)), swapped(rows)))
    upper = stack(*parts)
    far_upper = swap_pair(upper)
    gathered = gathered_y(rows)
    gathered, far_lower, lower, upper = tied((gathered, far_lower, lower, upper))
    near_upper = swap_core(upper)
    lower = [lower, swap_core(lower), far_lower, swap_core(far_lower)]
    gathered, low_right, up_right = tied((gathered, low_right, up_right))
    turned = scattered_x(
        kernel_call(turn_kernel, [shape((slots * rank_cols, width), BF16)] * SIDE)(
            low_right, up_right
        )
    )
    upper = [upper, near_upper, far_upper, swap_core(far_upper)]
    received = scattered_q(products(n, gathered, *lower, *upper))
    received, turned = tied((received, turned))
    dense, extra = kernel_call(
        lambda *refs: total_kernel(n, *refs),
        (shape((n, total), F32), shape((8, slots * share, total), BF16)),
    )(*received)
    mine = from_every_z(extra)
    packed = slots * n + 2 * rank_cols
    extra, send, later = kernel_call(
        couple_kernel,
        (
            shape((slots * rank_cols, total), BF16),
            shape((packed, rank_cols), BF16),
            shape((2 * rank_cols, rank_cols), BF16),
        ),
    )(dense, mine, swap_core(mine), *turned)

    def summed_everywhere(value):
        add = kernel_call(add_kernel, shape(value.shape, BF16))
        return gathered_x(add(*gathered_y(value)))

    def finished(is_lower, sums, dense, ranks):
        outs = [shape((SIDE, n, width), BF16)] if is_lower else [shape((n, width), BF16)] * SIDE
        return kernel_call(
            lambda *refs: finish_kernel(is_lower, *refs),
            outs,
            smem=(len(sums) + 2,),
            scratch=[pltpu.VMEM((SIDE, packed, rank_cols), BF16)],
        )(*sums, dense, extra, ranks)

    [rows] = finished(True, summed_everywhere(send), dense, low_ranks)
    rows, later = tied((swapped(rows), later))
    gathered = gathered_y(rows)
    add = kernel_call(add_kernel, shape(later.shape, BF16))
    later = add(*gathered_y(later))
    received = scattered_q(products(n, gathered, *upper))
    received, later = tied((received, gathered_x(later)))
    dense, send = kernel_call(
        last_project_kernel,
        (shape((n, total), F32), shape((slots * n, rank_cols), BF16)),
    )(*received, *turned)
    rows = finished(False, summed_everywhere(send) + list(later), dense, up_ranks)
    return kernel_call(
        lambda *refs: order_kernel(-1, *refs), shape((SIDE, n, width), F32)
    )(*scattered_x(rows, -1))


def solution(mesh):
    in_specs = (
        P(None, "row", "col"),
        P(None, "col", None),
        P(None, "col", None),
        P(None, "col", None),
        P(None, "col", None),
        P(),
        P(),
        P(None, "col", "row"),
        P(None, "col", "row"),
    )
    out_specs = P(None, "row", "col")
    return jax.shard_map(shards, mesh=mesh, in_specs=in_specs, out_specs=out_specs, check_vma=False)
```

```python
import jax
import jax.numpy as jnp
from jax import lax
from jax.experimental import pallas as pl
from jax.experimental.pallas import tpu as pltpu
from jax.sharding import PartitionSpec as P

RBLK = 32
BF16 = jnp.bfloat16
F32 = jnp.float32
SIDE = 4
Z_GROUPS = [[2 * z + core for z in range(8)] for core in range(2)]


def routes(to):
    index = lambda q, j, y, x: (SIDE * q + j) * SIDE * SIDE + SIDE * y + x
    span = range(SIDE)
    return [
        (index(q, j, y, x), index(*to(q, j, y, x)))
        for q in span for j in span for y in span for x in span
    ]


def permuted(value, to):
    return lax.ppermute(value, ("row", "col"), routes(to))


def gathered_y(value):
    return [value] + [
        permuted(value, lambda q, j, y, x: (q, j, (y + s) % SIDE, x)) for s in range(1, SIDE)
    ]


def gathered_x(value):
    return [value] + [
        permuted(value, lambda q, j, y, x: (q, j, y, (x + s) % SIDE)) for s in range(1, SIDE)
    ]


def scattered_q(values):
    return [values[0]] + [
        permuted(values[s], lambda q, j, y, x: ((q + s) % SIDE, j, y, x))
        for s in range(1, SIDE)
    ]


def scattered_x(values, sign=1):
    return [values[0]] + [
        permuted(values[s], lambda q, j, y, x: (q, j, y, (x + sign * s) % SIDE))
        for s in range(1, SIDE)
    ]


def from_every_z(value):
    return lax.all_to_all(value, "row", 0, 0, tiled=True, axis_index_groups=Z_GROUPS)


def own_tile():
    return lax.rem(lax.axis_index("col"), SIDE)


def wrapped(value):
    return lax.rem(value + 2 * SIDE, SIDE)


def swapped(value):
    return permuted(value, lambda q, j, y, x: (y, j, q, x))


def swap_core(value):
    return permuted(value, lambda q, j, y, x: (q, j ^ 1, y, x))


def swap_pair(value):
    return permuted(value, lambda q, j, y, x: (q, j ^ 2, y, x))


def dot(left, right):
    return jnp.dot(left, right, preferred_element_type=F32)


def dot_t(left, right):
    return lax.dot_general(
        left, right, (((1,), (1,)), ((), ())), preferred_element_type=F32
    )


def pair_of(i, j):
    high, low = max(i, j), min(i, j)
    return high * (high - 1) // 2 + low


def partners(tile):
    return [t for t in range(SIDE) if t != tile]


def kernel_call(body, out_shape, smem=(), flops=0, grid=None, in_specs=None, out_specs=None, scratch=()):
    def run(*args):
        specs = in_specs or [
            pl.BlockSpec(memory_space=pltpu.SMEM if at in smem else pltpu.VMEM)
            for at in range(len(args))
        ]
        outs = jax.tree.leaves(out_shape)
        moved = sum(a.size * a.dtype.itemsize for a in [*args, *outs])
        more = {} if grid is None else {"grid": grid, "out_specs": out_specs}
        return pl.pallas_call(
            body,
            out_shape=out_shape,
            in_specs=specs,
            scratch_shapes=list(scratch),
            compiler_params=pltpu.CompilerParams(vmem_limit_bytes=30 * 2**20),
            cost_estimate=pl.CostEstimate(
                flops=flops, bytes_accessed=moved, transcendentals=0
            ),
            **more,
        )(*args)

    return run


def pack_kernel(right_ref, low_ref, up_ref, *out_refs):
    n = right_ref.shape[1]
    rank_cols = low_ref.shape[2]
    share = rank_cols // lax.axis_size("row")
    row = lax.axis_index("row")
    at = lax.broadcasted_iota(jnp.int32, (share, rank_cols), 1)
    want = lax.broadcasted_iota(jnp.int32, (share, rank_cols), 0) + row * share
    pick = (at == want).astype(F32).astype(BF16)
    for s, out_ref in enumerate(out_refs):
        tile = wrapped(own_tile() + s)
        out_ref[:n] = right_ref[tile].astype(BF16)
        pieces = []
        for slot in range(SIDE - 1):
            pair, is_low = partner_pair(tile, slot)
            piece = jnp.where(is_low, dot_t(pick, low_ref[pair]), dot_t(pick, up_ref[pair]))
            pieces.append(piece)
        out_ref[n:] = jnp.concatenate(pieces, axis=0).astype(BF16)


def partner_pair(tile, slot):
    is_low = slot < tile
    partner = jnp.where(is_low, slot, slot + 1)
    high = jnp.where(is_low, tile, partner)
    low = jnp.where(is_low, partner, tile)
    return jnp.where(high == 1, 0, jnp.where(high == 2, 1, 3)) + low, is_low


def order_kernel(sign, *refs):
    out_ref = refs[-1]
    for s in range(SIDE):
        out_ref[wrapped(own_tile() - sign * s)] = refs[s][...].astype(out_ref.dtype)


def stack_kernel(*refs):
    rows = refs[0].shape[0]
    for s, ref in enumerate(refs[:-1]):
        refs[-1][s * rows : (s + 1) * rows] = ref[...]


def deal_kernel(inverse_ref, *out_refs):
    for s in range(SIDE):
        out_refs[s][...] = inverse_ref[wrapped(own_tile() + s)]


def turn_kernel(low_ref, up_ref, *out_refs):
    rank_cols = low_ref.shape[2]
    one = lax.broadcasted_iota(jnp.int32, (rank_cols, rank_cols), 0)
    two = lax.broadcasted_iota(jnp.int32, (rank_cols, rank_cols), 1)
    eye = (one == two).astype(F32).astype(BF16)
    for s, out_ref in enumerate(out_refs):
        tile = wrapped(own_tile() + s)
        for slot in range(SIDE - 1):
            pair, is_low = partner_pair(tile, slot)
            factor = jnp.where(is_low, up_ref[pair], low_ref[pair])
            out_ref[slot * rank_cols : (slot + 1) * rank_cols] = dot_t(eye, factor).astype(BF16)


def products_kernel(n, padded, count, *refs):
    x_refs, inverse_refs = refs[:SIDE], refs[SIDE : SIDE + count]
    out_refs = refs[SIDE + count : -2]
    joined_ref, extra_ref = refs[-2:]
    lower, upper = inverse_refs[:SIDE], inverse_refs[SIDE:]
    rows = x_refs[0].shape[1]

    @pl.when(pl.program_id(0) == 0)
    def _():
        row = lax.axis_index("row")
        flip, q = lax.rem(row, SIDE), row // SIDE
        y = lax.axis_index("col") // SIDE
        for s in range(SIDE):
            t = wrapped(y - s - q)
            for at in range(SIDE):
                block = x_refs[s][at ^ flip]
                joined_ref[at, t, :rows] = block
                if rows > n:
                    extra_ref[at, t, : rows - n] = block[n:]

    width = joined_ref.shape[3]
    value = sum(
        dot_t(joined_ref[at].reshape(SIDE * padded, width), lower[at][...])
        for at in range(SIDE)
    )
    if rows > n:
        other = sum(
            dot_t(extra_ref[at].reshape(SIDE * (padded - n), width), upper[at][...])
            for at in range(SIDE)
        )
        share = (rows - n) // (SIDE - 1)
        slot = lax.broadcasted_iota(jnp.int32, (rows - n, value.shape[1]), 0) // share
    for t in range(SIDE):
        start = t * padded
        out_refs[t][:n] = value[start : start + n].astype(BF16)
        if rows > n:
            mine = value[start + n : start + rows]
            its = other[t * (padded - n) : t * (padded - n) + rows - n]
            out_refs[t][n:] = jnp.where(slot < own_tile(), mine, its).astype(BF16)


def products(n, gathered, *inverses):
    blocks, rows, width = gathered[0].shape
    total = inverses[0].shape[0]
    padded = rows + -rows % 16
    count = len(inverses)
    whole = pl.BlockSpec(gathered[0].shape, lambda a: (0, 0, 0))
    return kernel_call(
        lambda *refs: products_kernel(n, padded, count, *refs),
        [jax.ShapeDtypeStruct((rows, total), BF16)] * SIDE,
        flops=2 * SIDE * blocks * rows * width * total,
        grid=(total // 256,),
        in_specs=[whole] * SIDE
        + [pl.BlockSpec((256, width), lambda a: (a, 0)) for _ in inverses],
        out_specs=[pl.BlockSpec((rows, 256), lambda a: (0, a))] * SIDE,
        scratch=[
            pltpu.VMEM((blocks, SIDE, padded, width), BF16),
            pltpu.VMEM((blocks, SIDE, max(padded - n, 16), width), BF16),
        ],
    )(*gathered, *inverses)


def summed(refs):
    whole = refs[0][...].astype(F32)
    for ref in refs[1:]:
        whole = whole + ref[...].astype(F32)
    return whole


def total_kernel(n, *refs):
    dense_ref, extra_ref = refs[SIDE:]
    whole = summed(refs[:SIDE])
    dense_ref[...] = whole[:n]
    extra = whole[n:].astype(BF16)
    for at in range(extra_ref.shape[0]):
        extra_ref[at] = extra


def project(dense, turned, slot, rank_cols):
    width = turned[0].shape[1]
    return sum(
        dot_t(
            dense[:, at * width : (at + 1) * width],
            turned[at][slot * rank_cols : (slot + 1) * rank_cols],
        )
        for at in range(SIDE)
    )


def couple_kernel(dense_ref, mine_ref, other_ref, *refs):
    turned, (extra_ref, send_ref, later_ref) = refs[:SIDE], refs[SIDE:]
    slots = SIDE - 1
    rank_cols = turned[0].shape[0] // slots
    width = turned[0].shape[1]
    share = mine_ref.shape[1] // slots
    even = lax.rem(lax.axis_index("row"), 2) == 0
    tile = own_tile()
    for z in range(mine_ref.shape[0]):
        mine, other = mine_ref[z].astype(F32), other_ref[z].astype(F32)
        first = jnp.where(even, mine, other)
        second = jnp.where(even, other, mine)
        for slot in range(slots):
            at = slice(slot * share, (slot + 1) * share)
            start = slot * rank_cols + z * 2 * share
            extra_ref[start : start + 2 * share] = jnp.concatenate(
                [first[at], second[at]], axis=0
            ).astype(BF16)
    dense = dense_ref[...].astype(BF16)
    pieces = [project(dense, turned, slot, rank_cols) for slot in range(slots)]

    def coupling(left, right):
        left = pl.multiple_of(left * rank_cols, rank_cols)
        right = pl.multiple_of(right * rank_cols, rank_cols)
        return sum(
            dot_t(
                extra_ref[pl.ds(left, rank_cols), at * width : (at + 1) * width],
                turned[at][pl.ds(right, rank_cols), :],
            )
            for at in range(SIDE)
        )

    one = tile == 1
    pick = lambda a, b: jnp.where(one, a, b)
    pieces += [coupling(0, pick(1, 2)), coupling(pick(0, 1), 2)]
    send_ref[...] = jnp.concatenate(pieces, axis=0).astype(BF16)
    later_ref[:rank_cols] = coupling(pick(1, 2), 0).astype(BF16)
    later_ref[rank_cols:] = coupling(2, pick(0, 1)).astype(BF16)


def last_project_kernel(*refs):
    turned, (later_ref, dense_ref, send_ref) = refs[SIDE : 2 * SIDE], refs[2 * SIDE :]
    slots = SIDE - 1
    rank_cols = turned[0].shape[0] // slots
    whole = summed(refs[:SIDE])
    dense_ref[...] = whole
    dense = whole.astype(BF16)
    pieces = [project(dense, turned, slot, rank_cols) for slot in range(slots)]
    send = jnp.concatenate(pieces, axis=0).astype(BF16)
    n = send.shape[0]
    send_ref[:n] = send
    send_ref[n:] = later_ref[...]


def add_kernel(*refs):
    refs[-1][...] = summed(refs[:-1]).astype(BF16)


def finish_kernel(is_lower, *refs):
    dense_ref, extra_ref, ranks_ref = refs[SIDE : SIDE + 3]
    out_refs, sums_ref = refs[SIDE + 3 : -1], refs[-1]
    for s in range(SIDE):
        sums_ref[wrapped(own_tile() - s)] = refs[s][...]
    n = dense_ref.shape[0]
    rank_cols = extra_ref.shape[0] // (SIDE - 1)
    width = dense_ref.shape[1] // SIDE
    tile = lax.rem(lax.axis_index("col"), SIDE)
    columns = lax.broadcasted_iota(jnp.int32, (n, rank_cols), 1)
    at_coupling = (SIDE - 1) * n
    coupling = {}
    order = list(range(SIDE)) if is_lower else list(range(SIDE))[::-1]
    first, second, third, last = order
    for which, key in enumerate(((third, second, first), (last, second, first))):
        coupling[key] = (second, which)
    for which, key in enumerate(((last, third, first), (last, third, second))):
        coupling[key] = (third, which)
    if not is_lower:
        coupling = {
            (0, 2, 3): (2, 0), (1, 2, 3): (2, 1), (0, 1, 2): (1, 0), (0, 1, 3): (1, 1)
        }
    masked = {}
    for at, source in enumerate(order):
        for target in order[at + 1 :]:
            slot = partners(source).index(target)
            value = sums_ref[source, slot * n : (slot + 1) * n].astype(F32)
            for before in order[:at]:
                held, which = coupling[target, source, before]
                start = at_coupling + which * rank_cols
                value = value - dot(
                    masked[source, before], sums_ref[held, start : start + rank_cols]
                )
            keep = columns < RBLK * ranks_ref[pair_of(source, target)]
            masked[target, source] = jnp.where(keep, value, 0.0).astype(BF16)
    result = dense_ref[...]
    nothing = jnp.zeros((n, rank_cols), BF16)
    for slot in range(SIDE - 1):
        mine = nothing
        for target in range(SIDE):
            source = partners(target)[slot]
            if (target, source) in masked:
                mine = jnp.where(tile == target, masked[target, source], mine)
        result = result - dot(
            mine, extra_ref[slot * rank_cols : (slot + 1) * rank_cols]
        )
    result = result.astype(BF16)
    for at in range(SIDE):
        block = result[:, at * width : (at + 1) * width]
        if is_lower:
            out_refs[0][wrapped(tile - at)] = block
        else:
            out_refs[at][...] = block


def shards(
    right_sides, low_left, low_right, up_left, up_right, low_ranks, up_ranks, inv_lower, inv_upper
):
    n, width = right_sides.shape[1:]
    rank_cols = low_left.shape[2]
    slots = SIDE - 1
    share = rank_cols // lax.axis_size("row")
    total = SIDE * width
    shape = jax.ShapeDtypeStruct

    height = n + slots * share
    tied = lax.optimization_barrier
    deal = kernel_call(deal_kernel, [shape((width, width), BF16)] * SIDE)
    stack = kernel_call(stack_kernel, shape((total, width), BF16))
    rows = kernel_call(pack_kernel, [shape((height, width), BF16)] * SIDE)(
        right_sides, low_left, up_left
    )
    rows, inv_lower = tied((rows, inv_lower))
    rows = scattered_x(rows)
    parts = scattered_x(deal(inv_lower))
    rows = kernel_call(
        lambda *refs: order_kernel(1, *refs), shape((SIDE, height, width), BF16)
    )(*rows)
    rows, inv_upper = tied((rows, inv_upper))
    lower = stack(*parts)
    far_lower = swap_pair(lower)
    parts, rows = tied((scattered_x(deal(inv_upper)), swapped(rows)))
    upper = stack(*parts)
    far_upper = swap_pair(upper)
    gathered = gathered_y(rows)
    gathered, far_lower, lower, upper = tied((gathered, far_lower, lower, upper))
    near_upper = swap_core(upper)
    lower = [lower, swap_core(lower), far_lower, swap_core(far_lower)]
    gathered, low_right, up_right = tied((gathered, low_right, up_right))
    turned = scattered_x(
        kernel_call(turn_kernel, [shape((slots * rank_cols, width), BF16)] * SIDE)(
            low_right, up_right
        )
    )
    upper = [upper, near_upper, far_upper, swap_core(far_upper)]
    received = scattered_q(products(n, gathered, *lower, *upper))
    received, turned = tied((received, turned))
    dense, extra = kernel_call(
        lambda *refs: total_kernel(n, *refs),
        (shape((n, total), F32), shape((8, slots * share, total), BF16)),
    )(*received)
    mine = from_every_z(extra)
    packed = slots * n + 2 * rank_cols
    extra, send, later = kernel_call(
        couple_kernel,
        (
            shape((slots * rank_cols, total), BF16),
            shape((packed, rank_cols), BF16),
            shape((2 * rank_cols, rank_cols), BF16),
        ),
    )(dense, mine, swap_core(mine), *turned)

    def finished(is_lower, send, dense, ranks):
        sums = kernel_call(add_kernel, shape((packed, rank_cols), BF16))(*gathered_y(send))
        outs = [shape((SIDE, n, width), BF16)] if is_lower else [shape((n, width), BF16)] * SIDE
        return kernel_call(
            lambda *refs: finish_kernel(is_lower, *refs),
            outs,
            smem=(SIDE + 2,),
            scratch=[pltpu.VMEM((SIDE, packed, rank_cols), BF16)],
        )(*gathered_x(sums), dense, extra, ranks)

    [rows] = finished(True, send, dense, low_ranks)
    parts = products(n, gathered_y(swapped(rows)), *upper)
    dense, send = kernel_call(
        last_project_kernel,
        (shape((n, total), F32), shape((packed, rank_cols), BF16)),
    )(*scattered_q(parts), *turned, later)
    rows = finished(False, send, dense, up_ranks)
    return kernel_call(
        lambda *refs: order_kernel(-1, *refs), shape((SIDE, n, width), F32)
    )(*scattered_x(rows, -1))


def solution(mesh):
    in_specs = (
        P(None, "row", "col"),
        P(None, "col", None),
        P(None, "col", None),
        P(None, "col", None),
        P(None, "col", None),
        P(),
        P(),
        P(None, "col", "row"),
        P(None, "col", "row"),
    )
    out_specs = P(None, "row", "col")
    return jax.shard_map(shards, mesh=mesh, in_specs=in_specs, out_specs=out_specs, check_vma=False)
```

```python
import jax
import jax.numpy as jnp
from jax import lax
from jax.experimental import pallas as pl
from jax.experimental.pallas import tpu as pltpu
from jax.sharding import PartitionSpec as P

RBLK = 32
BF16 = jnp.bfloat16
F32 = jnp.float32
SIDE = 4
Z_GROUPS = [[2 * z + core for z in range(8)] for core in range(2)]


def routes(to):
    index = lambda q, j, y, x: (SIDE * q + j) * SIDE * SIDE + SIDE * y + x
    span = range(SIDE)
    return [
        (index(q, j, y, x), index(*to(q, j, y, x)))
        for q in span for j in span for y in span for x in span
    ]


def permuted(value, to):
    return lax.ppermute(value, ("row", "col"), routes(to))


def gathered_y(value):
    return [value] + [
        permuted(value, lambda q, j, y, x: (q, j, (y + s) % SIDE, x)) for s in range(1, SIDE)
    ]


def gathered_x(value):
    return [value] + [
        permuted(value, lambda q, j, y, x: (q, j, y, (x + s) % SIDE)) for s in range(1, SIDE)
    ]


def scattered_q(values):
    return [values[0]] + [
        permuted(values[s], lambda q, j, y, x: ((q + s) % SIDE, j, y, x))
        for s in range(1, SIDE)
    ]


def scattered_x(values, sign=1):
    return [values[0]] + [
        permuted(values[s], lambda q, j, y, x: (q, j, y, (x + sign * s) % SIDE))
        for s in range(1, SIDE)
    ]


def from_every_z(value):
    return lax.all_to_all(value, "row", 0, 0, tiled=True, axis_index_groups=Z_GROUPS)


def own_tile():
    return lax.rem(lax.axis_index("col"), SIDE)


def wrapped(value):
    return lax.rem(value + 2 * SIDE, SIDE)


def swapped(value):
    return permuted(value, lambda q, j, y, x: (y, j, q, x))


def swap_core(value):
    return permuted(value, lambda q, j, y, x: (q, j ^ 1, y, x))


def swap_pair(value):
    return permuted(value, lambda q, j, y, x: (q, j ^ 2, y, x))


def dot(left, right):
    return jnp.dot(left, right, preferred_element_type=F32)


def dot_t(left, right):
    return lax.dot_general(
        left, right, (((1,), (1,)), ((), ())), preferred_element_type=F32
    )


def pair_of(i, j):
    high, low = max(i, j), min(i, j)
    return high * (high - 1) // 2 + low


def partners(tile):
    return [t for t in range(SIDE) if t != tile]


def kernel_call(body, out_shape, smem=(), flops=0, grid=None, in_specs=None, out_specs=None, scratch=()):
    def run(*args):
        specs = in_specs or [
            pl.BlockSpec(memory_space=pltpu.SMEM if at in smem else pltpu.VMEM)
            for at in range(len(args))
        ]
        outs = jax.tree.leaves(out_shape)
        moved = sum(a.size * a.dtype.itemsize for a in [*args, *outs])
        more = {} if grid is None else {"grid": grid, "out_specs": out_specs}
        return pl.pallas_call(
            body,
            out_shape=out_shape,
            in_specs=specs,
            scratch_shapes=list(scratch),
            compiler_params=pltpu.CompilerParams(vmem_limit_bytes=14 * 2**20),
            cost_estimate=pl.CostEstimate(
                flops=flops, bytes_accessed=moved, transcendentals=0
            ),
            **more,
        )(*args)

    return run


def pack_kernel(right_ref, low_ref, up_ref, *out_refs):
    n = right_ref.shape[1]
    rank_cols = low_ref.shape[2]
    share = rank_cols // lax.axis_size("row")
    row = lax.axis_index("row")
    at = lax.broadcasted_iota(jnp.int32, (share, rank_cols), 1)
    want = lax.broadcasted_iota(jnp.int32, (share, rank_cols), 0) + row * share
    pick = (at == want).astype(F32).astype(BF16)
    for s, out_ref in enumerate(out_refs):
        tile = wrapped(own_tile() + s)
        out_ref[:n] = right_ref[tile].astype(BF16)
        pieces = []
        for slot in range(SIDE - 1):
            pair, is_low = partner_pair(tile, slot)
            piece = jnp.where(is_low, dot_t(pick, low_ref[pair]), dot_t(pick, up_ref[pair]))
            pieces.append(piece)
        out_ref[n:] = jnp.concatenate(pieces, axis=0).astype(BF16)


def partner_pair(tile, slot):
    is_low = slot < tile
    partner = jnp.where(is_low, slot, slot + 1)
    high = jnp.where(is_low, tile, partner)
    low = jnp.where(is_low, partner, tile)
    return jnp.where(high == 1, 0, jnp.where(high == 2, 1, 3)) + low, is_low


def order_kernel(sign, *refs):
    out_ref = refs[-1]
    for s in range(SIDE):
        out_ref[wrapped(own_tile() - sign * s)] = refs[s][...].astype(out_ref.dtype)


def stack_kernel(*refs):
    rows = refs[0].shape[0]
    for s, ref in enumerate(refs[:-1]):
        refs[-1][s * rows : (s + 1) * rows] = ref[...]


def deal_kernel(inverse_ref, *out_refs):
    for s in range(SIDE):
        out_refs[s][...] = inverse_ref[wrapped(own_tile() + s)]


def turn_kernel(low_ref, up_ref, *out_refs):
    rank_cols = low_ref.shape[2]
    one = lax.broadcasted_iota(jnp.int32, (rank_cols, rank_cols), 0)
    two = lax.broadcasted_iota(jnp.int32, (rank_cols, rank_cols), 1)
    eye = (one == two).astype(F32).astype(BF16)
    for s, out_ref in enumerate(out_refs):
        tile = wrapped(own_tile() + s)
        for slot in range(SIDE - 1):
            pair, is_low = partner_pair(tile, slot)
            factor = jnp.where(is_low, up_ref[pair], low_ref[pair])
            out_ref[slot * rank_cols : (slot + 1) * rank_cols] = dot_t(eye, factor).astype(BF16)


def products_kernel(n, padded, count, *refs):
    x_refs, inverse_refs = refs[:SIDE], refs[SIDE : SIDE + count]
    out_refs = refs[SIDE + count : -2]
    joined_ref, extra_ref = refs[-2:]
    lower, upper = inverse_refs[:SIDE], inverse_refs[SIDE:]
    rows = x_refs[0].shape[1]

    @pl.when(pl.program_id(0) == 0)
    def _():
        row = lax.axis_index("row")
        flip, q = lax.rem(row, SIDE), row // SIDE
        y = lax.axis_index("col") // SIDE
        for s in range(SIDE):
            t = wrapped(y - s - q)
            for at in range(SIDE):
                block = x_refs[s][at ^ flip]
                joined_ref[at, t, :rows] = block
                if rows > n:
                    extra_ref[at, t, : rows - n] = block[n:]

    width = joined_ref.shape[3]
    value = sum(
        dot_t(joined_ref[at].reshape(SIDE * padded, width), lower[at][...])
        for at in range(SIDE)
    )
    if rows > n:
        other = sum(
            dot_t(extra_ref[at].reshape(SIDE * (padded - n), width), upper[at][...])
            for at in range(SIDE)
        )
        share = (rows - n) // (SIDE - 1)
        slot = lax.broadcasted_iota(jnp.int32, (rows - n, value.shape[1]), 0) // share
    for t in range(SIDE):
        start = t * padded
        out_refs[t][:n] = value[start : start + n].astype(BF16)
        if rows > n:
            mine = value[start + n : start + rows]
            its = other[t * (padded - n) : t * (padded - n) + rows - n]
            out_refs[t][n:] = jnp.where(slot < own_tile(), mine, its).astype(BF16)


def products(n, gathered, *inverses):
    blocks, rows, width = gathered[0].shape
    total = inverses[0].shape[0]
    padded = rows + -rows % 16
    count = len(inverses)
    whole = pl.BlockSpec(gathered[0].shape, lambda a: (0, 0, 0))
    return kernel_call(
        lambda *refs: products_kernel(n, padded, count, *refs),
        [jax.ShapeDtypeStruct((rows, total), BF16)] * SIDE,
        flops=2 * SIDE * blocks * rows * width * total,
        grid=(total // 256,),
        in_specs=[whole] * SIDE
        + [pl.BlockSpec((256, width), lambda a: (a, 0)) for _ in inverses],
        out_specs=[pl.BlockSpec((rows, 256), lambda a: (0, a))] * SIDE,
        scratch=[
            pltpu.VMEM((blocks, SIDE, padded, width), BF16),
            pltpu.VMEM((blocks, SIDE, max(padded - n, 16), width), BF16),
        ],
    )(*gathered, *inverses)


def summed(refs):
    whole = refs[0][...].astype(F32)
    for ref in refs[1:]:
        whole = whole + ref[...].astype(F32)
    return whole


def total_kernel(n, *refs):
    dense_ref, extra_ref = refs[SIDE:]
    whole = summed(refs[:SIDE])
    dense_ref[...] = whole[:n]
    extra = whole[n:].astype(BF16)
    for at in range(extra_ref.shape[0]):
        extra_ref[at] = extra


def project(dense, turned, slot, rank_cols):
    width = turned[0].shape[1]
    return sum(
        dot_t(
            dense[:, at * width : (at + 1) * width],
            turned[at][slot * rank_cols : (slot + 1) * rank_cols],
        )
        for at in range(SIDE)
    )


def couple_kernel(dense_ref, mine_ref, other_ref, *refs):
    turned, (extra_ref, send_ref, later_ref) = refs[:SIDE], refs[SIDE:]
    slots = SIDE - 1
    rank_cols = turned[0].shape[0] // slots
    width = turned[0].shape[1]
    share = mine_ref.shape[1] // slots
    even = lax.rem(lax.axis_index("row"), 2) == 0
    tile = own_tile()
    for z in range(mine_ref.shape[0]):
        mine, other = mine_ref[z].astype(F32), other_ref[z].astype(F32)
        first = jnp.where(even, mine, other)
        second = jnp.where(even, other, mine)
        for slot in range(slots):
            at = slice(slot * share, (slot + 1) * share)
            start = slot * rank_cols + z * 2 * share
            extra_ref[start : start + 2 * share] = jnp.concatenate(
                [first[at], second[at]], axis=0
            ).astype(BF16)
    dense = dense_ref[...].astype(BF16)
    pieces = [project(dense, turned, slot, rank_cols) for slot in range(slots)]

    def coupling(left, right):
        left = pl.multiple_of(left * rank_cols, rank_cols)
        right = pl.multiple_of(right * rank_cols, rank_cols)
        return sum(
            dot_t(
                extra_ref[pl.ds(left, rank_cols), at * width : (at + 1) * width],
                turned[at][pl.ds(right, rank_cols), :],
            )
            for at in range(SIDE)
        )

    one = tile == 1
    pick = lambda a, b: jnp.where(one, a, b)
    pieces += [coupling(0, pick(1, 2)), coupling(pick(0, 1), 2)]
    send_ref[...] = jnp.concatenate(pieces, axis=0).astype(BF16)
    later_ref[:rank_cols] = coupling(pick(1, 2), 0).astype(BF16)
    later_ref[rank_cols:] = coupling(2, pick(0, 1)).astype(BF16)


def last_project_kernel(*refs):
    turned, (later_ref, dense_ref, send_ref) = refs[SIDE : 2 * SIDE], refs[2 * SIDE :]
    slots = SIDE - 1
    rank_cols = turned[0].shape[0] // slots
    whole = summed(refs[:SIDE])
    dense_ref[...] = whole
    dense = whole.astype(BF16)
    pieces = [project(dense, turned, slot, rank_cols) for slot in range(slots)]
    send = jnp.concatenate(pieces, axis=0).astype(BF16)
    n = send.shape[0]
    send_ref[:n] = send
    send_ref[n:] = later_ref[...]


def add_kernel(*refs):
    refs[-1][...] = summed(refs[:-1]).astype(BF16)


def finish_kernel(is_lower, *refs):
    dense_ref, extra_ref, ranks_ref = refs[SIDE : SIDE + 3]
    out_refs, sums_ref = refs[SIDE + 3 : -1], refs[-1]
    for s in range(SIDE):
        sums_ref[wrapped(own_tile() - s)] = refs[s][...]
    n = dense_ref.shape[0]
    rank_cols = extra_ref.shape[0] // (SIDE - 1)
    width = dense_ref.shape[1] // SIDE
    tile = lax.rem(lax.axis_index("col"), SIDE)
    columns = lax.broadcasted_iota(jnp.int32, (n, rank_cols), 1)
    at_coupling = (SIDE - 1) * n
    coupling = {}
    order = list(range(SIDE)) if is_lower else list(range(SIDE))[::-1]
    first, second, third, last = order
    for which, key in enumerate(((third, second, first), (last, second, first))):
        coupling[key] = (second, which)
    for which, key in enumerate(((last, third, first), (last, third, second))):
        coupling[key] = (third, which)
    if not is_lower:
        coupling = {
            (0, 2, 3): (2, 0), (1, 2, 3): (2, 1), (0, 1, 2): (1, 0), (0, 1, 3): (1, 1)
        }
    masked = {}
    for at, source in enumerate(order):
        for target in order[at + 1 :]:
            slot = partners(source).index(target)
            value = sums_ref[source, slot * n : (slot + 1) * n].astype(F32)
            for before in order[:at]:
                held, which = coupling[target, source, before]
                start = at_coupling + which * rank_cols
                value = value - dot(
                    masked[source, before], sums_ref[held, start : start + rank_cols]
                )
            keep = columns < RBLK * ranks_ref[pair_of(source, target)]
            masked[target, source] = jnp.where(keep, value, 0.0).astype(BF16)
    result = dense_ref[...]
    nothing = jnp.zeros((n, rank_cols), BF16)
    for slot in range(SIDE - 1):
        mine = nothing
        for target in range(SIDE):
            source = partners(target)[slot]
            if (target, source) in masked:
                mine = jnp.where(tile == target, masked[target, source], mine)
        result = result - dot(
            mine, extra_ref[slot * rank_cols : (slot + 1) * rank_cols]
        )
    result = result.astype(BF16)
    for at in range(SIDE):
        block = result[:, at * width : (at + 1) * width]
        if is_lower:
            out_refs[0][wrapped(tile - at)] = block
        else:
            out_refs[at][...] = block


def shards(
    right_sides, low_left, low_right, up_left, up_right, low_ranks, up_ranks, inv_lower, inv_upper
):
    n, width = right_sides.shape[1:]
    rank_cols = low_left.shape[2]
    slots = SIDE - 1
    share = rank_cols // lax.axis_size("row")
    total = SIDE * width
    shape = jax.ShapeDtypeStruct

    height = n + slots * share
    tied = lax.optimization_barrier
    deal = kernel_call(deal_kernel, [shape((width, width), BF16)] * SIDE)
    stack = kernel_call(stack_kernel, shape((total, width), BF16))
    rows = kernel_call(pack_kernel, [shape((height, width), BF16)] * SIDE)(
        right_sides, low_left, up_left
    )
    rows, inv_lower = tied((rows, inv_lower))
    rows = scattered_x(rows)
    parts = scattered_x(deal(inv_lower))
    rows = kernel_call(
        lambda *refs: order_kernel(1, *refs), shape((SIDE, height, width), BF16)
    )(*rows)
    rows, inv_upper = tied((rows, inv_upper))
    lower = stack(*parts)
    far_lower = swap_pair(lower)
    parts, rows = tied((scattered_x(deal(inv_upper)), swapped(rows)))
    upper = stack(*parts)
    far_upper = swap_pair(upper)
    gathered = gathered_y(rows)
    gathered, far_lower, lower, upper = tied((gathered, far_lower, lower, upper))
    near_upper = swap_core(upper)
    lower = [lower, swap_core(lower), far_lower, swap_core(far_lower)]
    gathered, low_right, up_right = tied((gathered, low_right, up_right))
    turned = scattered_x(
        kernel_call(turn_kernel, [shape((slots * rank_cols, width), BF16)] * SIDE)(
            low_right, up_right
        )
    )
    upper = [upper, near_upper, far_upper, swap_core(far_upper)]
    received = scattered_q(products(n, gathered, *lower, *upper))
    received, turned = tied((received, turned))
    dense, extra = kernel_call(
        lambda *refs: total_kernel(n, *refs),
        (shape((n, total), F32), shape((8, slots * share, total), BF16)),
    )(*received)
    mine = from_every_z(extra)
    packed = slots * n + 2 * rank_cols
    extra, send, later = kernel_call(
        couple_kernel,
        (
            shape((slots * rank_cols, total), BF16),
            shape((packed, rank_cols), BF16),
            shape((2 * rank_cols, rank_cols), BF16),
        ),
    )(dense, mine, swap_core(mine), *turned)

    def finished(is_lower, send, dense, ranks):
        sums = kernel_call(add_kernel, shape((packed, rank_cols), BF16))(*gathered_y(send))
        outs = [shape((SIDE, n, width), BF16)] if is_lower else [shape((n, width), BF16)] * SIDE
        return kernel_call(
            lambda *refs: finish_kernel(is_lower, *refs),
            outs,
            smem=(SIDE + 2,),
            scratch=[pltpu.VMEM((SIDE, packed, rank_cols), BF16)],
        )(*gathered_x(sums), dense, extra, ranks)

    [rows] = finished(True, send, dense, low_ranks)
    parts = products(n, gathered_y(swapped(rows)), *upper)
    dense, send = kernel_call(
        last_project_kernel,
        (shape((n, total), F32), shape((packed, rank_cols), BF16)),
    )(*scattered_q(parts), *turned, later)
    rows = finished(False, send, dense, up_ranks)
    return kernel_call(
        lambda *refs: order_kernel(-1, *refs), shape((SIDE, n, width), F32)
    )(*scattered_x(rows, -1))


def solution(mesh):
    in_specs = (
        P(None, "row", "col"),
        P(None, "col", None),
        P(None, "col", None),
        P(None, "col", None),
        P(None, "col", None),
        P(),
        P(),
        P(None, "col", "row"),
        P(None, "col", "row"),
    )
    out_specs = P(None, "row", "col")
    return jax.shard_map(shards, mesh=mesh, in_specs=in_specs, out_specs=out_specs, check_vma=False)
```
